32 devices in a mesh: dp: 16 (over z, y, x), tensor: 2 (over core).
Axes of the slice: x: 2, y: 2, z: 4, core: 2. Of those that a mesh axis runs over, the one named last changes fastest.
Arguments:
- tokens: bfloat16 [16, 256, 2048], P('dp', 'tensor'), may hold values from -6 to 6
- doc_lengths: int32 [16, 4], P('dp'), may hold values from 0 to 255, as said below
- recurrent_norm_gain: bfloat16 [2048], P('dp'), may hold values from 0.25 to 1.75
- w_branch: bfloat16 [2048, 2560], P('dp', 'tensor'), may hold values from -0.125 to 0.125
- w_input: bfloat16 [2048, 2560], P('dp', 'tensor'), may hold values from -0.125 to 0.125
- w_rgate: bfloat16 [10, 256, 256], P('tensor', 'dp'), may hold values from -0.375 to 0.375
- w_igate: bfloat16 [10, 256, 256], P('tensor', 'dp'), may hold values from -0.375 to 0.375
- rgate_bias: bfloat16 [10, 256], P('tensor', 'dp'), may hold values from -3 to 3
- igate_bias: bfloat16 [10, 256], P('tensor', 'dp'), may hold values from -3 to 3
- decay_param: bfloat16 [10, 256], P('tensor', 'dp'), may hold values from 4.1875 to 8.5
- conv_weight: bfloat16 [4, 10, 256], P(None, 'tensor', 'dp'), may hold values from -3 to 3
- conv_bias: bfloat16 [10, 256], P('tensor', 'dp'), may hold values from -2 to 2
- w_output: bfloat16 [2560, 2048], P('tensor', 'dp'), may hold values from -0.25 to 0.25
- perceptron_norm_gain: bfloat16 [2048], P('dp'), may hold values from 0.25 to 1.75
- w_gate: bfloat16 [2048, 6144], P('dp', 'tensor'), may hold values from -0.125 to 0.125
- w_up: bfloat16 [2048, 6144], P('dp', 'tensor'), may hold values from -0.125 to 0.125
- w_down: bfloat16 [6144, 2048], P('tensor', 'dp'), may hold values from -0.078125 to 0.078125
- cotangent: float32 [16, 256, 2048], P('dp', 'tensor'), may hold values from -6 to 6
Outputs:
- result: bfloat16 [16, 256, 2048], P('dp', 'tensor')
- token_input_gradient: float32 [16, 256, 2048], P('dp', 'tensor')
- grad_rec_gain: float32 [2048], P('dp')
- grad_w_branch: float32 [2048, 2560], P('dp', 'tensor')
- grad_w_input: float32 [2048, 2560], P('dp', 'tensor')
- grad_w_rgate: float32 [10, 256, 256], P('tensor', 'dp')
- grad_w_igate: float32 [10, 256, 256], P('tensor', 'dp')
- grad_rgate_bias: float32 [10, 256], P('tensor', 'dp')
- grad_igate_bias: float32 [10, 256], P('tensor', 'dp')
- grad_decay_param: float32 [10, 256], P('tensor', 'dp')
- grad_conv_weight: float32 [4, 10, 256], P(None, 'tensor', 'dp')
- grad_conv_bias: float32 [10, 256], P('tensor', 'dp')
- grad_w_output: float32 [2560, 2048], P('tensor', 'dp')
- grad_mlp_gain: float32 [2048], P('dp')
- grad_w_gate: float32 [2048, 6144], P('dp', 'tensor')
- grad_w_up: float32 [2048, 6144], P('dp', 'tensor')
- grad_w_down: float32 [6144, 2048], P('tensor', 'dp')
The draws below stay inside these ranges and needn't reach their ends.
Inputs may be any that keep to these rules, and one draw needn't show every extreme that they name: `doc_lengths`: in each row the 4 lengths are documents placed one after another from the row's first position, the first at least one token long; together they cover more than 128 positions and the positions after them are padding.
All inputs are finite; a program needn't handle non-finite values.
Results may differ from the reference program's by a relative error of at most 0.015.
Values may be sent and summed in bfloat16 or wider, within the bound.
A program may use at most 256 MiB of HBM per device.

```python
import jax
import jax.numpy as jnp
from jax import lax

D = 2048
FF = 6144
HEADS = 10
BLK = 256
CONV = 4
SEQ = 256
LRU = 2560
BATCH = 16


def draw_doc_lengths(key, part):
    keys = jax.random.split(key, 5)
    total = jax.random.randint(keys[0], (BATCH,), SEQ // 2 + 2, SEQ + 1)
    first = jax.random.randint(keys[1], (BATCH,), 1, SEQ // 2)
    second_end = jax.random.randint(keys[2], (BATCH,), SEQ // 2 + 1, total + 1)
    third_end = jax.random.randint(keys[3], (BATCH,), second_end, total + 1)
    picked = jax.random.randint(keys[4], (), 0, BATCH)
    chosen = jnp.arange(BATCH, dtype=jnp.int32) == picked
    total = jnp.where(chosen, SEQ, total)
    first = jnp.where(chosen, 1, first)
    second_end = jnp.where(chosen, SEQ, second_end)
    third_end = jnp.where(chosen, SEQ, third_end)
    lengths = jnp.stack([first, second_end - first, third_end - second_end, total - third_end], axis=1)
    return lengths.astype(jnp.int32)


def strengthened(drawn, rng, source, target, shards_of, factor):
    def block_of(position):
        return (jnp.arange(drawn.shape[position]) // (drawn.shape[position] // shards_of)).reshape((-1,) + (1,) * (drawn.ndim - 1 - position))

    one_side = jax.random.permutation(rng, shards_of)[block_of(target)]
    far = (block_of(target) + shards_of // 2) % shards_of
    return jnp.where((block_of(source) == one_side) | (block_of(source) == far), factor * drawn, drawn)


def levels(rng, shape, pieces, smallest, top_value):
    def one(position, blocks):
        draws = jax.random.uniform(jax.random.fold_in(jax.random.fold_in(rng, 6), position), (blocks,), jnp.float32, smallest / len(pieces), top_value / len(pieces))
        return jnp.repeat(jnp.exp(draws), shape[position] // blocks).reshape((-1,) + (1,) * (len(shape) - position - 1))

    factor_of = one(*pieces[0])
    for cut in pieces[1:]:
        factor_of = factor_of * one(*cut)
    return factor_of


def scatter_about(own_key, extent, deviation, reach, pieces=(), kind=jnp.bfloat16):
    loudness = levels(own_key, extent, pieces, -0.22, 0.18) if pieces else 1.0
    values = jax.random.normal(own_key, extent, jnp.float32) * deviation * loudness
    return jnp.minimum(jnp.maximum(values, -reach), reach).astype(kind)


def heavy_noise(key, dims, scale, most, pieces, heavy, kind=jnp.bfloat16):
    entries = scale * jax.random.normal(key, dims, jnp.float32)
    if pieces:
        entries = entries * levels(key, dims, pieces, -0.22, 0.18)
    return jnp.clip(strengthened(entries, jax.random.fold_in(key, 3), *heavy), -most, most).astype(kind)


def setup_inputs(seed: int = 0) -> dict:
    arg_keys = jax.random.split(jax.random.key(seed), 19)
    return {
        "tokens": heavy_noise(arg_keys[0], (BATCH, SEQ, D), 1.0, 6.0, ((0, 16), (1, 2)), (0, 2, 16, 2.0)),
        "doc_lengths": draw_doc_lengths(jax.random.fold_in(arg_keys[18], 71), 0),
        "recurrent_norm_gain": jnp.clip(1.0 + 0.15 * jax.random.normal(arg_keys[2], (D,), jnp.float32), 0.25, 1.75).astype(jnp.bfloat16),
        "w_branch": scatter_about(arg_keys[3], (D, LRU), D ** -0.5, 0.125, ((0, 16), (1, 2))),
        "w_input": scatter_about(arg_keys[4], (D, LRU), D ** -0.5, 0.125, ((0, 16), (1, 2))),
        "w_rgate": scatter_about(arg_keys[5], (HEADS, BLK, BLK), BLK ** -0.5, 0.375, ((0, 2), (1, 16))),
        "w_igate": scatter_about(arg_keys[6], (HEADS, BLK, BLK), BLK ** -0.5, 0.375, ((0, 2), (1, 16))),
        "rgate_bias": scatter_about(arg_keys[7], (HEADS, BLK), 0.5, 3.0, ((0, 2), (1, 16))),
        "igate_bias": scatter_about(arg_keys[8], (HEADS, BLK), 0.5, 3.0, ((0, 2), (1, 16))),
        "decay_param": jnp.clip(4.1875 + 4.3125 * jax.random.uniform(arg_keys[9], (HEADS, BLK), jnp.float32) ** levels(arg_keys[9], (HEADS, BLK), ((0, 2), (1, 16)), -0.2, 0.2), 4.1875, 8.5).astype(jnp.bfloat16),
        "conv_weight": scatter_about(arg_keys[10], (CONV, HEADS, BLK), 0.5, 3.0, ((1, 2), (2, 16))),
        "conv_bias": scatter_about(arg_keys[11], (HEADS, BLK), 0.3, 2.0, ((0, 2), (1, 16))),
        "w_output": scatter_about(arg_keys[12], (LRU, D), (HEADS * BLK // 4) ** -0.5, 0.25, ((0, 2), (1, 16))),
        "perceptron_norm_gain": jnp.clip(1.0 + 0.15 * jax.random.normal(arg_keys[13], (D,), jnp.float32), 0.25, 1.75).astype(jnp.bfloat16),
        "w_gate": scatter_about(arg_keys[14], (D, FF), D ** -0.5, 0.125, ((0, 16), (1, 2))),
        "w_up": scatter_about(arg_keys[15], (D, FF), D ** -0.5, 0.125, ((0, 16), (1, 2))),
        "w_down": scatter_about(arg_keys[16], (FF, D), FF ** -0.5, 0.078125, ((0, 2), (1, 16))),
        "cotangent": heavy_noise(arg_keys[17], (BATCH, SEQ, D), 1.0, 6.0, ((0, 16), (1, 2)), (0, 2, 16, 2.0), jnp.float32),
    }


highest = lax.Precision.HIGHEST
norm_epsilon = 1e-06
decay_scale = 8.0

@jax.custom_vjp
def reduced_precision(v):
    return lax.optimization_barrier(v.astype(jnp.bfloat16)).astype(jnp.float32)

@jax.custom_vjp
def low_back(v):
    return v

def low_keep(v):
    return (reduced_precision(v), None)

def low_pass(kept, grad):
    return (grad,)

def back_keep(v):
    return (v, None)

def back_low(kept, grad):
    return (reduced_precision(grad),)
reduced_precision.defvjp(low_keep, low_pass)
low_back.defvjp(back_keep, back_low)

def gelu_tanh(values):
    return jax.nn.gelu(values, approximate=True)

def combine(first, second):
    return (first[0] * second[0], second[0] * first[1] + second[1])

def doc_layout(doc_lengths, length):
    ends = jnp.cumsum(doc_lengths, axis=-1).astype(jnp.int32)
    places = jnp.arange(length, dtype=jnp.int32)
    segment = lax.optimization_barrier(jnp.sum((places[None, :, None] >= ends[:, None, :]).astype(jnp.int32), axis=-1)).astype(jnp.int32)
    valid = places[None, :] < ends[:, -1:]
    earlier = jnp.pad(segment, ((0, 0), (1, 0)), constant_values=-1)[:, :-1]
    start = earlier != segment
    return (segment, valid, start)

def conv_mix(values, weights, bias, segment):
    total = values * weights[0] + bias
    for shift in range(1, weights.shape[0]):
        moved = jnp.pad(values, ((0, 0), (shift, 0), (0, 0)))[:, :-shift]
        earlier = jnp.pad(segment, ((0, 0), (shift, 0)), constant_values=-1)[:, :-shift]
        total = total + jnp.where((earlier == segment)[..., None], moved, 0.0) * weights[shift]
    return total

def gate_terms(pre_r, pre_i, conv_out, decay_row, start_col):
    rate = jax.nn.sigmoid(pre_r)
    entry = jax.nn.sigmoid(pre_i)
    log_decay = -decay_scale * rate * jax.nn.softplus(-decay_row)
    a_eff = jnp.where(start_col, 0.0, jnp.exp(log_decay))
    scaling = jnp.where(start_col, 1.0, jnp.sqrt(-jnp.expm1(2.0 * log_decay)))
    return (a_eff, scaling * entry * conv_out)

def forward(layer_input_rows, recurrent_norm_gain, w_branch, w_input, w_rgate, w_igate, rgate_bias, igate_bias, decay_param, conv_weight, conv_bias, w_output, perceptron_norm_gain, w_gate, w_up, w_down, segment, valid, start):
    row_count, length, width = layer_input_rows.shape
    head_count, block_size = rgate_bias.shape
    channels = head_count * block_size
    centered_rows1 = layer_input_rows * lax.rsqrt(lax.optimization_barrier(jnp.mean(layer_input_rows * layer_input_rows, axis=-1, keepdims=True)) + norm_epsilon)
    normalized_input_rows = reduced_precision(centered_rows1 * recurrent_norm_gain)
    branch_pre = low_back(jnp.einsum('rld,dc->rlc', normalized_input_rows, w_branch, precision=highest))
    conv_in = low_back(jnp.einsum('rld,dc->rlc', normalized_input_rows, w_input, precision=highest))
    conv_out = conv_mix(conv_in, conv_weight.reshape(-1, channels), conv_bias.reshape(channels), segment)
    conv_low = reduced_precision(conv_out).reshape(row_count, length, head_count, block_size)
    pre_r = low_back(jnp.einsum('rlhi,hij->rlhj', conv_low, w_rgate, precision=highest)) + rgate_bias
    pre_i = low_back(jnp.einsum('rlhi,hij->rlhj', conv_low, w_igate, precision=highest)) + igate_bias
    a_eff, drive = gate_terms(pre_r.reshape(row_count, length, channels), pre_i.reshape(row_count, length, channels), conv_out, decay_param.reshape(channels), start[..., None])
    state = lax.associative_scan(combine, (a_eff, drive), axis=1)[1]
    mixed = reduced_precision(state * gelu_tanh(branch_pre))
    rec_out = low_back(jnp.einsum('rlc,cd->rld', mixed, w_output, precision=highest))
    residual_stream = layer_input_rows + rec_out
    centered_rows2 = residual_stream * lax.rsqrt(lax.optimization_barrier(jnp.mean(residual_stream * residual_stream, axis=-1, keepdims=True)) + norm_epsilon)
    normalized_rows = reduced_precision(centered_rows2 * perceptron_norm_gain)
    gate_pre = low_back(jnp.einsum('rld,df->rlf', normalized_rows, w_gate, precision=highest))
    up_pre = low_back(jnp.einsum('rld,df->rlf', normalized_rows, w_up, precision=highest))
    hidden = reduced_precision(gelu_tanh(gate_pre) * up_pre)
    mlp_out = low_back(jnp.einsum('rlf,fd->rld', hidden, w_down, precision=highest))
    return jnp.where(valid[..., None], residual_stream + mlp_out, 0.0)

def reference(tokens, doc_lengths, recurrent_norm_gain, w_branch, w_input, w_rgate, w_igate, rgate_bias, igate_bias, decay_param, conv_weight, conv_bias, w_output, perceptron_norm_gain, w_gate, w_up, w_down, cotangent):
    params = tuple((item.astype(jnp.float32) for item in (recurrent_norm_gain, w_branch, w_input, w_rgate, w_igate, rgate_bias, igate_bias, decay_param, conv_weight, conv_bias, w_output, perceptron_norm_gain, w_gate, w_up, w_down)))
    row_total, length = (doc_lengths.shape[0], tokens.shape[1])
    segment, valid, start = doc_layout(doc_lengths, length)
    group = 1
    while group * 2 * length <= 4096 and row_total % (group * 2) == 0:
        group = group * 2
    count = row_total // group

    def regroup(array):
        return array.reshape((count, group) + array.shape[1:])
    items = (regroup(tokens.astype(jnp.float32)), regroup(cotangent.astype(jnp.float32)), regroup(segment), regroup(valid), regroup(start))
    zeros = tuple((jnp.zeros(item.shape, jnp.float32) for item in params))

    def step(totals, item):
        layer_input_rows, grads_out, seg_part, valid_part, start_part = item

        def run(values, *weights):
            return forward(values, *weights, seg_part, valid_part, start_part)
        value, back = jax.vjp(run, layer_input_rows, *params)
        grads = back(grads_out)
        totals = tuple((left + right for left, right in zip(totals, grads[1:])))
        return (totals, (value.astype(jnp.bfloat16), grads[0]))
    totals, (outputs, input_grads) = lax.scan(step, zeros, items)
    result = outputs.reshape(tokens.shape)
    token_input_gradient = input_grads.reshape(tokens.shape)
    return (result, token_input_gradient, totals[0], totals[1], totals[2], totals[3], totals[4], totals[5], totals[6], totals[7], totals[8], totals[9], totals[10], totals[11], totals[12], totals[13], totals[14])
```

```python
import functools

import jax
import jax.numpy as jnp
from jax import lax
from jax.experimental import pallas as pl
from jax.experimental.pallas import tpu as pltpu
from jax.sharding import PartitionSpec as P

MESH = pl.DeviceIdType.MESH
BF = jnp.bfloat16
F32 = jnp.float32
EPS = 1e-06
DECAY = 8.0
GC = 0.7978845608028654
GK = 0.044715
VMEM_LIMIT = 60 * 1024 * 1024


def dp_at(zh, zl, y, x):
    return ((zh * 2 + zl) * 2 + y) * 2 + x


def place():
    dp = lax.axis_index("dp")
    return dp // 8, (dp // 4) % 2, (dp // 2) % 2, dp % 2, lax.axis_index("tensor")


def dev(dp, core):
    return {"dp": dp, "tensor": core}


def greet(devices):
    sem = pltpu.get_barrier_semaphore()
    for d in devices:
        pl.semaphore_signal(sem, inc=1, device_id=d, device_id_type=MESH)
    pl.semaphore_wait(sem, len(devices))


def remote(src, dst, ssem, rsem, d):
    return pltpu.make_async_remote_copy(
        src_ref=src, dst_ref=dst, send_sem=ssem, recv_sem=rsem, device_id=d, device_id_type=MESH
    )


def peers_of_group(zh, zl, y, x):
    out = []
    for kl, kx in ((0, 1), (1, 0), (1, 1)):
        pz, px = (zl + kl) % 2, (x + kx) % 2
        out.append((pz * 2 + px, dp_at(zh, pz, y, px)))
    return out


def act_gather_kernel(x_ref, out_ref, send, recv, fsend, frecv, local):
    zh, zl, y, x, c = place()
    q, me = zl * 2 + x, dp_at(zh, zl, y, x)
    sib = dev(me, 1 - c)
    peers = peers_of_group(zh, zl, y, x)
    greet([sib] + [dev(d, c) for _, d in peers])
    own = pltpu.make_async_copy(x_ref, out_ref.at[q, c], local)
    own.start()
    copies = []
    for k, (pq, d) in enumerate(peers):
        cp = remote(x_ref, out_ref.at[q, c], send.at[k], recv.at[q], dev(d, c))
        cp.start()
        copies.append(cp)
    fwd = [remote(x_ref, out_ref.at[q, c], fsend.at[3], frecv.at[q], sib)]
    fwd[0].start()
    for k, (pq, d) in enumerate(peers):
        land = out_ref.at[pq, c]
        remote(land, land, send.at[k], recv.at[pq], dev(d, c)).wait_recv()
        cp = remote(land, land, fsend.at[k], frecv.at[pq], sib)
        cp.start()
        fwd.append(cp)
    for j in range(4):
        land = out_ref.at[j, 1 - c]
        remote(land, land, fsend.at[0], frecv.at[j], sib).wait_recv()
    for cp in copies + fwd:
        cp.wait_send()
    own.wait()


def act_gather(x, cid):
    half, width = x.shape
    return pl.pallas_call(
        act_gather_kernel,
        out_shape=jax.ShapeDtypeStruct((4, 2, half, width), x.dtype),
        in_specs=[pl.BlockSpec(memory_space=pl.ANY)],
        out_specs=pl.BlockSpec(memory_space=pl.ANY),
        scratch_shapes=[
            pltpu.SemaphoreType.DMA((3,)),
            pltpu.SemaphoreType.DMA((4,)),
            pltpu.SemaphoreType.DMA((4,)),
            pltpu.SemaphoreType.DMA((4,)),
            pltpu.SemaphoreType.DMA,
        ],
        compiler_params=pltpu.CompilerParams(collective_id=cid, has_side_effects=True),
        name="act_gather",
    )(x)


def act_reduce_kernel(p_ref, out_ref, sbuf, tbuf, rbuf, ssend, srecv, send, recv):
    zh, zl, y, x, c = place()
    q, me = zl * 2 + x, dp_at(zh, zl, y, x)
    sib = dev(me, 1 - c)
    peers = peers_of_group(zh, zl, y, x)
    greet([sib] + [dev(d, c) for _, d in peers])
    order = [peers[2], peers[1], peers[0], (q, me)]
    half = []
    for k, (pq, d) in enumerate(order):
        cp = remote(p_ref.at[pq, 1 - c], sbuf.at[pq], ssend.at[k], srecv.at[pq], sib)
        cp.start()
        half.append(cp)
    out = []
    for k, (pq, d) in enumerate(order):
        remote(sbuf.at[pq], sbuf.at[pq], ssend.at[k], srecv.at[pq], sib).wait_recv()
        total = p_ref[pq, c].astype(F32) + sbuf[pq].astype(F32)
        if k < 3:
            tbuf[k] = total.astype(BF)
            cp = remote(tbuf.at[k], rbuf.at[q], send.at[k], recv.at[q], dev(d, c))
            cp.start()
            out.append(cp)
        else:
            out_ref[...] = total
    for pq, d in peers:
        remote(rbuf.at[pq], rbuf.at[pq], send.at[0], recv.at[pq], dev(d, c)).wait_recv()
        out_ref[...] += rbuf[pq].astype(F32)
    for cp in half + out:
        cp.wait_send()


def act_reduce(parts, cid):
    _, _, half, width = parts.shape
    vm = pl.BlockSpec(memory_space=pltpu.VMEM)
    return pl.pallas_call(
        act_reduce_kernel,
        out_shape=jax.ShapeDtypeStruct((half, width), F32),
        in_specs=[vm],
        out_specs=vm,
        scratch_shapes=[
            pltpu.VMEM((4, half, width), BF),
            pltpu.VMEM((3, half, width), BF),
            pltpu.VMEM((4, half, width), BF),
            pltpu.SemaphoreType.DMA((4,)),
            pltpu.SemaphoreType.DMA((4,)),
            pltpu.SemaphoreType.DMA((3,)),
            pltpu.SemaphoreType.DMA((4,)),
        ],
        compiler_params=pltpu.CompilerParams(
            collective_id=cid, has_side_effects=True, vmem_limit_bytes=VMEM_LIMIT
        ),
        name="act_reduce",
    )(parts)


def plane(zh, zl, y, x, high):
    out = []
    for kh in range(high):
        for kl in range(2):
            for kx in range(2):
                ph, pz, px = (zh + kh) % high, (zl + kl) % 2, (x + kx) % 2
                out.append((ph, pz, px))
    return out


def weight_gather_kernel(high, narr, picked, *refs):
    src, dst = refs[:narr], refs[narr : 2 * narr]
    send, recv, fsend, local = refs[2 * narr :]
    zh, zl, y, x, c = place()
    me = dp_at(zh, zl, y, x)
    there = plane(zh, zl, y, x, high)
    other = dev(dp_at(zh, zl, 1 - y, x), c)
    greet([dev(dp_at(h, z, y, w), c) for h, z, w in there[1:]] + [other])
    pend = []
    for a in range(narr):
        for k, (h, z, w) in enumerate(there):
            piece = src[a].at[z * 2 + w] if picked[a] else src[a]
            if k == 0:
                cp = pltpu.make_async_copy(piece, dst[a].at[me], local.at[a])
            else:
                cp = remote(piece, dst[a].at[me], send.at[a, k], recv.at[a, me], dev(dp_at(h, z, y, w), c))
            cp.start()
            pend.append((k, cp))
    for a in range(narr):
        for k, (h, z, w) in enumerate(there):
            s = dp_at(h, z, y, w)
            land = dst[a].at[s]
            if k == 0:
                pend[a * len(there)][1].wait()
            else:
                remote(land, land, send.at[a, k], recv.at[a, s], other).wait_recv()
            cp = remote(land, land, fsend.at[a, k], recv.at[a, s], other)
            cp.start()
            pend.append((1, cp))
    for a in range(narr):
        for k, (h, z, w) in enumerate(there):
            s = dp_at(h, z, 1 - y, w)
            land = dst[a].at[s]
            remote(land, land, fsend.at[a, k], recv.at[a, s], other).wait_recv()
    for k, cp in pend:
        if k:
            cp.wait_send()


def weight_gather(arrays, picked, n, cid):
    high = n // 8
    narr = len(arrays)
    shapes = tuple(
        jax.ShapeDtypeStruct((n,) + (a.shape[1:] if p else a.shape), a.dtype) for a, p in zip(arrays, picked)
    )
    anyspec = pl.BlockSpec(memory_space=pl.ANY)
    return pl.pallas_call(
        functools.partial(weight_gather_kernel, high, narr, picked),
        out_shape=shapes,
        in_specs=[anyspec] * narr,
        out_specs=[anyspec] * narr,
        scratch_shapes=[
            pltpu.SemaphoreType.DMA((narr, high * 4)),
            pltpu.SemaphoreType.DMA((narr, n)),
            pltpu.SemaphoreType.DMA((narr, high * 4)),
            pltpu.SemaphoreType.DMA((narr,)),
        ],
        compiler_params=pltpu.CompilerParams(collective_id=cid, has_side_effects=True),
        name="weight_gather",
    )(*arrays)


def grad_reduce_kernel(high, narr, picked, *refs):
    src, dst = refs[:narr], refs[narr : 2 * narr]
    ybuf, tbuf, rbuf = (refs[(2 + i) * narr : (3 + i) * narr] for i in range(3))
    ysend, yrecv, send, recv = refs[5 * narr :]
    zh, zl, y, x, c = place()
    q = zl * 2 + x
    there = plane(zh, zl, y, x, high)
    other = dev(dp_at(zh, zl, 1 - y, x), c)
    greet([dev(dp_at(h, z, y, w), c) for h, z, w in there[1:]] + [other])
    mine = zh * 4 + q
    order = there[1:] + there[:1]
    pend = []
    for a in range(narr):
        for h, z, w in order:
            j = h * 4 + z * 2 + w
            cp = remote(src[a].at[dp_at(h, z, 1 - y, w)], ybuf[a].at[j], ysend.at[a, j], yrecv.at[a, j], other)
            cp.start()
            pend.append(cp)
    for a in range(narr):
        for k, (h, z, w) in enumerate(order):
            j = h * 4 + z * 2 + w
            remote(ybuf[a].at[j], ybuf[a].at[j], ysend.at[a, j], yrecv.at[a, j], other).wait_recv()
            total = src[a][dp_at(h, z, y, w)].astype(F32) + ybuf[a][j].astype(F32)
            if k < len(order) - 1:
                tbuf[a][j] = total.astype(tbuf[a].dtype)
                cp = remote(
                    tbuf[a].at[j], rbuf[a].at[mine], send.at[a, j], recv.at[a, mine], dev(dp_at(h, z, y, w), c)
                )
                cp.start()
                pend.append(cp)
            elif picked[a]:
                dst[a][...] = jnp.zeros(dst[a].shape, F32)
                dst[a][q] = total
            else:
                dst[a][...] = total
    for a in range(narr):
        for h, z, w in there[1:]:
            j = h * 4 + z * 2 + w
            remote(rbuf[a].at[j], rbuf[a].at[j], send.at[a, j], recv.at[a, j], other).wait_recv()
            if picked[a]:
                dst[a][z * 2 + w] += rbuf[a][j].astype(F32)
            else:
                dst[a][...] += rbuf[a][j].astype(F32)
    for cp in pend:
        cp.wait_send()


def grad_reduce(arrays, picked, n, cid):
    high = n // 8
    narr = len(arrays)
    vm = pl.BlockSpec(memory_space=pltpu.VMEM)
    shapes = tuple(
        jax.ShapeDtypeStruct(((4,) if p else ()) + a.shape[1:], F32) for a, p in zip(arrays, picked)
    )
    bufs = [pltpu.VMEM((high * 4,) + a.shape[1:], a.dtype) for a in arrays]
    return pl.pallas_call(
        functools.partial(grad_reduce_kernel, high, narr, picked),
        out_shape=shapes,
        in_specs=[vm] * narr,
        out_specs=[vm] * narr,
        scratch_shapes=bufs * 3 + [pltpu.SemaphoreType.DMA((narr, high * 4))] * 4,
        compiler_params=pltpu.CompilerParams(
            collective_id=cid, has_side_effects=True, vmem_limit_bytes=VMEM_LIMIT
        ),
        name="grad_reduce",
    )(*arrays)


def gelu_parts(v):
    t = jnp.tanh(GC * (v + GK * v * v * v))
    act = 0.5 * v * (1.0 + t)
    der = 0.5 * (1.0 + t) + 0.5 * v * (1.0 - t * t) * GC * (1.0 + 3.0 * GK * v * v)
    return act, der


def segments(ends, length, width, taps):
    t = lax.broadcasted_iota(jnp.int32, (length, width), 0).astype(F32)

    def seg(at):
        total = jnp.zeros((length, width), F32)
        for j in range(4):
            total = total + jnp.where(at >= ends[:, j : j + 1], 1.0, 0.0)
        return total

    here = seg(t)
    same = []
    for k in range(1, taps):
        same.append(jnp.where((t >= float(k)) & (seg(t - float(k)) == here), 1.0, 0.0))
    return same


def scan8(a, b, reverse):
    length, width = a.shape
    row = lax.broadcasted_iota(jnp.int32, (length, width), 0) % 8
    for d in (1, 2, 4):
        if reverse:
            ash, bsh = pltpu.roll(a, length - d, 0), pltpu.roll(b, length - d, 0)
            ok = row < 8 - d
        else:
            ash, bsh = pltpu.roll(a, d, 0), pltpu.roll(b, d, 0)
            ok = row >= d
        b = b + a * jnp.where(ok, bsh, 0.0)
        a = a * jnp.where(ok, ash, 1.0)
    return a, b


def full_scan(a, b, out_ref, a_ref, reverse):
    length, width = a.shape
    a8, b8 = scan8(a, b, reverse)
    a_ref[...] = a8
    out_ref[...] = b8
    blocks = length // 8

    def step(i, carry):
        at = (blocks - 1 - i if reverse else i) * 8
        at = pl.multiple_of(at, 8)
        now = out_ref[pl.ds(at, 8), :] + a_ref[pl.ds(at, 8), :] * carry
        out_ref[pl.ds(at, 8), :] = now
        return now[0:1, :] if reverse else now[7:8, :]

    lax.fori_loop(0, blocks, step, jnp.zeros((1, width), F32))


def rec_forward_kernel(taps, p_ref, g_ref, v_ref, e_ref, mixed_ref, conv_ref, r_ref, i_ref, state_ref, a_ref):
    length, two = p_ref.shape[1:]
    blk = two // 2
    branch, conv_in = p_ref[0, :, :blk], p_ref[0, :, blk:]
    vec = v_ref[0]
    same = segments(e_ref[0, 0:1, :], length, blk, taps)
    conv = conv_in * vec[4:5] + vec[4 + taps : 5 + taps]
    for k in range(1, taps):
        conv = conv + pltpu.roll(conv_in, k, 0) * same[k - 1] * vec[4 + k : 5 + k]
    pre = jnp.dot(conv.astype(BF), g_ref[0], preferred_element_type=F32)
    r = jax.nn.sigmoid(pre[:, :blk] + vec[0:1])
    gate = jax.nn.sigmoid(pre[:, blk:] + vec[1:2])
    log_a = (-DECAY * r) * vec[2:3]
    a = jnp.exp(log_a)
    start = same[0] == 0.0
    a_eff = jnp.where(start, 0.0, a)
    mult = jnp.where(start, 1.0, jnp.sqrt(-jnp.tanh(log_a) * (1.0 + a * a)))
    full_scan(a_eff, mult * gate * conv, state_ref.at[0], a_ref, False)
    act, _ = gelu_parts(branch)
    mixed_ref[0] = (state_ref[0] * act).astype(BF)
    conv_ref[0] = conv
    r_ref[0] = r
    i_ref[0] = gate


def rec_backward_kernel(
    taps, p_ref, g_ref, v_ref, e_ref, conv_ref, r_ref, i_ref, state_ref, m_ref,
    low_ref, gg_ref, vg_ref, carry_ref, a_ref,
):
    unit = pl.program_id(0)
    length, two = p_ref.shape[1:]
    blk = two // 2
    branch, conv_in = p_ref[0, :, :blk], p_ref[0, :, blk:]
    vec = v_ref[0]
    same = segments(e_ref[0, 0:1, :], length, blk, taps)
    start = same[0] == 0.0
    r, gate, conv, state, mg = r_ref[0], i_ref[0], conv_ref[0], state_ref[0], m_ref[0]
    act, der = gelu_parts(branch)
    low_ref[0, :, :blk] = (mg * state * der).astype(BF)
    log_a = (-DECAY * r) * vec[2:3]
    a = jnp.exp(log_a)
    a_eff = jnp.where(start, 0.0, a)
    row = lax.broadcasted_iota(jnp.int32, (length, blk), 0)
    a_next = jnp.where(row < length - 1, pltpu.roll(a_eff, length - 1, 0), 0.0)
    full_scan(a_next, mg * act, carry_ref, a_ref, True)
    carry = carry_ref[...]
    prev = jnp.where(row > 0, pltpu.roll(state, 1, 0), 0.0)
    raw = jnp.sqrt(-jnp.tanh(log_a) * (1.0 + a * a))
    mult = jnp.where(start, 1.0, raw)
    log_grad = jnp.where(start, 0.0, carry * prev * a - carry * gate * conv * (a * a) / raw)
    r_grad = log_grad * (-DECAY * vec[2:3]) * (r * (1.0 - r))
    i_grad = carry * mult * conv * (gate * (1.0 - gate))
    pre_low = jnp.concatenate([r_grad.astype(BF), i_grad.astype(BF)], axis=1)
    conv_grad = carry * mult * gate + lax.dot_general(
        pre_low, g_ref[0], (((1,), (1,)), ((), ())), preferred_element_type=F32
    )
    gg = lax.dot_general(conv.astype(BF), pre_low, (((0,), (0,)), ((), ())), preferred_element_type=F32)

    def total(v):
        return jnp.sum(v, axis=0, keepdims=True)

    rows = [total(r_grad), total(i_grad), total(log_grad * (DECAY * r) * vec[3:4]), total(conv_grad)]
    inp = conv_grad * vec[4:5]
    rows.append(total(conv_grad * conv_in))
    for k in range(1, taps):
        masked = conv_grad * same[k - 1]
        rows.append(total(masked * pltpu.roll(conv_in, k, 0)))
        inp = inp + pltpu.roll(masked, length - k, 0) * vec[4 + k : 5 + k]
    low_ref[0, :, blk:] = inp.astype(BF)
    vg = jnp.concatenate(rows, axis=0)

    @pl.when((unit == 0) | (unit == 4))
    def _():
        gg_ref[0] = gg
        vg_ref[0] = vg

    @pl.when((unit != 0) & (unit != 4))
    def _():
        gg_ref[0] += gg
        vg_ref[0] += vg


def unit_spec(a):
    return pl.BlockSpec((1,) + a.shape[1:], lambda u: (u, 0, 0))


def head_spec(a):
    return pl.BlockSpec((1,) + a.shape[1:], lambda u: (u // 4, 0, 0))


def rec_forward(taps, pre, gates, vec, ends):
    units, length, two = pre.shape
    blk = two // 2
    block = pl.BlockSpec((1, length, blk), lambda u: (u, 0, 0))
    f32 = jax.ShapeDtypeStruct((units, length, blk), F32)
    return pl.pallas_call(
        functools.partial(rec_forward_kernel, taps),
        grid=(units,),
        out_shape=(jax.ShapeDtypeStruct((units, length, blk), BF), f32, f32, f32, f32),
        in_specs=[unit_spec(pre), head_spec(gates), head_spec(vec), unit_spec(ends)],
        out_specs=[block] * 5,
        scratch_shapes=[pltpu.VMEM((length, blk), F32)],
        compiler_params=pltpu.CompilerParams(vmem_limit_bytes=VMEM_LIMIT),
        name="rec_forward",
    )(pre, gates, vec, ends)


def rec_backward(taps, pre, gates, vec, ends, conv, r, gate, state, mixed_grad):
    units, length, two = pre.shape
    blk = two // 2
    vrows = 4 + taps
    return pl.pallas_call(
        functools.partial(rec_backward_kernel, taps),
        grid=(units,),
        out_shape=(
            jax.ShapeDtypeStruct((units, length, two), BF),
            jax.ShapeDtypeStruct((2, blk, two), F32),
            jax.ShapeDtypeStruct((2, vrows, blk), F32),
        ),
        in_specs=[unit_spec(pre), head_spec(gates), head_spec(vec), unit_spec(ends)]
        + [unit_spec(conv)] * 5,
        out_specs=[
            unit_spec(pre),
            pl.BlockSpec((1, blk, two), lambda u: (u // 4, 0, 0)),
            pl.BlockSpec((1, vrows, blk), lambda u: (u // 4, 0, 0)),
        ],
        scratch_shapes=[pltpu.VMEM((length, blk), F32)] * 2,
        compiler_params=pltpu.CompilerParams(vmem_limit_bytes=VMEM_LIMIT),
        name="rec_backward",
    )(pre, gates, vec, ends, conv, r, gate, state, mixed_grad)


def mm(a, b):
    return jnp.dot(a, b, preferred_element_type=F32)


def mm_t(a, b):
    return lax.dot_general(a, b, (((1,), (1,)), ((), ())), preferred_element_type=F32)


def t_mm(a, b):
    return lax.dot_general(a, b, (((0,), (0,)), ((), ())), preferred_element_type=F32)


def gelu_tanh(values):
    return jax.nn.gelu(values, approximate=True)


def norm_scale(values):
    return lax.rsqrt(jnp.mean(values * values, axis=-1, keepdims=True) + EPS)


def norm_back(grad, unit, inverse):
    return inverse * (grad - unit * jnp.mean(grad * unit, axis=-1, keepdims=True))


def local(
    tokens, doc_lengths, rec_gain, w_branch, w_input, w_rgate, w_igate, rgate_bias, igate_bias,
    decay_param, conv_weight, conv_bias, w_output, mlp_gain, w_gate, w_up, w_down, cotangent,
):
    n = lax.axis_size("dp")
    zh, zl, y, x, c = place()
    q = zl * 2 + x
    _, half, width = tokens.shape
    length = half * 2
    heads, rb, blk = w_rgate.shape
    taps = conv_weight.shape[0]
    rows = w_branch.shape[0]
    ff = w_gate.shape[1] // 4

    def by_head(w):
        return w.reshape(rows, heads, blk)

    rec_piece = jnp.concatenate([by_head(w_branch), by_head(w_input), by_head(w_output.T)], axis=2)
    rec_piece = rec_piece.transpose(1, 0, 2)

    def by_quarter(w):
        return w.reshape(rows, 4, ff)

    mlp_piece = jnp.concatenate([by_quarter(w_gate), by_quarter(w_up), by_quarter(w_down.T)], axis=2)
    mlp_piece = mlp_piece.transpose(1, 0, 2)
    gate_piece = jnp.concatenate([w_rgate, w_igate], axis=2)
    d32 = decay_param.astype(F32)
    vecs = jnp.stack(
        [rgate_bias.astype(F32), igate_bias.astype(F32), jax.nn.softplus(-d32), jax.nn.sigmoid(-d32)]
        + [conv_weight[k].astype(F32) for k in range(taps)]
        + [conv_bias.astype(F32)]
    )
    nv = vecs.shape[0]
    vecs = jnp.pad(vecs.reshape(nv, heads * rb), ((0, 0), (0, 128 - heads * rb)))
    lens = doc_lengths.reshape(4).astype(F32)
    e0 = lens[0]
    e1 = e0 + lens[1]
    e2 = e1 + lens[2]
    e3 = e2 + lens[3]
    ends_own = jnp.stack([e0, e1, e2, e3])

    def line(v):
        v = v.astype(F32).reshape(1, -1)
        return jnp.pad(v, ((0, 0), (0, 128 - v.shape[1])))

    smalls = jnp.concatenate([vecs, line(rec_gain), line(mlp_gain), line(ends_own)], axis=0)
    smalls = jnp.pad(smalls, ((0, 16 - smalls.shape[0]), (0, 0)))

    recq, rec4, gq, g4, small, mlp = weight_gather(
        (rec_piece[:4], rec_piece[4], gate_piece[:4], gate_piece[4], smalls, mlp_piece),
        (True, False, True, False, False, True), n, 1,
    )
    recq, rec4, mlp = recq.reshape(width, -1), rec4.reshape(width, -1), mlp.reshape(width, -1)
    gates = jnp.stack([gq.reshape(blk, 2 * blk), g4.reshape(blk, 2 * blk)])
    vec_all = small[:, :nv, : heads * rb].reshape(n, nv, heads, rb).transpose(2, 1, 0, 3).reshape(heads, nv, blk)
    vec = jnp.stack([lax.dynamic_index_in_dim(vec_all, q, 0, False), vec_all[4]])
    vec = jnp.pad(vec, ((0, 0), (0, 16 - nv), (0, 0)))
    gain1 = small[:, nv, :rows].reshape(1, width)
    gain2 = small[:, nv + 1, :rows].reshape(1, width)
    group_ends = small[:, nv + 2].reshape(n // 8, 2, 2, 2, 128)
    group_ends = lax.dynamic_index_in_dim(group_ends, zh, 0, False)
    group_ends = lax.dynamic_index_in_dim(group_ends, y, 1, False).reshape(4, 128)
    own_ends = lax.dynamic_index_in_dim(group_ends, q, 0, True)
    ends = jnp.concatenate([group_ends, own_ends], axis=0)[:, None, :]
    ends = jnp.broadcast_to(ends, (5, 8, 128))
    valid_own = ((lax.broadcasted_iota(jnp.int32, (half, 1), 0) + c * half).astype(F32)) < e3

    x_in = tokens[0].astype(F32)
    scale1 = norm_scale(x_in)
    unit1 = x_in * scale1
    u = act_gather((unit1 * gain1).astype(BF), 2)
    u_all = u.reshape(4 * length, width)
    u_own = lax.dynamic_index_in_dim(u, q, 0, False).reshape(length, width)
    pre = jnp.concatenate(
        [
            mm(u_all, recq[:, : 2 * blk]).reshape(4, length, 2 * blk),
            mm(u_own, rec4[:, : 2 * blk]).reshape(1, length, 2 * blk),
        ],
        axis=0,
    )
    mixed, conv, rate, gate, state = rec_forward(taps, pre, gates, vec, ends)
    mixed_a, mixed_b = mixed[:4].reshape(4 * length, blk), mixed[4]

    def with_own(a, b):
        a = a.reshape(4, length, -1)
        own = lax.dynamic_index_in_dim(a, q, 0, False) + b
        return lax.dynamic_update_index_in_dim(a, own, q, 0)

    def by_half(a):
        return a.astype(BF).reshape(4, 2, half, width)

    rec_part = with_own(mm_t(mixed_a, recq[:, 2 * blk :]), mm_t(mixed_b, rec4[:, 2 * blk :]))
    resid = x_in + act_reduce(by_half(rec_part), 3)
    scale2 = norm_scale(resid)
    unit2 = resid * scale2
    normed = act_gather((unit2 * gain2).astype(BF), 4).reshape(4 * length, width)
    w_g, w_u, w_d = mlp[:, :ff], mlp[:, ff : 2 * ff], mlp[:, 2 * ff :]
    gate_pre = mm(normed, w_g)
    up_pre = mm(normed, w_u)
    gate_act, gate_back = jax.vjp(gelu_tanh, gate_pre)
    hidden = (gate_act * up_pre).astype(BF)
    mlp_out = act_reduce(by_half(mm_t(hidden, w_d)), 5)
    result = jnp.where(valid_own, resid + mlp_out, 0.0).astype(BF)
    out_grad = jnp.where(valid_own, cotangent[0], 0.0)
    mlp_grad = act_gather(out_grad.astype(BF), 6).reshape(4 * length, width)
    hidden_grad = mm(mlp_grad, w_d)
    gate_grad = gate_back(hidden_grad * up_pre)[0].astype(BF)
    up_grad = (hidden_grad * gate_act).astype(BF)
    normed_grad = act_reduce(by_half(mm_t(gate_grad, w_g) + mm_t(up_grad, w_u)), 7)
    grad_mlp = jnp.concatenate(
        [t_mm(normed, gate_grad).astype(BF), t_mm(normed, up_grad).astype(BF), t_mm(mlp_grad, hidden).astype(BF)],
        axis=1,
    )
    gain2_part = jnp.sum(normed_grad * unit2, axis=0)
    resid_grad = out_grad + norm_back(normed_grad * gain2, unit2, scale2)
    rg = act_gather(resid_grad.astype(BF), 8)
    rec_grad = rg.reshape(4 * length, width)
    rec_grad_own = lax.dynamic_index_in_dim(rg, q, 0, False).reshape(length, width)
    mixed_grad = jnp.concatenate(
        [
            mm(rec_grad, recq[:, 2 * blk :]).reshape(4, length, blk),
            mm(rec_grad_own, rec4[:, 2 * blk :]).reshape(1, length, blk),
        ],
        axis=0,
    )
    low, gate_w_grad, vec_grad = rec_backward(taps, pre, gates, vec, ends, conv, rate, gate, state, mixed_grad)
    low_a, low_b = low[:4].reshape(4 * length, 2 * blk), low[4]
    u_part = with_own(mm_t(low_a, recq[:, : 2 * blk]), mm_t(low_b, rec4[:, : 2 * blk]))
    u_grad = act_reduce(by_half(u_part), 9)
    grad_q = jnp.concatenate([t_mm(u_all, low_a).astype(BF), t_mm(rec_grad, mixed_a).astype(BF)], axis=1)
    grad_4 = jnp.concatenate([t_mm(u_own, low_b).astype(BF), t_mm(rec_grad_own, mixed_b).astype(BF)], axis=1)
    gain1_part = jnp.sum(u_grad * unit1, axis=0)
    token_grad = resid_grad + norm_back(u_grad * gain1, unit1, scale1)
    gains = lax.psum(jnp.stack([gain1_part, gain2_part]), "tensor")

    nvg = vec_grad.shape[1]
    depth = -(-(rb + nvg + 2) // 8) * 8

    def small_grads(h, extra):
        v = vec_grad[h].reshape(nvg, n, rb).transpose(1, 0, 2)
        v = jnp.pad(v, ((0, 0), (0, 0), (0, 2 * blk - rb)))
        g = extra.reshape(2, n, rows).transpose(1, 0, 2)
        g = jnp.pad(g, ((0, 0), (0, 0), (0, 2 * blk - rows)))
        s = jnp.concatenate([gate_w_grad[h].reshape(n, rb, 2 * blk), v, g], axis=1)
        return jnp.pad(s, ((0, 0), (0, depth - s.shape[1]), (0, 0)))

    sq = small_grads(0, jnp.zeros_like(gains))
    s4 = small_grads(1, gains)

    def slots(a):
        return a.reshape(n, rows, a.shape[1])

    o_mlp, o_q, o_4, o_sq, o_s4 = grad_reduce(
        (slots(grad_mlp), slots(grad_q), slots(grad_4), sq, s4), (True, True, False, True, False), n, 10
    )
    rec_out = jnp.concatenate([o_q, o_4[None]], axis=0)
    so = jnp.concatenate([o_sq, o_s4[None]], axis=0)

    def heads_cols(a):
        return a.transpose(1, 0, 2).reshape(rows, heads * blk)

    def quarter_cols(a):
        return a.transpose(1, 0, 2).reshape(rows, 4 * ff)

    def vec_out(i):
        return so[:, rb + i, :rb]

    return (
        result[None],
        token_grad[None],
        o_s4[rb + nvg, :rows],
        heads_cols(rec_out[:, :, :blk]),
        heads_cols(rec_out[:, :, blk : 2 * blk]),
        so[:, :rb, :blk],
        so[:, :rb, blk:],
        vec_out(0),
        vec_out(1),
        vec_out(2),
        jnp.stack([vec_out(4 + k) for k in range(taps)]),
        vec_out(3),
        rec_out[:, :, 2 * blk :].transpose(0, 2, 1).reshape(heads * blk, rows),
        o_s4[rb + nvg + 1, :rows],
        quarter_cols(o_mlp[:, :, :ff]),
        quarter_cols(o_mlp[:, :, ff : 2 * ff]),
        o_mlp[:, :, 2 * ff :].transpose(0, 2, 1).reshape(4 * ff, rows),
    )


def solution(mesh):
    return jax.shard_map(
        local,
        mesh=mesh,
        in_specs=(
            P("dp", "tensor", None),
            P("dp", None),
            P("dp"),
            P("dp", "tensor"),
            P("dp", "tensor"),
            P("tensor", "dp", None),
            P("tensor", "dp", None),
            P("tensor", "dp"),
            P("tensor", "dp"),
            P("tensor", "dp"),
            P(None, "tensor", "dp"),
            P("tensor", "dp"),
            P("tensor", "dp"),
            P("dp"),
            P("dp", "tensor"),
            P("dp", "tensor"),
            P("tensor", "dp"),
            P("dp", "tensor", None),
        ),
        out_specs=(
            P("dp", "tensor", None),
            P("dp", "tensor", None),
            P("dp"),
            P("dp", "tensor"),
            P("dp", "tensor"),
            P("tensor", "dp", None),
            P("tensor", "dp", None),
            P("tensor", "dp"),
            P("tensor", "dp"),
            P("tensor", "dp"),
            P(None, "tensor", "dp"),
            P("tensor", "dp"),
            P("tensor", "dp"),
            P("dp"),
            P("dp", "tensor"),
            P("dp", "tensor"),
            P("tensor", "dp"),
        ),
        check_vma=False,
    )
```

```python
import functools

import jax
import jax.numpy as jnp
from jax import lax
from jax.experimental import pallas as pl
from jax.experimental.pallas import tpu as pltpu
from jax.sharding import PartitionSpec as P

MESH = pl.DeviceIdType.MESH
BF = jnp.bfloat16
F32 = jnp.float32
EPS = 1e-06
DECAY = 8.0
GC = 0.7978845608028654
GK = 0.044715
VMEM_LIMIT = 60 * 1024 * 1024


def dp_at(zh, zl, y, x):
    return ((zh * 2 + zl) * 2 + y) * 2 + x


def place():
    dp = lax.axis_index("dp")
    return dp // 8, (dp // 4) % 2, (dp // 2) % 2, dp % 2, lax.axis_index("tensor")


def dev(dp, core):
    return {"dp": dp, "tensor": core}


def greet(devices):
    sem = pltpu.get_barrier_semaphore()
    for d in devices:
        pl.semaphore_signal(sem, inc=1, device_id=d, device_id_type=MESH)
    pl.semaphore_wait(sem, len(devices))


def remote(src, dst, ssem, rsem, d):
    return pltpu.make_async_remote_copy(
        src_ref=src, dst_ref=dst, send_sem=ssem, recv_sem=rsem, device_id=d, device_id_type=MESH
    )


def peers_of_group(zh, zl, y, x):
    out = []
    for kl, kx in ((0, 1), (1, 0), (1, 1)):
        pz, px = (zl + kl) % 2, (x + kx) % 2
        out.append((pz * 2 + px, dp_at(zh, pz, y, px)))
    return out


def act_gather_kernel(x_ref, out_ref, send, recv, fsend, frecv, local):
    zh, zl, y, x, c = place()
    q, me = zl * 2 + x, dp_at(zh, zl, y, x)
    sib = dev(me, 1 - c)
    peers = peers_of_group(zh, zl, y, x)
    greet([sib] + [dev(d, c) for _, d in peers])
    own = pltpu.make_async_copy(x_ref, out_ref.at[q, c], local)
    own.start()
    copies = []
    for k, (pq, d) in enumerate(peers):
        cp = remote(x_ref, out_ref.at[q, c], send.at[k], recv.at[q], dev(d, c))
        cp.start()
        copies.append(cp)
    fwd = [remote(x_ref, out_ref.at[q, c], fsend.at[3], frecv.at[q], sib)]
    fwd[0].start()
    for k, (pq, d) in enumerate(peers):
        land = out_ref.at[pq, c]
        remote(land, land, send.at[k], recv.at[pq], dev(d, c)).wait_recv()
        cp = remote(land, land, fsend.at[k], frecv.at[pq], sib)
        cp.start()
        fwd.append(cp)
    for j in range(4):
        land = out_ref.at[j, 1 - c]
        remote(land, land, fsend.at[0], frecv.at[j], sib).wait_recv()
    for cp in copies + fwd:
        cp.wait_send()
    own.wait()


def act_gather(x, cid):
    half, width = x.shape
    return pl.pallas_call(
        act_gather_kernel,
        out_shape=jax.ShapeDtypeStruct((4, 2, half, width), x.dtype),
        in_specs=[pl.BlockSpec(memory_space=pl.ANY)],
        out_specs=pl.BlockSpec(memory_space=pl.ANY),
        scratch_shapes=[
            pltpu.SemaphoreType.DMA((3,)),
            pltpu.SemaphoreType.DMA((4,)),
            pltpu.SemaphoreType.DMA((4,)),
            pltpu.SemaphoreType.DMA((4,)),
            pltpu.SemaphoreType.DMA,
        ],
        compiler_params=pltpu.CompilerParams(collective_id=cid, has_side_effects=True),
        name="act_gather",
    )(x)


def act_reduce_kernel(p_ref, out_ref, sbuf, tbuf, rbuf, ssend, srecv, send, recv):
    zh, zl, y, x, c = place()
    q, me = zl * 2 + x, dp_at(zh, zl, y, x)
    sib = dev(me, 1 - c)
    peers = peers_of_group(zh, zl, y, x)
    greet([sib] + [dev(d, c) for _, d in peers])
    order = [peers[2], peers[1], peers[0], (q, me)]
    half = []
    for k, (pq, d) in enumerate(order):
        cp = remote(p_ref.at[pq, 1 - c], sbuf.at[pq], ssend.at[k], srecv.at[pq], sib)
        cp.start()
        half.append(cp)
    out = []
    for k, (pq, d) in enumerate(order):
        remote(sbuf.at[pq], sbuf.at[pq], ssend.at[k], srecv.at[pq], sib).wait_recv()
        total = p_ref[pq, c].astype(F32) + sbuf[pq].astype(F32)
        if k < 3:
            tbuf[k] = total.astype(BF)
            cp = remote(tbuf.at[k], rbuf.at[q], send.at[k], recv.at[q], dev(d, c))
            cp.start()
            out.append(cp)
        else:
            out_ref[...] = total
    for pq, d in peers:
        remote(rbuf.at[pq], rbuf.at[pq], send.at[0], recv.at[pq], dev(d, c)).wait_recv()
        out_ref[...] += rbuf[pq].astype(F32)
    for cp in half + out:
        cp.wait_send()


def act_reduce(parts, cid):
    _, _, half, width = parts.shape
    vm = pl.BlockSpec(memory_space=pltpu.VMEM)
    return pl.pallas_call(
        act_reduce_kernel,
        out_shape=jax.ShapeDtypeStruct((half, width), F32),
        in_specs=[vm],
        out_specs=vm,
        scratch_shapes=[
            pltpu.VMEM((4, half, width), BF),
            pltpu.VMEM((3, half, width), BF),
            pltpu.VMEM((4, half, width), BF),
            pltpu.SemaphoreType.DMA((4,)),
            pltpu.SemaphoreType.DMA((4,)),
            pltpu.SemaphoreType.DMA((3,)),
            pltpu.SemaphoreType.DMA((4,)),
        ],
        compiler_params=pltpu.CompilerParams(
            collective_id=cid, has_side_effects=True, vmem_limit_bytes=VMEM_LIMIT
        ),
        name="act_reduce",
    )(parts)


def plane(zh, zl, y, x, high):
    out = []
    for kh in range(high):
        for kl in range(2):
            for kx in range(2):
                ph, pz, px = (zh + kh) % high, (zl + kl) % 2, (x + kx) % 2
                out.append((ph, pz, px))
    return out


def weight_gather_kernel(high, narr, picked, *refs):
    src, dst = refs[:narr], refs[narr : 2 * narr]
    send, recv, fsend, local = refs[2 * narr :]
    zh, zl, y, x, c = place()
    me = dp_at(zh, zl, y, x)
    there = plane(zh, zl, y, x, high)
    other = dev(dp_at(zh, zl, 1 - y, x), c)
    greet([dev(dp_at(h, z, y, w), c) for h, z, w in there[1:]] + [other])
    pend = []
    for a in range(narr):
        for k, (h, z, w) in enumerate(there):
            piece = src[a].at[z * 2 + w] if picked[a] else src[a]
            if k == 0:
                cp = pltpu.make_async_copy(piece, dst[a].at[me], local.at[a])
            else:
                cp = remote(piece, dst[a].at[me], send.at[a, k], recv.at[a, me], dev(dp_at(h, z, y, w), c))
            cp.start()
            pend.append((k, cp))
    for a in range(narr):
        for k, (h, z, w) in enumerate(there):
            s = dp_at(h, z, y, w)
            land = dst[a].at[s]
            if k == 0:
                pend[a * len(there)][1].wait()
            else:
                remote(land, land, send.at[a, k], recv.at[a, s], other).wait_recv()
            cp = remote(land, land, fsend.at[a, k], recv.at[a, s], other)
            cp.start()
            pend.append((1, cp))
    for a in range(narr):
        for k, (h, z, w) in enumerate(there):
            s = dp_at(h, z, 1 - y, w)
            land = dst[a].at[s]
            remote(land, land, fsend.at[a, k], recv.at[a, s], other).wait_recv()
    for k, cp in pend:
        if k:
            cp.wait_send()


def weight_gather(arrays, picked, n, cid):
    high = n // 8
    narr = len(arrays)
    shapes = tuple(
        jax.ShapeDtypeStruct((n,) + (a.shape[1:] if p else a.shape), a.dtype) for a, p in zip(arrays, picked)
    )
    anyspec = pl.BlockSpec(memory_space=pl.ANY)
    return pl.pallas_call(
        functools.partial(weight_gather_kernel, high, narr, picked),
        out_shape=shapes,
        in_specs=[anyspec] * narr,
        out_specs=[anyspec] * narr,
        scratch_shapes=[
            pltpu.SemaphoreType.DMA((narr, high * 4)),
            pltpu.SemaphoreType.DMA((narr, n)),
            pltpu.SemaphoreType.DMA((narr, high * 4)),
            pltpu.SemaphoreType.DMA((narr,)),
        ],
        compiler_params=pltpu.CompilerParams(collective_id=cid, has_side_effects=True),
        name="weight_gather",
    )(*arrays)


def grad_reduce_kernel(high, narr, picked, *refs):
    src, dst = refs[:narr], refs[narr : 2 * narr]
    ybuf, tbuf, rbuf = (refs[(2 + i) * narr : (3 + i) * narr] for i in range(3))
    ysend, yrecv, send, recv = refs[5 * narr :]
    zh, zl, y, x, c = place()
    q = zl * 2 + x
    there = plane(zh, zl, y, x, high)
    other = dev(dp_at(zh, zl, 1 - y, x), c)
    greet([dev(dp_at(h, z, y, w), c) for h, z, w in there[1:]] + [other])
    mine = zh * 4 + q
    order = there[1:] + there[:1]
    pend = []
    for a in range(narr):
        for h, z, w in order:
            j = h * 4 + z * 2 + w
            cp = remote(src[a].at[dp_at(h, z, 1 - y, w)], ybuf[a].at[j], ysend.at[a, j], yrecv.at[a, j], other)
            cp.start()
            pend.append(cp)
    for a in range(narr):
        for k, (h, z, w) in enumerate(order):
            j = h * 4 + z * 2 + w
            remote(ybuf[a].at[j], ybuf[a].at[j], ysend.at[a, j], yrecv.at[a, j], other).wait_recv()
            total = src[a][dp_at(h, z, y, w)].astype(F32) + ybuf[a][j].astype(F32)
            if k < len(order) - 1:
                tbuf[a][j] = total.astype(tbuf[a].dtype)
                cp = remote(
                    tbuf[a].at[j], rbuf[a].at[mine], send.at[a, j], recv.at[a, mine], dev(dp_at(h, z, y, w), c)
                )
                cp.start()
                pend.append(cp)
            elif picked[a]:
                dst[a][...] = jnp.zeros(dst[a].shape, F32)
                dst[a][q] = total
            else:
                dst[a][...] = total
    for a in range(narr):
        for h, z, w in there[1:]:
            j = h * 4 + z * 2 + w
            remote(rbuf[a].at[j], rbuf[a].at[j], send.at[a, j], recv.at[a, j], other).wait_recv()
            if picked[a]:
                dst[a][z * 2 + w] += rbuf[a][j].astype(F32)
            else:
                dst[a][...] += rbuf[a][j].astype(F32)
    for cp in pend:
        cp.wait_send()


def grad_reduce(arrays, picked, n, cid):
    high = n // 8
    narr = len(arrays)
    vm = pl.BlockSpec(memory_space=pltpu.VMEM)
    shapes = tuple(
        jax.ShapeDtypeStruct(((4,) if p else ()) + a.shape[1:], F32) for a, p in zip(arrays, picked)
    )
    bufs = [pltpu.VMEM((high * 4,) + a.shape[1:], a.dtype) for a in arrays]
    return pl.pallas_call(
        functools.partial(grad_reduce_kernel, high, narr, picked),
        out_shape=shapes,
        in_specs=[vm] * narr,
        out_specs=[vm] * narr,
        scratch_shapes=bufs * 3 + [pltpu.SemaphoreType.DMA((narr, high * 4))] * 4,
        compiler_params=pltpu.CompilerParams(
            collective_id=cid, has_side_effects=True, vmem_limit_bytes=VMEM_LIMIT
        ),
        name="grad_reduce",
    )(*arrays)


def gelu_parts(v):
    t = jnp.tanh(GC * (v + GK * v * v * v))
    act = 0.5 * v * (1.0 + t)
    der = 0.5 * (1.0 + t) + 0.5 * v * (1.0 - t * t) * GC * (1.0 + 3.0 * GK * v * v)
    return act, der


def segments(ends, length, width, taps):
    t = lax.broadcasted_iota(jnp.int32, (length, width), 0).astype(F32)

    def seg(at):
        total = jnp.zeros((length, width), F32)
        for j in range(4):
            total = total + jnp.where(at >= ends[:, j : j + 1], 1.0, 0.0)
        return total

    here = seg(t)
    same = []
    for k in range(1, taps):
        same.append(jnp.where((t >= float(k)) & (seg(t - float(k)) == here), 1.0, 0.0))
    return same


def scan8(a, b, reverse):
    length, width = a.shape
    row = lax.broadcasted_iota(jnp.int32, (length, width), 0) % 8
    for d in (1, 2, 4):
        if reverse:
            ash, bsh = pltpu.roll(a, length - d, 0), pltpu.roll(b, length - d, 0)
            ok = row < 8 - d
        else:
            ash, bsh = pltpu.roll(a, d, 0), pltpu.roll(b, d, 0)
            ok = row >= d
        b = b + a * jnp.where(ok, bsh, 0.0)
        a = a * jnp.where(ok, ash, 1.0)
    return a, b


def full_scan(a, b, out_ref, a_ref, reverse):
    length, width = a.shape
    a8, b8 = scan8(a, b, reverse)
    a_ref[...] = a8
    out_ref[...] = b8
    blocks = length // 8

    def step(i, carry):
        at = (blocks - 1 - i if reverse else i) * 8
        at = pl.multiple_of(at, 8)
        now = out_ref[pl.ds(at, 8), :] + a_ref[pl.ds(at, 8), :] * carry
        out_ref[pl.ds(at, 8), :] = now
        return now[0:1, :] if reverse else now[7:8, :]

    lax.fori_loop(0, blocks, step, jnp.zeros((1, width), F32))


def rec_forward_kernel(taps, p_ref, g_ref, v_ref, e_ref, mixed_ref, conv_ref, r_ref, i_ref, state_ref, a_ref):
    length, two = p_ref.shape[1:]
    blk = two // 2
    branch, conv_in = p_ref[0, :, :blk], p_ref[0, :, blk:]
    vec = v_ref[0]
    same = segments(e_ref[0, 0:1, :], length, blk, taps)
    conv = conv_in * vec[4:5] + vec[4 + taps : 5 + taps]
    for k in range(1, taps):
        conv = conv + pltpu.roll(conv_in, k, 0) * same[k - 1] * vec[4 + k : 5 + k]
    pre = jnp.dot(conv.astype(BF), g_ref[0], preferred_element_type=F32)
    r = jax.nn.sigmoid(pre[:, :blk] + vec[0:1])
    gate = jax.nn.sigmoid(pre[:, blk:] + vec[1:2])
    log_a = (-DECAY * r) * vec[2:3]
    a = jnp.exp(log_a)
    start = same[0] == 0.0
    a_eff = jnp.where(start, 0.0, a)
    mult = jnp.where(start, 1.0, jnp.sqrt(-jnp.tanh(log_a) * (1.0 + a * a)))
    full_scan(a_eff, mult * gate * conv, state_ref.at[0], a_ref, False)
    act, _ = gelu_parts(branch)
    mixed_ref[0] = (state_ref[0] * act).astype(BF)
    conv_ref[0] = conv
    r_ref[0] = r
    i_ref[0] = gate


def rec_backward_kernel(
    taps, p_ref, g_ref, v_ref, e_ref, conv_ref, r_ref, i_ref, state_ref, m_ref,
    low_ref, gg_ref, vg_ref, carry_ref, a_ref,
):
    unit = pl.program_id(0)
    length, two = p_ref.shape[1:]
    blk = two // 2
    branch, conv_in = p_ref[0, :, :blk], p_ref[0, :, blk:]
    vec = v_ref[0]
    same = segments(e_ref[0, 0:1, :], length, blk, taps)
    start = same[0] == 0.0
    r, gate, conv, state, mg = r_ref[0], i_ref[0], conv_ref[0], state_ref[0], m_ref[0]
    act, der = gelu_parts(branch)
    low_ref[0, :, :blk] = (mg * state * der).astype(BF)
    log_a = (-DECAY * r) * vec[2:3]
    a = jnp.exp(log_a)
    a_eff = jnp.where(start, 0.0, a)
    row = lax.broadcasted_iota(jnp.int32, (length, blk), 0)
    a_next = jnp.where(row < length - 1, pltpu.roll(a_eff, length - 1, 0), 0.0)
    full_scan(a_next, mg * act, carry_ref, a_ref, True)
    carry = carry_ref[...]
    prev = jnp.where(row > 0, pltpu.roll(state, 1, 0), 0.0)
    raw = jnp.sqrt(-jnp.tanh(log_a) * (1.0 + a * a))
    mult = jnp.where(start, 1.0, raw)
    log_grad = jnp.where(start, 0.0, carry * prev * a - carry * gate * conv * (a * a) / raw)
    r_grad = log_grad * (-DECAY * vec[2:3]) * (r * (1.0 - r))
    i_grad = carry * mult * conv * (gate * (1.0 - gate))
    pre_low = jnp.concatenate([r_grad.astype(BF), i_grad.astype(BF)], axis=1)
    conv_grad = carry * mult * gate + lax.dot_general(
        pre_low, g_ref[0], (((1,), (1,)), ((), ())), preferred_element_type=F32
    )
    gg = lax.dot_general(conv.astype(BF), pre_low, (((0,), (0,)), ((), ())), preferred_element_type=F32)

    def total(v):
        return jnp.sum(v, axis=0, keepdims=True)

    rows = [total(r_grad), total(i_grad), total(log_grad * (DECAY * r) * vec[3:4]), total(conv_grad)]
    inp = conv_grad * vec[4:5]
    rows.append(total(conv_grad * conv_in))
    for k in range(1, taps):
        masked = conv_grad * same[k - 1]
        rows.append(total(masked * pltpu.roll(conv_in, k, 0)))
        inp = inp + pltpu.roll(masked, length - k, 0) * vec[4 + k : 5 + k]
    low_ref[0, :, blk:] = inp.astype(BF)
    vg = jnp.concatenate(rows, axis=0)

    @pl.when((unit == 0) | (unit == 4))
    def _():
        gg_ref[0] = gg
        vg_ref[0] = vg

    @pl.when((unit != 0) & (unit != 4))
    def _():
        gg_ref[0] += gg
        vg_ref[0] += vg


def unit_spec(a):
    return pl.BlockSpec((1,) + a.shape[1:], lambda u: (u, 0, 0))


def head_spec(a):
    return pl.BlockSpec((1,) + a.shape[1:], lambda u: (u // 4, 0, 0))


def rec_forward(taps, pre, gates, vec, ends):
    units, length, two = pre.shape
    blk = two // 2
    block = pl.BlockSpec((1, length, blk), lambda u: (u, 0, 0))
    f32 = jax.ShapeDtypeStruct((units, length, blk), F32)
    return pl.pallas_call(
        functools.partial(rec_forward_kernel, taps),
        grid=(units,),
        out_shape=(jax.ShapeDtypeStruct((units, length, blk), BF), f32, f32, f32, f32),
        in_specs=[unit_spec(pre), head_spec(gates), head_spec(vec), unit_spec(ends)],
        out_specs=[block] * 5,
        scratch_shapes=[pltpu.VMEM((length, blk), F32)],
        compiler_params=pltpu.CompilerParams(vmem_limit_bytes=VMEM_LIMIT),
        name="rec_forward",
    )(pre, gates, vec, ends)


def rec_backward(taps, pre, gates, vec, ends, conv, r, gate, state, mixed_grad):
    units, length, two = pre.shape
    blk = two // 2
    vrows = 4 + taps
    return pl.pallas_call(
        functools.partial(rec_backward_kernel, taps),
        grid=(units,),
        out_shape=(
            jax.ShapeDtypeStruct((units, length, two), BF),
            jax.ShapeDtypeStruct((2, blk, two), F32),
            jax.ShapeDtypeStruct((2, vrows, blk), F32),
        ),
        in_specs=[unit_spec(pre), head_spec(gates), head_spec(vec), unit_spec(ends)]
        + [unit_spec(conv)] * 5,
        out_specs=[
            unit_spec(pre),
            pl.BlockSpec((1, blk, two), lambda u: (u // 4, 0, 0)),
            pl.BlockSpec((1, vrows, blk), lambda u: (u // 4, 0, 0)),
        ],
        scratch_shapes=[pltpu.VMEM((length, blk), F32)] * 2,
        compiler_params=pltpu.CompilerParams(vmem_limit_bytes=VMEM_LIMIT),
        name="rec_backward",
    )(pre, gates, vec, ends, conv, r, gate, state, mixed_grad)


class Gather:
    def __init__(self, slot, parts, sems, here, there, core):
        self.slot, self.parts, (self.send, self.recv, self.fsend) = slot, parts, sems
        zh, zl, y, x = here
        self.q = zl * 2 + x
        self.me = dp_at(zh, zl, y, x)
        self.near = [dp_at(h, z, y, w) for h, z, w in there]
        self.far = [dp_at(h, z, 1 - y, w) for h, z, w in there]
        self.pick = [z * 2 + w for _, z, w in there]
        self.core = core
        self.other = dev(dp_at(zh, zl, 1 - y, x), core)

    def ks(self, far):
        count = len(self.near)
        return range(4, count) if far else range(4)

    def start(self, far):
        for k in self.ks(far):
            for piece, part in self.parts:
                src = piece(self.pick[k])
                dst = part(self.slot(self.me, self.pick[k]))
                if k == 0:
                    pltpu.make_async_copy(src, dst, self.send.at[0]).start()
                else:
                    d = dev(self.near[k], self.core)
                    remote(src, dst, self.send.at[k], self.recv.at[self.me], d).start()

    def forward(self, k):
        land = self.slot(self.near[k], self.q)
        if k == 0:
            pltpu.make_async_copy(land, land, self.send.at[0]).wait()
        else:
            remote(land, land, self.send.at[k], self.recv.at[self.near[k]], self.other).wait_recv()
        remote(land, land, self.fsend.at[k], self.recv.at[self.near[k]], self.other).start()

    def forward_all(self, far):
        for k in self.ks(far):
            self.forward(k)

    def arrive_all(self):
        for k in range(len(self.far)):
            land = self.slot(self.far[k], self.q)
            remote(land, land, self.fsend.at[k], self.recv.at[self.far[k]], self.other).wait_recv()

    def finish(self):
        for k in range(len(self.near)):
            land = self.slot(self.near[k], self.q)
            remote(land, land, self.fsend.at[k], self.recv.at[self.near[k]], self.other).wait_send()
            if k:
                remote(land, land, self.send.at[k], self.recv.at[self.near[k]], self.other).wait_send()


class Rows:
    def __init__(self, buf, sems, here, core):
        self.buf, (self.send, self.recv, self.fsend, self.frecv) = buf, sems
        self.here, self.core = here, core
        zh, zl, y, x = here
        self.q = zl * 2 + x
        self.sib = dev(dp_at(zh, zl, y, x), 1 - core)

    def at(self, k):
        zh, zl, y, x = self.here
        pz, px = (zl + k // 2) % 2, (x + k % 2) % 2
        return pz * 2 + px, dev(dp_at(zh, pz, y, px), self.core)

    def start(self):
        own = self.buf.at[self.q, self.core]
        remote(own, own, self.fsend.at[0], self.frecv.at[self.q], self.sib).start()
        for k in (1, 2, 3):
            _, d = self.at(k)
            remote(own, own, self.send.at[k], self.recv.at[self.q], d).start()

    def forward(self, k):
        pq, d = self.at(k)
        land = self.buf.at[pq, self.core]
        remote(land, land, self.send.at[k], self.recv.at[pq], d).wait_recv()
        remote(land, land, self.fsend.at[k], self.frecv.at[pq], self.sib).start()

    def arrive(self, k):
        pq, _ = self.at(k)
        land = self.buf.at[pq, 1 - self.core]
        remote(land, land, self.fsend.at[k], self.frecv.at[pq], self.sib).wait_recv()

    def finish(self):
        own = self.buf.at[self.q, self.core]
        for k in range(4):
            remote(own, own, self.fsend.at[k], self.frecv.at[self.q], self.sib).wait_send()
            if k:
                remote(own, own, self.send.at[k], self.recv.at[self.q], self.sib).wait_send()


def row_sems():
    return [pltpu.SemaphoreType.DMA((4,))] * 4


class Sums:
    def __init__(self, part, sib, got, sems, rows):
        self.part, self.sib_buf, self.got = part, sib, got
        self.ssend, self.srecv, self.send, self.recv = sems
        self.rows = rows

    def push(self, k):
        r = self.rows
        pq, _ = r.at(k)
        remote(
            self.part.at[pq, 1 - r.core], self.sib_buf.at[pq], self.ssend.at[k], self.srecv.at[pq], r.sib
        ).start()

    def pair(self, k):
        r = self.rows
        pq, _ = r.at(k)
        land = self.sib_buf.at[pq]
        remote(land, land, self.ssend.at[k], self.srecv.at[pq], r.sib).wait_recv()
        return self.part[pq, r.core].astype(F32) + self.sib_buf[pq].astype(F32)

    def pass_on(self, k):
        r = self.rows
        pq, d = r.at(k)
        self.part[pq, r.core] = self.pair(k).astype(BF)
        remote(self.part.at[pq, r.core], self.got.at[r.q], self.send.at[k], self.recv.at[r.q], d).start()

    def take(self, k):
        r = self.rows
        pq, _ = r.at(k)
        land = self.got.at[pq]
        remote(land, land, self.send.at[k], self.recv.at[pq], r.sib).wait_recv()
        return self.got[pq].astype(F32)

    def finish(self):
        r = self.rows
        land = self.got.at[r.q]
        for k in range(4):
            remote(land, land, self.ssend.at[k], self.srecv.at[r.q], r.sib).wait_send()
            if k:
                remote(land, land, self.send.at[k], self.recv.at[r.q], r.sib).wait_send()


def rec_unit(taps, branch, conv_in, vec, gates, ends, state_ref, a_ref):
    length, blk = branch.shape
    same = segments(ends, length, blk, taps)
    conv = conv_in * vec[4:5] + vec[4 + taps : 5 + taps]
    for k in range(1, taps):
        conv = conv + pltpu.roll(conv_in, k, 0) * same[k - 1] * vec[4 + k : 5 + k]
    pre = jnp.dot(conv.astype(BF), gates, preferred_element_type=F32)
    r = jax.nn.sigmoid(pre[:, :blk] + vec[0:1])
    gate = jax.nn.sigmoid(pre[:, blk:] + vec[1:2])
    log_a = (-DECAY * r) * vec[2:3]
    a = jnp.exp(log_a)
    start = same[0] == 0.0
    a_eff = jnp.where(start, 0.0, a)
    mult = jnp.where(start, 1.0, jnp.sqrt(-jnp.tanh(log_a) * (1.0 + a * a)))
    full_scan(a_eff, mult * gate * conv, state_ref, a_ref, False)
    act, _ = gelu_parts(branch)
    return conv, r, gate, (state_ref[...] * act).astype(BF)


SMALL_ROWS = 96


def forward_kernel(n, taps, heads, *refs):
    (tok, cot, wb, wi, wo, wg, wu, wd, wr, wig, small) = refs[:11]
    (o_rec, o_mlp, o_gate, o_vec, o_gain, o_ends, o_u, o_grad, pre, conv, rate, gate, state, mixed, resid, o_norm) = refs[11:27]
    (rec, gat, sml, u_buf, og, part, sibb, got, extra, a_scr, gfull) = refs[27:38]
    sems = refs[38:]
    g_sems, r1, r2, s1, (fin, h_send, h_recv) = sems[:48], sems[48:52], sems[52:56], sems[56:60], sems[60:]
    zh, zl, y, x, c = place()
    here = (zh, zl, y, x)
    q, me = zl * 2 + x, dp_at(zh, zl, y, x)
    high = n // 8
    there = plane(zh, zl, y, x, high)
    half, width = tok.shape
    length, blk = pre.shape[1], pre.shape[2] // 2
    ff = wg.shape[1] // 4
    rb, rr = wr.shape[1], wb.shape[0]
    greet(
        [dev(dp_at(h, z, y, w), c) for h, z, w in there[1:]]
        + [dev(dp_at(zh, zl, 1 - y, x), c), dev(me, 1 - c)]
    )

    def whole(ref):
        return ref

    def head_cols(ref):
        return lambda p: ref.at[:, pl.ds(pl.multiple_of(p * blk, 128), blk)]

    def make(i, slot, parts):
        return Gather(slot, parts, g_sems[3 * i : 3 * i + 3], here, there, c)

    smalls = make(0, lambda s, g: sml.at[s], [(lambda p: small, whole)])
    gats, recs, mlps = [], [], []
    for h in range(2):
        pick = (lambda ref: lambda p: ref.at[p]) if h == 0 else (lambda ref: lambda p: ref.at[heads - 1])
        gats.append(
            make(
                1 + h,
                lambda s, g, h=h: gat.at[h, s],
                [
                    (pick(w), lambda r, i=i: r.at[:, pl.ds(i * blk, blk)])
                    for i, w in enumerate((wr, wig))
                ],
            )
        )
    for i, w in enumerate((wb, wi, wo)):
        recs.append(make(3 + i, lambda s, g, i=i: rec.at[0, i, s], [(head_cols(w), whole)]))
    quarter = rr // 4

    def shared_piece(ref):
        return lambda p: ref.at[pl.ds(pl.multiple_of(p * quarter, 8), quarter), pl.ds((heads - 1) * blk, blk)]

    def shared_rows(s, g):
        return rec.at[1, :, s, pl.ds(pl.multiple_of(g * quarter, 8), quarter), :]

    shared = make(
        6, shared_rows, [(shared_piece(w), lambda r, i=i: r.at[i]) for i, w in enumerate((wb, wi, wo))]
    )
    for i, w in enumerate((wg, wu, wd)):
        for t in range(ff // blk):
            piece = lambda p, w=w, t=t: w.at[:, pl.ds(pl.multiple_of(p * ff + t * blk, 128), blk)]
            j = i * (ff // blk) + t
            mlps.append(make(7 + j, lambda s, g, j=j: o_mlp.at[j, s], [(piece, whole)]))
    count = len(there)
    order = [recs[0], gats[0], recs[1], gats[1], shared, recs[2]] + mlps
    ahead = 2

    def pump(j):
        if j + ahead < len(order):
            order[j + ahead].forward_all(False)
        order[j].forward_all(True)
        if j + ahead < len(order):
            order[j + ahead].start(True)
        if j + 2 * ahead < len(order):
            order[j + 2 * ahead].start(False)

    smalls.start(True)
    smalls.start(False)
    for j in range(2 * ahead):
        if j < ahead:
            order[j].start(True)
        order[j].start(False)

    xin = tok[...].astype(F32)
    unit = xin * lax.rsqrt(jnp.mean(xin * xin, axis=-1, keepdims=True) + EPS)
    resid[...] = unit
    smalls.forward_all(False)
    smalls.forward_all(True)
    for j in range(ahead):
        order[j].forward_all(False)
    smalls.arrive_all()
    per_vec, per_gain = blk // 128, width // 128
    base = (heads - 1) * 16
    for h in range(2):
        at = pl.multiple_of(q * 16, 16) if h == 0 else base
        groups = [jnp.zeros((16, 128), F32)] * per_vec
        for s in range(n):
            g = s * rb // 128
            groups[g] = groups[g] + sml[s, pl.ds(at, 16), :].astype(F32)
        raw = jnp.concatenate(groups, axis=1)
        decay = raw[2:3]
        o_vec[h, 0:2, :] = raw[0:2]
        o_vec[h, 2:3, :] = jnp.log1p(jnp.exp(-decay))
        o_vec[h, 3:4, :] = jax.nn.sigmoid(-decay)
        o_vec[h, 4 : 5 + taps, :] = raw[3 : 4 + taps]
    groups = [None] * per_gain
    for s in range(n):
        g = s * rr // 128
        v = sml[s, SMALL_ROWS - 16 : SMALL_ROWS, :].astype(F32)
        groups[g] = v if groups[g] is None else groups[g] + v
    for g in range(per_gain):
        o_gain[:, g * 128 : (g + 1) * 128] = groups[g][0:8]
    for j in range(4):
        v = sml[dp_at(zh, j // 2, y, j % 2), SMALL_ROWS - 16 : SMALL_ROWS, :].astype(F32)
        o_ends[j] = jnp.broadcast_to(v[2:3], (8, 128))
    u_rows = Rows(u_buf, r1, here, c)
    g_rows = Rows(o_grad, r2, here, c)
    u_buf[q, c] = (resid[...] * o_gain[0:1, :]).astype(BF)
    u_rows.start()
    e3 = o_ends[q][0:1, 3:4]
    spot = lax.broadcasted_iota(jnp.int32, (half, 1), 0).astype(F32) + (c * half).astype(F32)
    og[...] = jnp.where(spot < e3, cot[...], 0.0).astype(BF)
    own_grad = o_grad.at[q, c]
    place_grad = pltpu.make_async_copy(og, own_grad, fin.at[0])
    place_grad.start()
    place_grad.wait()
    g_rows.start()
    for j in range(3):
        pump(j)
    for k in (1, 2, 3):
        u_rows.forward(k)
    for j in range(3, 6):
        pump(j)
    for a in gats + recs[:2] + [shared]:
        a.arrive_all()

    def group_region(g):
        return rec.at[1, :, :, pl.ds(pl.multiple_of(g * quarter, 8), quarter), :]

    for k in (1, 2, 3):
        _, d = u_rows.at(k)
        remote(group_region(q), group_region(q), h_send.at[k], h_recv.at[q], d).start()
    for h in range(2):
        if rb % 16 == 0:
            o_gate[h] = gat[h].reshape(blk, 2 * blk)
        else:
            for s in range(n):
                gfull[s * rb : (s + 1) * rb, :] = gat[h, s].astype(F32)
            o_gate[h] = gfull[...].astype(BF)
    for k in range(4):
        u_rows.arrive(k)
    recs[2].arrive_all()
    for k in (1, 2, 3):
        pq, d = u_rows.at(k)
        remote(group_region(pq), group_region(pq), h_send.at[k], h_recv.at[pq], d).wait_recv()
    keep = [pltpu.make_async_copy(rec, o_rec, fin.at[1]), pltpu.make_async_copy(u_buf, o_u, fin.at[2])]
    for cp in keep:
        cp.start()

    sums = Sums(part, sibb, got, s1, u_rows)

    def step(i, carry):
        h = jnp.where(i == 0, 1, 0)
        k = jnp.maximum(i - 1, 0)
        pq, _ = u_rows.at(k)
        at = jnp.where(i == 0, 4, pq)
        rows = u_buf[pq].reshape(2 * half, width)
        for j in range(2):
            w = rec[h, j].reshape(width, blk)
            pre[at, :, j * blk : (j + 1) * blk] = mm(rows, w)
        cv, rt, gt, mx = rec_unit(
            taps, pre[at, :, :blk], pre[at, :, blk:], o_vec[h], o_gate[h], o_ends[pq][0:1, :], state.at[at], a_scr
        )
        conv[at], rate[at], gate[at], mixed[at] = cv, rt, gt, mx
        per = 512 // rr if rr <= 512 else 1

        def cols_out(t, carry):
            w = rec[h, 2, pl.ds(t * per, per)].reshape(per * rr, blk)
            tile = mm_t(mx, w)
            lanes = pl.ds(pl.multiple_of(t * (per * rr), 128), per * rr)
            tile = tile + jnp.where(i == 1, extra[:, lanes], 0.0)

            @pl.when(i == 0)
            def _():
                extra[:, lanes] = tile

            @pl.when(i > 0)
            def _():
                part[pq, 0, :, lanes] = tile[:half].astype(BF)
                part[pq, 1, :, lanes] = tile[half:].astype(BF)

            return carry

        lax.fori_loop(0, width // (per * rr), cols_out, 0)

        @pl.when(i > 0)
        def _():
            sums.push(k)

        @pl.when(i == 2)
        def _():
            resid[...] = tok[...].astype(F32) + sums.pair(0)

        @pl.when(i > 2)
        def _():
            sums.pass_on(k - 1)

        for j, m in ((1, 6), (3, 7)):

            @pl.when(i == j)
            def _():
                pump(m)

        return carry

    extra[...] = jnp.zeros_like(extra)
    lax.fori_loop(0, 5, step, 0)
    sums.pass_on(3)
    pump(8)
    for k in (1, 2, 3):
        g_rows.forward(k)
    for k in (1, 2, 3):
        resid[...] += sums.take(k)
    total = resid[...]
    unit = total * lax.rsqrt(jnp.mean(total * total, axis=-1, keepdims=True) + EPS)
    o_norm[...] = (unit * o_gain[1:2, :]).astype(BF)
    for j in range(9, len(order)):
        pump(j)
    for a in mlps:
        a.arrive_all()
    for k in range(4):
        g_rows.arrive(k)
    for k in (1, 2, 3):
        _, d = u_rows.at(k)
        remote(group_region(q), group_region(q), h_send.at[k], h_recv.at[q], d).wait_send()
    for a in [smalls, shared] + mlps + gats + recs + [u_rows, g_rows, sums]:
        a.finish()
    for cp in keep:
        cp.wait()


def forward(tok, cot, wb, wi, wo, wg, wu, wd, wr, wig, small, n, taps, cid):
    half, width = tok.shape
    heads, rb, blk = wr.shape
    rr = wb.shape[0]
    length = 2 * half
    ff = wg.shape[1] // 4
    vm = pl.BlockSpec(memory_space=pltpu.VMEM)
    hb = pl.BlockSpec(memory_space=pl.ANY)

    def sds(*shape, t=F32):
        return jax.ShapeDtypeStruct(shape, t)

    unit = sds(5, length, blk)
    outs = (
        (sds(2, 3, n, rr, blk, t=BF), hb),
        (sds(3 * ff // blk, n, rr, blk, t=BF), hb),
        (sds(2, blk, 2 * blk, t=BF), vm),
        (sds(2, 16, blk), vm),
        (sds(8, width), vm),
        (sds(4, 8, 128), vm),
        (sds(4, 2, half, width, t=BF), hb),
        (sds(4, 2, half, width, t=BF), hb),
        (sds(5, length, 2 * blk), vm),
        (unit, vm),
        (unit, vm),
        (unit, vm),
        (unit, vm),
        (sds(5, length, blk, t=BF), vm),
        (sds(half, width), vm),
        (sds(half, width, t=BF), vm),
    )
    count = n // 2
    return pl.pallas_call(
        functools.partial(forward_kernel, n, taps, heads),
        out_shape=tuple(o for o, _ in outs),
        in_specs=[vm, vm] + [hb] * 9,
        out_specs=[s for _, s in outs],
        scratch_shapes=[
            pltpu.VMEM((2, 3, n, rr, blk), BF),
            pltpu.VMEM((2, n, rb, 2 * blk), BF),
            pltpu.VMEM((n, SMALL_ROWS, 128), BF),
            pltpu.VMEM((4, 2, half, width), BF),
            pltpu.VMEM((half, width), BF),
            pltpu.VMEM((4, 2, half, width), BF),
            pltpu.VMEM((4, half, width), BF),
            pltpu.VMEM((4, half, width), BF),
            pltpu.VMEM((length, width), F32),
            pltpu.VMEM((length, blk), F32),
            pltpu.VMEM((blk, 2 * blk), F32),
        ]
        + [
            pltpu.SemaphoreType.DMA((count,)),
            pltpu.SemaphoreType.DMA((n,)),
            pltpu.SemaphoreType.DMA((count,)),
        ]
        * 16
        + row_sems() * 3
        + [pltpu.SemaphoreType.DMA((3,)), pltpu.SemaphoreType.DMA((4,)), pltpu.SemaphoreType.DMA((4,))],
        compiler_params=pltpu.CompilerParams(
            collective_id=cid, has_side_effects=True, vmem_limit_bytes=VMEM_LIMIT
        ),
        name="forward",
    )(tok, cot, wb, wi, wo, wg, wu, wd, wr, wig, small)


def mlp_kernel(norm, resid, gain, cot, ends, w_hbm, mg_hbm, g_hbm, o_rec, o_rgrad, o_hid, o_gain,
               w, nbuf, mg, hg, hu, gbuf, part, sibb, got, wsem, msem, gsem, *sems):
    zh, zl, y, x, c = place()
    here = (zh, zl, y, x)
    q, me = zl * 2 + x, dp_at(zh, zl, y, x)
    half, width = norm.shape
    nt, n, rr, blk = w.shape
    tiles, steps, per = nt // 3, width // blk, blk // rr
    rows = Rows(nbuf, sems[:4], here, c)
    sums = Sums(part, sibb, got, sems[4:8], rows)
    greet([dev(me, 1 - c)] + [rows.at(k)[1] for k in (1, 2, 3)])
    nbuf[q, c] = norm[...]
    rows.start()
    loads = []
    for t in range(tiles):
        for i in range(3):
            j = i * tiles + t
            loads.append((t, pltpu.make_async_copy(w_hbm.at[j], w.at[j], wsem.at[j])))
    loads.insert(2, (0, pltpu.make_async_copy(mg_hbm, mg, msem)))
    for _, cp in loads:
        cp.start()

    def row(k, carry):
        pq, _ = rows.at(k)
        rows.arrive(k)

        def first(t, carry):
            @pl.when(k == 0)
            def _():
                for j, cp in loads:

                    @pl.when(t == j)
                    def _():
                        cp.wait()

            a = nbuf[pq].reshape(2 * half, width)
            gate = mm(a, w[t].reshape(width, blk))
            up = mm(a, w[tiles + t].reshape(width, blk))
            grad = mm(mg[pq].reshape(2 * half, width), w[2 * tiles + t].reshape(width, blk))
            act, der = gelu_parts(gate)
            o_hid[pq, t] = (act * up).astype(BF)
            hg[pq, t] = (grad * up * der).astype(BF)
            hu[pq, t] = (grad * act).astype(BF)
            return carry

        lax.fori_loop(0, tiles, first, 0)

        @pl.when(k < 3)
        def _():
            rows.forward(k + 1)

        @pl.when(k > 1)
        def _():
            sums.pass_on(k - 1)

        def second(d, carry):
            total = jnp.zeros((2 * half, blk), F32)
            for t in range(tiles):
                total = total + mm_t(hg[pq, t], w[t, pl.ds(d * per, per)].reshape(blk, blk))
                total = total + mm_t(hu[pq, t], w[tiles + t, pl.ds(d * per, per)].reshape(blk, blk))
            lanes = pl.ds(pl.multiple_of(d * blk, 128), blk)
            part[pq, 0, :, lanes] = total[:half].astype(BF)
            part[pq, 1, :, lanes] = total[half:].astype(BF)
            return carry

        lax.fori_loop(0, steps, second, 0)
        sums.push(k)
        return carry

    def rows_from(k, carry):
        return row(k, carry)

    lax.fori_loop(0, 4, rows_from, 0)
    sums.pass_on(3)

    def out_tile(d):
        at = pl.ds(d * per, per)
        return pltpu.make_async_copy(gbuf.at[:, at], g_hbm.at[:, at], gsem.at[d])

    def grads(d, carry):
        lanes = pl.ds(pl.multiple_of(d * blk, 128), blk)
        nt_ = nbuf[:, :, :, lanes].reshape(8 * half, blk).T
        mt_ = mg[:, :, :, lanes].reshape(8 * half, blk).T
        for i, (left, right) in enumerate(((nt_, hg), (nt_, hu), (mt_, o_hid))):
            for t in range(tiles):
                tile = mm(left, right[:, t].reshape(8 * half, blk))
                gbuf[i * tiles + t, pl.ds(d * per, per)] = tile.astype(BF).reshape(per, rr, blk)
        out_tile(d).start()
        return carry

    lax.fori_loop(0, steps, grads, 0)
    total = sums.pair(0)
    for k in (1, 2, 3):
        total = total + sums.take(k)
    r = resid[...]
    scale = lax.rsqrt(jnp.mean(r * r, axis=-1, keepdims=True) + EPS)
    unit = r * scale
    o_gain[...] = jnp.broadcast_to(jnp.sum(total * unit, axis=0, keepdims=True), o_gain.shape)
    g2 = total * gain[1:2, :]
    back = scale * (g2 - unit * jnp.mean(g2 * unit, axis=-1, keepdims=True))
    e3 = ends[q][0:1, 3:4]
    spot = lax.broadcasted_iota(jnp.int32, (half, 1), 0).astype(F32) + (c * half).astype(F32)
    back = back + jnp.where(spot < e3, cot[...], 0.0)
    o_rgrad[...] = back
    o_rec[...] = back.astype(BF)
    for d in range(steps):
        out_tile(d).wait()
    rows.finish()
    sums.finish()


def mlp_block(norm, resid, gain, cot, ends, mlp_w, mlp_grad, cid):
    half, width = norm.shape
    nt, n, rr, blk = mlp_w.shape
    tiles = nt // 3
    vm = pl.BlockSpec(memory_space=pltpu.VMEM)
    hb = pl.BlockSpec(memory_space=pl.ANY)
    hid = (4, tiles, 2 * half, blk)
    return pl.pallas_call(
        mlp_kernel,
        out_shape=(
            jax.ShapeDtypeStruct(mlp_w.shape, BF),
            jax.ShapeDtypeStruct((half, width), BF),
            jax.ShapeDtypeStruct((half, width), F32),
            jax.ShapeDtypeStruct(hid, BF),
            jax.ShapeDtypeStruct((8, width), F32),
        ),
        in_specs=[vm] * 5 + [hb] * 2,
        out_specs=[hb] + [vm] * 4,
        scratch_shapes=[
            pltpu.VMEM(mlp_w.shape, BF),
            pltpu.VMEM((4, 2, half, width), BF),
            pltpu.VMEM((4, 2, half, width), BF),
            pltpu.VMEM(hid, BF),
            pltpu.VMEM(hid, BF),
            pltpu.VMEM(mlp_w.shape, BF),
            pltpu.VMEM((4, 2, half, width), BF),
            pltpu.VMEM((4, half, width), BF),
            pltpu.VMEM((4, half, width), BF),
            pltpu.SemaphoreType.DMA((nt,)),
            pltpu.SemaphoreType.DMA,
            pltpu.SemaphoreType.DMA((width // blk,)),
        ]
        + row_sems() * 2,
        compiler_params=pltpu.CompilerParams(
            collective_id=cid, has_side_effects=True, vmem_limit_bytes=VMEM_LIMIT
        ),
        name="mlp_block",
    )(norm, resid, gain, cot, ends, mlp_w, mlp_grad)


def mm(a, b):
    return jnp.dot(a, b, preferred_element_type=F32)


def mm_t(a, b):
    return lax.dot_general(a, b, (((1,), (1,)), ((), ())), preferred_element_type=F32)


def t_mm(a, b):
    return lax.dot_general(a, b, (((0,), (0,)), ((), ())), preferred_element_type=F32)


def gelu_tanh(values):
    return jax.nn.gelu(values, approximate=True)


def norm_scale(values):
    return lax.rsqrt(jnp.mean(values * values, axis=-1, keepdims=True) + EPS)


def norm_back(grad, unit, inverse):
    return inverse * (grad - unit * jnp.mean(grad * unit, axis=-1, keepdims=True))


def local(
    tokens, doc_lengths, rec_gain, w_branch, w_input, w_rgate, w_igate, rgate_bias, igate_bias,
    decay_param, conv_weight, conv_bias, w_output, mlp_gain, w_gate, w_up, w_down, cotangent,
):
    n = lax.axis_size("dp")
    zh, zl, y, x, c = place()
    q = zl * 2 + x
    _, half, width = tokens.shape
    length = half * 2
    heads, rb, blk = w_rgate.shape
    taps = conv_weight.shape[0]
    rows = w_branch.shape[0]
    ff = w_gate.shape[1] // 4

    dp = lax.axis_index("dp")

    def lanes(v, per):
        v = v.astype(BF).reshape(-1, per)
        at = (dp * per) % 128
        return lax.dynamic_update_slice(jnp.zeros((v.shape[0], 128), BF), v, (0, at))

    params = jnp.concatenate(
        [rgate_bias[:, None], igate_bias[:, None], decay_param[:, None], conv_weight.transpose(1, 0, 2), conv_bias[:, None]],
        axis=1,
    )
    params = jnp.pad(params, ((0, 0), (0, 16 - params.shape[1]), (0, 0))).reshape(heads * 16, rb)
    lens = doc_lengths.reshape(4).astype(F32)
    e0 = lens[0]
    e1 = e0 + lens[1]
    e2 = e1 + lens[2]
    e3 = e2 + lens[3]
    ends_own = jnp.pad(jnp.stack([e0, e1, e2, e3]).astype(BF)[None], ((0, 13), (0, 124)))
    small = jnp.concatenate([lanes(params, rb), lanes(jnp.stack([rec_gain, mlp_gain]), rows), ends_own], axis=0)
    (
        rec_w, mlp_w, gates, vec, gains_all, group_ends, u, mlp_grad, pre, conv, rate, gate, state, mixed, resid, norm_own,
    ) = forward(
        tokens[0], cotangent[0], w_branch, w_input, w_output.T, w_gate, w_up, w_down.T, w_rgate, w_igate, small, n, taps, 1,
    )
    rec_w = rec_w.reshape(2, 3, width, blk)
    recq, rec4 = (jnp.concatenate([rec_w[h, i] for i in range(3)], axis=1) for h in range(2))
    gain1, gain2 = gains_all[0:1], gains_all[1:2]
    own_ends = lax.dynamic_index_in_dim(group_ends, q, 0, True)
    ends = jnp.concatenate([group_ends, own_ends], axis=0)
    valid_own = ((lax.broadcasted_iota(jnp.int32, (half, 1), 0) + c * half).astype(F32)) < e3
    x_in = tokens[0].astype(F32)
    scale1 = norm_scale(x_in)
    unit1 = x_in * scale1
    u_all = u.reshape(4 * length, width)
    u_own = lax.dynamic_index_in_dim(u, q, 0, False).reshape(length, width)
    mixed_a, mixed_b = mixed[:4].reshape(4 * length, blk), mixed[4]

    def with_own(a, b):
        a = a.reshape(4, length, -1)
        own = lax.dynamic_index_in_dim(a, q, 0, False) + b
        return lax.dynamic_update_index_in_dim(a, own, q, 0)

    def by_half(a):
        return a.astype(BF).reshape(4, 2, half, width)

    g_mlp, rec_own, resid_grad, hid, gain2_sum = mlp_block(
        norm_own, resid, gains_all, cotangent[0], group_ends, mlp_w, mlp_grad, 4
    )
    hidden = hid.transpose(0, 2, 1, 3).reshape(4 * length, ff)
    w_d = mlp_w[2 * ff // blk :].reshape(ff // blk, width, blk).transpose(1, 0, 2).reshape(width, ff)
    mlp_out = act_reduce(by_half(mm_t(hidden, w_d)), 5)
    result = jnp.where(valid_own, resid + mlp_out, 0.0).astype(BF)
    gain2_part = gain2_sum[0]
    grad_mlp = g_mlp.reshape(3 * ff // blk, width, blk).transpose(1, 0, 2).reshape(width, 3 * ff)
    rg = act_gather(rec_own, 8)
    rec_grad = rg.reshape(4 * length, width)
    rec_grad_own = lax.dynamic_index_in_dim(rg, q, 0, False).reshape(length, width)
    mixed_grad = jnp.concatenate(
        [
            mm(rec_grad, recq[:, 2 * blk :]).reshape(4, length, blk),
            mm(rec_grad_own, rec4[:, 2 * blk :]).reshape(1, length, blk),
        ],
        axis=0,
    )
    low, gate_w_grad, vec_grad = rec_backward(taps, pre, gates, vec, ends, conv, rate, gate, state, mixed_grad)
    low_a, low_b = low[:4].reshape(4 * length, 2 * blk), low[4]
    u_part = with_own(mm_t(low_a, recq[:, : 2 * blk]), mm_t(low_b, rec4[:, : 2 * blk]))
    u_grad = act_reduce(by_half(u_part), 9)
    grad_q = jnp.concatenate([t_mm(u_all, low_a).astype(BF), t_mm(rec_grad, mixed_a).astype(BF)], axis=1)
    grad_4 = jnp.concatenate([t_mm(u_own, low_b).astype(BF), t_mm(rec_grad_own, mixed_b).astype(BF)], axis=1)
    gain1_part = jnp.sum(u_grad * unit1, axis=0)
    token_grad = resid_grad + norm_back(u_grad * gain1, unit1, scale1)
    gains = lax.psum(jnp.stack([gain1_part, gain2_part]), "tensor")

    nvg = vec_grad.shape[1]
    depth = -(-(rb + nvg + 2) // 8) * 8

    def small_grads(h, extra):
        v = vec_grad[h].reshape(nvg, n, rb).transpose(1, 0, 2)
        v = jnp.pad(v, ((0, 0), (0, 0), (0, 2 * blk - rb)))
        g = extra.reshape(2, n, rows).transpose(1, 0, 2)
        g = jnp.pad(g, ((0, 0), (0, 0), (0, 2 * blk - rows)))
        s = jnp.concatenate([gate_w_grad[h].reshape(n, rb, 2 * blk), v, g], axis=1)
        return jnp.pad(s, ((0, 0), (0, depth - s.shape[1]), (0, 0)))

    sq = small_grads(0, jnp.zeros_like(gains))
    s4 = small_grads(1, gains)

    def slots(a):
        return a.reshape(n, rows, a.shape[1])

    o_mlp, o_q, o_4, o_sq, o_s4 = grad_reduce(
        (slots(grad_mlp), slots(grad_q), slots(grad_4), sq, s4), (True, True, False, True, False), n, 10
    )
    rec_out = jnp.concatenate([o_q, o_4[None]], axis=0)
    so = jnp.concatenate([o_sq, o_s4[None]], axis=0)

    def heads_cols(a):
        return a.transpose(1, 0, 2).reshape(rows, heads * blk)

    def quarter_cols(a):
        return a.transpose(1, 0, 2).reshape(rows, 4 * ff)

    def vec_out(i):
        return so[:, rb + i, :rb]

    return (
        result[None],
        token_grad[None],
        o_s4[rb + nvg, :rows],
        heads_cols(rec_out[:, :, :blk]),
        heads_cols(rec_out[:, :, blk : 2 * blk]),
        so[:, :rb, :blk],
        so[:, :rb, blk:],
        vec_out(0),
        vec_out(1),
        vec_out(2),
        jnp.stack([vec_out(4 + k) for k in range(taps)]),
        vec_out(3),
        rec_out[:, :, 2 * blk :].transpose(0, 2, 1).reshape(heads * blk, rows),
        o_s4[rb + nvg + 1, :rows],
        quarter_cols(o_mlp[:, :, :ff]),
        quarter_cols(o_mlp[:, :, ff : 2 * ff]),
        o_mlp[:, :, 2 * ff :].transpose(0, 2, 1).reshape(4 * ff, rows),
    )


def solution(mesh):
    return jax.shard_map(
        local,
        mesh=mesh,
        in_specs=(
            P("dp", "tensor", None),
            P("dp", None),
            P("dp"),
            P("dp", "tensor"),
            P("dp", "tensor"),
            P("tensor", "dp", None),
            P("tensor", "dp", None),
            P("tensor", "dp"),
            P("tensor", "dp"),
            P("tensor", "dp"),
            P(None, "tensor", "dp"),
            P("tensor", "dp"),
            P("tensor", "dp"),
            P("dp"),
            P("dp", "tensor"),
            P("dp", "tensor"),
            P("tensor", "dp"),
            P("dp", "tensor", None),
        ),
        out_specs=(
            P("dp", "tensor", None),
            P("dp", "tensor", None),
            P("dp"),
            P("dp", "tensor"),
            P("dp", "tensor"),
            P("tensor", "dp", None),
            P("tensor", "dp", None),
            P("tensor", "dp"),
            P("tensor", "dp"),
            P("tensor", "dp"),
            P(None, "tensor", "dp"),
            P("tensor", "dp"),
            P("tensor", "dp"),
            P("dp"),
            P("dp", "tensor"),
            P("dp", "tensor"),
            P("tensor", "dp"),
        ),
        check_vma=False,
    )
```

```python
import functools

import jax
import jax.numpy as jnp
from jax import lax
from jax.experimental import pallas as pl
from jax.experimental.pallas import tpu as pltpu
from jax.sharding import PartitionSpec as P

MESH = pl.DeviceIdType.MESH
BF = jnp.bfloat16
F32 = jnp.float32
EPS = 1e-06
DECAY = 8.0
GC = 0.7978845608028654
GK = 0.044715
VMEM_LIMIT = 62 * 1024 * 1024


def dp_at(zh, zl, y, x):
    return ((zh * 2 + zl) * 2 + y) * 2 + x


def place():
    dp = lax.axis_index("dp")
    return dp // 8, (dp // 4) % 2, (dp // 2) % 2, dp % 2, lax.axis_index("tensor")


def dev(dp, core):
    return {"dp": dp, "tensor": core}


def greet(devices):
    sem = pltpu.get_barrier_semaphore()
    for d in devices:
        pl.semaphore_signal(sem, inc=1, device_id=d, device_id_type=MESH)
    pl.semaphore_wait(sem, len(devices))


def remote(src, dst, ssem, rsem, d):
    return pltpu.make_async_remote_copy(
        src_ref=src, dst_ref=dst, send_sem=ssem, recv_sem=rsem, device_id=d, device_id_type=MESH
    )


def plane(zh, zl, y, x, high):
    out = []
    for kh in range(high):
        for kl in range(2):
            for kx in range(2):
                ph, pz, px = (zh + kh) % high, (zl + kl) % 2, (x + kx) % 2
                out.append((ph, pz, px))
    return out


def gelu_parts(v):
    t = jnp.tanh(GC * (v + GK * v * v * v))
    act = 0.5 * v * (1.0 + t)
    der = 0.5 * (1.0 + t) + 0.5 * v * (1.0 - t * t) * GC * (1.0 + 3.0 * GK * v * v)
    return act, der


def segments(ends, length, width, taps):
    t = lax.broadcasted_iota(jnp.int32, (length, width), 0).astype(F32)

    def seg(at):
        total = jnp.zeros((length, width), F32)
        for j in range(4):
            total = total + jnp.where(at >= ends[:, j : j + 1], 1.0, 0.0)
        return total

    here = seg(t)
    same = []
    for k in range(1, taps):
        same.append(jnp.where((t >= float(k)) & (seg(t - float(k)) == here), 1.0, 0.0))
    return same


def scan8(a, b, reverse):
    length, width = a.shape
    row = lax.broadcasted_iota(jnp.int32, (length, width), 0) % 8
    for d in (1, 2, 4):
        if reverse:
            ash, bsh = pltpu.roll(a, length - d, 0), pltpu.roll(b, length - d, 0)
            ok = row < 8 - d
        else:
            ash, bsh = pltpu.roll(a, d, 0), pltpu.roll(b, d, 0)
            ok = row >= d
        b = b + a * jnp.where(ok, bsh, 0.0)
        a = a * jnp.where(ok, ash, 1.0)
    return a, b


def full_scan(a, b, out_ref, a_ref, reverse):
    length, width = a.shape
    a8, b8 = scan8(a, b, reverse)
    a_ref[...] = a8
    out_ref[...] = b8
    blocks = length // 8

    def step(i, carry):
        at = (blocks - 1 - i if reverse else i) * 8
        at = pl.multiple_of(at, 8)
        now = out_ref[pl.ds(at, 8), :] + a_ref[pl.ds(at, 8), :] * carry
        out_ref[pl.ds(at, 8), :] = now
        return now[0:1, :] if reverse else now[7:8, :]

    lax.fori_loop(0, blocks, step, jnp.zeros((1, width), F32))


class Gather:
    def __init__(self, slot, parts, sems, here, there, core):
        self.slot, self.parts, (self.send, self.recv, self.fsend) = slot, parts, sems
        zh, zl, y, x = here
        self.q = zl * 2 + x
        self.me = dp_at(zh, zl, y, x)
        self.near = [dp_at(h, z, y, w) for h, z, w in there]
        self.far = [dp_at(h, z, 1 - y, w) for h, z, w in there]
        self.pick = [z * 2 + w for _, z, w in there]
        self.core = core
        self.other = dev(dp_at(zh, zl, 1 - y, x), core)

    def ks(self, far):
        count = len(self.near)
        return range(4, count) if far else range(4)

    def start(self, far):
        for k in self.ks(far):
            for piece, part in self.parts:
                src = piece(self.pick[k])
                dst = part(self.slot(self.me, self.pick[k]))
                if k == 0:
                    pltpu.make_async_copy(src, dst, self.send.at[0]).start()
                else:
                    d = dev(self.near[k], self.core)
                    remote(src, dst, self.send.at[k], self.recv.at[self.me], d).start()

    def forward(self, k):
        land = self.slot(self.near[k], self.q)
        if k == 0:
            pltpu.make_async_copy(land, land, self.send.at[0]).wait()
        else:
            remote(land, land, self.send.at[k], self.recv.at[self.near[k]], self.other).wait_recv()
        remote(land, land, self.fsend.at[k], self.recv.at[self.near[k]], self.other).start()

    def forward_all(self, far):
        for k in self.ks(far):
            self.forward(k)

    def arrive_all(self):
        for k in range(len(self.far)):
            land = self.slot(self.far[k], self.q)
            remote(land, land, self.fsend.at[k], self.recv.at[self.far[k]], self.other).wait_recv()

    def finish(self):
        for k in range(len(self.near)):
            land = self.slot(self.near[k], self.q)
            remote(land, land, self.fsend.at[k], self.recv.at[self.near[k]], self.other).wait_send()
            if k:
                remote(land, land, self.send.at[k], self.recv.at[self.near[k]], self.other).wait_send()


class Rows:
    def __init__(self, buf, sems, here, core):
        self.buf, (self.send, self.recv, self.fsend, self.frecv) = buf, sems
        self.here, self.core = here, core
        zh, zl, y, x = here
        self.q = zl * 2 + x
        self.sib = dev(dp_at(zh, zl, y, x), 1 - core)

    def at(self, k):
        zh, zl, y, x = self.here
        pz, px = (zl + k // 2) % 2, (x + k % 2) % 2
        return pz * 2 + px, dev(dp_at(zh, pz, y, px), self.core)

    def start(self):
        own = self.buf.at[self.q, self.core]
        remote(own, own, self.fsend.at[0], self.frecv.at[self.q], self.sib).start()
        for k in (1, 2, 3):
            _, d = self.at(k)
            remote(own, own, self.send.at[k], self.recv.at[self.q], d).start()

    def forward(self, k):
        pq, d = self.at(k)
        land = self.buf.at[pq, self.core]
        remote(land, land, self.send.at[k], self.recv.at[pq], d).wait_recv()
        remote(land, land, self.fsend.at[k], self.frecv.at[pq], self.sib).start()

    def arrive(self, k):
        pq, _ = self.at(k)
        land = self.buf.at[pq, 1 - self.core]
        remote(land, land, self.fsend.at[k], self.frecv.at[pq], self.sib).wait_recv()

    def finish(self):
        own = self.buf.at[self.q, self.core]
        for k in range(4):
            remote(own, own, self.fsend.at[k], self.frecv.at[self.q], self.sib).wait_send()
            if k:
                remote(own, own, self.send.at[k], self.recv.at[self.q], self.sib).wait_send()


def row_sems():
    return [pltpu.SemaphoreType.DMA((4,))] * 4


class Sums:
    def __init__(self, part, sib, got, sems, rows):
        self.part, self.sib_buf, self.got = part, sib, got
        self.ssend, self.srecv, self.send, self.recv = sems
        self.rows = rows

    def push(self, k):
        r = self.rows
        pq, _ = r.at(k)
        remote(
            self.part.at[pq, 1 - r.core], self.sib_buf.at[pq], self.ssend.at[k], self.srecv.at[pq], r.sib
        ).start()

    def pair(self, k):
        r = self.rows
        pq, _ = r.at(k)
        land = self.sib_buf.at[pq]
        remote(land, land, self.ssend.at[k], self.srecv.at[pq], r.sib).wait_recv()
        return self.part[pq, r.core].astype(F32) + self.sib_buf[pq].astype(F32)

    def pass_on(self, k):
        r = self.rows
        pq, d = r.at(k)
        self.part[pq, r.core] = self.pair(k).astype(BF)
        remote(self.part.at[pq, r.core], self.got.at[r.q], self.send.at[k], self.recv.at[r.q], d).start()

    def take(self, k):
        r = self.rows
        pq, _ = r.at(k)
        land = self.got.at[pq]
        remote(land, land, self.send.at[k], self.recv.at[pq], r.sib).wait_recv()
        return self.got[pq].astype(F32)

    def ready(self):
        r = self.rows
        land = self.sib_buf.at[r.q]
        remote(land, land, self.ssend.at[0], self.srecv.at[r.q], r.sib).wait_recv()
        for k in (1, 2, 3):
            pq, _ = r.at(k)
            land = self.got.at[pq]
            remote(land, land, self.send.at[k], self.recv.at[pq], r.sib).wait_recv()

    def own(self, at):
        r = self.rows
        total = self.part[r.q, r.core, at].astype(F32) + self.sib_buf[r.q, at].astype(F32)
        for k in (1, 2, 3):
            total = total + self.got[r.at(k)[0], at].astype(F32)
        return total

    def finish(self):
        r = self.rows
        land = self.got.at[r.q]
        for k in range(4):
            remote(land, land, self.ssend.at[k], self.srecv.at[r.q], r.sib).wait_send()
            if k:
                remote(land, land, self.send.at[k], self.recv.at[r.q], r.sib).wait_send()


def rec_unit(taps, branch, conv_in, vec, gates, ends, state_ref, a_ref):
    same, conv, r, gate = rec_gates(taps, conv_in, vec, gates, ends)
    log_a = (-DECAY * r) * vec[2:3]
    a = jnp.exp(log_a)
    start = same[0] == 0.0
    a_eff = jnp.where(start, 0.0, a)
    mult = jnp.where(start, 1.0, jnp.sqrt(-jnp.tanh(log_a) * (1.0 + a * a)))
    full_scan(a_eff, mult * gate * conv, state_ref, a_ref, False)
    act, _ = gelu_parts(branch)
    return (state_ref[...] * act).astype(BF)


SMALL_ROWS = 96


def forward_kernel(n, taps, heads, *refs):
    (tok, cot, wb, wi, wo, wg, wu, wd, wr, wig, small) = refs[:11]
    (o_rec, o_mlp, o_gate, o_vec, o_gain, o_ends, o_u, o_grad, pre, state, mixed, resid, o_norm) = refs[11:24]
    (rec, gat, sml, u_buf, og, part, sibb, got, extra, a_scr, gfull) = refs[24:35]
    sems = refs[35:]
    g_sems, r1, r2, s1, (fin, h_send, h_recv) = sems[:48], sems[48:52], sems[52:56], sems[56:60], sems[60:]
    zh, zl, y, x, c = place()
    here = (zh, zl, y, x)
    q, me = zl * 2 + x, dp_at(zh, zl, y, x)
    high = n // 8
    there = plane(zh, zl, y, x, high)
    half, width = tok.shape
    length, blk = pre.shape[1], pre.shape[2] // 2
    ff = wg.shape[1] // 4
    rb, rr = wr.shape[1], wb.shape[0]
    greet(
        [dev(dp_at(h, z, y, w), c) for h, z, w in there[1:]]
        + [dev(dp_at(zh, zl, 1 - y, x), c), dev(me, 1 - c)]
    )

    def whole(ref):
        return ref

    def head_cols(ref):
        return lambda p: ref.at[:, pl.ds(pl.multiple_of(p * blk, 128), blk)]

    def make(i, slot, parts):
        return Gather(slot, parts, g_sems[3 * i : 3 * i + 3], here, there, c)

    smalls = make(0, lambda s, g: sml.at[s], [(lambda p: small, whole)])
    gats, recs, mlps = [], [], []
    for h in range(2):
        pick = (lambda ref: lambda p: ref.at[p]) if h == 0 else (lambda ref: lambda p: ref.at[heads - 1])
        gats.append(
            make(
                1 + h,
                lambda s, g, h=h: gat.at[h, s],
                [
                    (pick(w), lambda r, i=i: r.at[:, pl.ds(i * blk, blk)])
                    for i, w in enumerate((wr, wig))
                ],
            )
        )
    for i, w in enumerate((wb, wi, wo)):
        recs.append(make(3 + i, lambda s, g, i=i: rec.at[0, i, s], [(head_cols(w), whole)]))
    quarter = rr // 4

    def shared_piece(ref):
        return lambda p: ref.at[pl.ds(pl.multiple_of(p * quarter, 8), quarter), pl.ds((heads - 1) * blk, blk)]

    def shared_rows(s, g):
        return rec.at[1, :, s, pl.ds(pl.multiple_of(g * quarter, 8), quarter), :]

    shared = make(
        6, shared_rows, [(shared_piece(w), lambda r, i=i: r.at[i]) for i, w in enumerate((wb, wi, wo))]
    )
    for i, w in enumerate((wg, wu, wd)):
        for t in range(ff // blk):
            piece = lambda p, w=w, t=t: w.at[:, pl.ds(pl.multiple_of(p * ff + t * blk, 128), blk)]
            j = i * (ff // blk) + t
            mlps.append(make(7 + j, lambda s, g, j=j: o_mlp.at[j, s], [(piece, whole)]))
    count = len(there)
    order = [recs[0], gats[0], recs[1], gats[1], shared, recs[2]] + mlps
    ahead = 2

    def pump(j):
        if j + ahead < len(order):
            order[j + ahead].forward_all(False)
        order[j].forward_all(True)
        if j + ahead < len(order):
            order[j + ahead].start(True)
        if j + 2 * ahead < len(order):
            order[j + 2 * ahead].start(False)

    smalls.start(True)
    smalls.start(False)
    for j in range(2 * ahead):
        if j < ahead:
            order[j].start(True)
        order[j].start(False)

    xin = tok[...].astype(F32)
    unit = xin * lax.rsqrt(jnp.mean(xin * xin, axis=-1, keepdims=True) + EPS)
    resid[...] = unit
    smalls.forward_all(False)
    smalls.forward_all(True)
    for j in range(ahead):
        order[j].forward_all(False)
    smalls.arrive_all()
    per_vec, per_gain = blk // 128, width // 128
    base = (heads - 1) * 16
    for h in range(2):
        at = pl.multiple_of(q * 16, 16) if h == 0 else base
        groups = [jnp.zeros((16, 128), F32)] * per_vec
        for s in range(n):
            g = s * rb // 128
            groups[g] = groups[g] + sml[s, pl.ds(at, 16), :].astype(F32)
        raw = jnp.concatenate(groups, axis=1)
        decay = raw[2:3]
        o_vec[h, 0:2, :] = raw[0:2]
        o_vec[h, 2:3, :] = jnp.log1p(jnp.exp(-decay))
        o_vec[h, 3:4, :] = jax.nn.sigmoid(-decay)
        o_vec[h, 4 : 5 + taps, :] = raw[3 : 4 + taps]
    groups = [None] * per_gain
    for s in range(n):
        g = s * rr // 128
        v = sml[s, SMALL_ROWS - 16 : SMALL_ROWS, :].astype(F32)
        groups[g] = v if groups[g] is None else groups[g] + v
    for g in range(per_gain):
        o_gain[:, g * 128 : (g + 1) * 128] = groups[g][0:8]
    for j in range(4):
        v = sml[dp_at(zh, j // 2, y, j % 2), SMALL_ROWS - 16 : SMALL_ROWS, :].astype(F32)
        o_ends[j] = jnp.broadcast_to(v[2:3], (8, 128))
    u_rows = Rows(u_buf, r1, here, c)
    g_rows = Rows(o_grad, r2, here, c)
    u_buf[q, c] = (resid[...] * o_gain[0:1, :]).astype(BF)
    u_rows.start()
    e3 = o_ends[q][0:1, 3:4]
    spot = lax.broadcasted_iota(jnp.int32, (half, 1), 0).astype(F32) + (c * half).astype(F32)
    og[...] = jnp.where(spot < e3, cot[...], 0.0).astype(BF)
    own_grad = o_grad.at[q, c]
    place_grad = pltpu.make_async_copy(og, own_grad, fin.at[0])
    place_grad.start()
    place_grad.wait()
    g_rows.start()
    for j in range(3):
        pump(j)
    for k in (1, 2, 3):
        u_rows.forward(k)
    for j in range(3, 6):
        pump(j)
    for a in gats + recs[:2] + [shared]:
        a.arrive_all()

    def group_region(g):
        return rec.at[1, :, :, pl.ds(pl.multiple_of(g * quarter, 8), quarter), :]

    for k in (1, 2, 3):
        _, d = u_rows.at(k)
        remote(group_region(q), group_region(q), h_send.at[k], h_recv.at[q], d).start()
    for h in range(2):
        if rb % 16 == 0:
            o_gate[h] = gat[h].reshape(blk, 2 * blk)
        else:
            for s in range(n):
                gfull[s * rb : (s + 1) * rb, :] = gat[h, s].astype(F32)
            o_gate[h] = gfull[...].astype(BF)
    for k in range(4):
        u_rows.arrive(k)
    recs[2].arrive_all()
    for k in (1, 2, 3):
        pq, d = u_rows.at(k)
        remote(group_region(pq), group_region(pq), h_send.at[k], h_recv.at[pq], d).wait_recv()
    keep = [pltpu.make_async_copy(rec, o_rec, fin.at[1]), pltpu.make_async_copy(u_buf, o_u, fin.at[2])]
    for cp in keep:
        cp.start()

    sums = Sums(part, sibb, got, s1, u_rows)

    def step(i, carry):
        h = jnp.where(i == 0, 1, 0)
        k = jnp.maximum(i - 1, 0)
        pq, _ = u_rows.at(k)
        at = jnp.where(i == 0, 4, pq)
        rows = u_buf[pq].reshape(2 * half, width)
        for j in range(2):
            w = rec[h, j].reshape(width, blk)
            pre[at, :, j * blk : (j + 1) * blk] = mm(rows, w)
        mx = rec_unit(
            taps, pre[at, :, :blk], pre[at, :, blk:], o_vec[h], o_gate[h], o_ends[pq][0:1, :], state.at[at], a_scr
        )
        mixed[at] = mx
        per = 512 // rr if rr <= 512 else 1

        def cols_out(t, carry):
            w = rec[h, 2, pl.ds(t * per, per)].reshape(per * rr, blk)
            tile = mm_t(mx, w)
            lanes = pl.ds(pl.multiple_of(t * (per * rr), 128), per * rr)
            tile = tile + jnp.where(i == 1, extra[:, lanes], 0.0)

            @pl.when(i == 0)
            def _():
                extra[:, lanes] = tile

            @pl.when(i > 0)
            def _():
                part[pq, 0, :, lanes] = tile[:half].astype(BF)
                part[pq, 1, :, lanes] = tile[half:].astype(BF)

            return carry

        lax.fori_loop(0, width // (per * rr), cols_out, 0)

        @pl.when(i > 0)
        def _():
            sums.push(k)

        @pl.when(i == 2)
        def _():
            resid[...] = tok[...].astype(F32) + sums.pair(0)

        @pl.when(i > 2)
        def _():
            sums.pass_on(k - 1)

        for j, m in ((1, 6), (3, 7)):

            @pl.when(i == j)
            def _():
                pump(m)

        return carry

    extra[...] = jnp.zeros_like(extra)
    lax.fori_loop(0, 5, step, 0)
    sums.pass_on(3)
    pump(8)
    for k in (1, 2, 3):
        g_rows.forward(k)
    for k in (1, 2, 3):
        resid[...] += sums.take(k)
    total = resid[...]
    unit = total * lax.rsqrt(jnp.mean(total * total, axis=-1, keepdims=True) + EPS)
    o_norm[...] = (unit * o_gain[1:2, :]).astype(BF)
    for j in range(9, len(order)):
        pump(j)
    for a in mlps:
        a.arrive_all()
    for k in range(4):
        g_rows.arrive(k)
    for k in (1, 2, 3):
        _, d = u_rows.at(k)
        remote(group_region(q), group_region(q), h_send.at[k], h_recv.at[q], d).wait_send()
    for a in [smalls, shared] + mlps + gats + recs + [u_rows, g_rows, sums]:
        a.finish()
    for cp in keep:
        cp.wait()


def forward(tok, cot, wb, wi, wo, wg, wu, wd, wr, wig, small, n, taps, cid):
    half, width = tok.shape
    heads, rb, blk = wr.shape
    rr = wb.shape[0]
    length = 2 * half
    ff = wg.shape[1] // 4
    vm = pl.BlockSpec(memory_space=pltpu.VMEM)
    hb = pl.BlockSpec(memory_space=pl.ANY)

    def sds(*shape, t=F32):
        return jax.ShapeDtypeStruct(shape, t)

    unit = sds(5, length, blk)
    outs = (
        (sds(2, 3, n, rr, blk, t=BF), hb),
        (sds(3 * ff // blk, n, rr, blk, t=BF), hb),
        (sds(2, blk, 2 * blk, t=BF), vm),
        (sds(2, 16, blk), vm),
        (sds(8, width), vm),
        (sds(4, 8, 128), vm),
        (sds(4, 2, half, width, t=BF), hb),
        (sds(4, 2, half, width, t=BF), hb),
        (sds(5, length, 2 * blk), vm),
        (unit, vm),
        (sds(5, length, blk, t=BF), vm),
        (sds(half, width), vm),
        (sds(half, width, t=BF), vm),
    )
    count = n // 2
    return pl.pallas_call(
        functools.partial(forward_kernel, n, taps, heads),
        out_shape=tuple(o for o, _ in outs),
        in_specs=[vm, vm] + [hb] * 9,
        out_specs=[s for _, s in outs],
        scratch_shapes=[
            pltpu.VMEM((2, 3, n, rr, blk), BF),
            pltpu.VMEM((2, n, rb, 2 * blk), BF),
            pltpu.VMEM((n, SMALL_ROWS, 128), BF),
            pltpu.VMEM((4, 2, half, width), BF),
            pltpu.VMEM((half, width), BF),
            pltpu.VMEM((4, 2, half, width), BF),
            pltpu.VMEM((4, half, width), BF),
            pltpu.VMEM((4, half, width), BF),
            pltpu.VMEM((length, width), F32),
            pltpu.VMEM((length, blk), F32),
            pltpu.VMEM((blk, 2 * blk), F32),
        ]
        + [
            pltpu.SemaphoreType.DMA((count,)),
            pltpu.SemaphoreType.DMA((n,)),
            pltpu.SemaphoreType.DMA((count,)),
        ]
        * 16
        + row_sems() * 3
        + [pltpu.SemaphoreType.DMA((3,)), pltpu.SemaphoreType.DMA((4,)), pltpu.SemaphoreType.DMA((4,))],
        compiler_params=pltpu.CompilerParams(
            collective_id=cid, has_side_effects=True, vmem_limit_bytes=VMEM_LIMIT
        ),
        name="forward",
    )(tok, cot, wb, wi, wo, wg, wu, wd, wr, wig, small)


def mlp_kernel(norm, resid, gain, cot, ends, w_hbm, mg_hbm, g_hbm, o_rec, o_rgrad, o_hid, o_gain,
               w, nbuf, mg, hg, hu, gbuf, part, sibb, got, wsem, msem, gsem, *sems):
    zh, zl, y, x, c = place()
    here = (zh, zl, y, x)
    q, me = zl * 2 + x, dp_at(zh, zl, y, x)
    half, width = norm.shape
    nt, n, rr, blk = w.shape
    tiles, steps, per = nt // 3, width // blk, blk // rr
    rows = Rows(nbuf, sems[:4], here, c)
    sums = Sums(part, sibb, got, sems[4:8], rows)
    greet([dev(me, 1 - c)] + [rows.at(k)[1] for k in (1, 2, 3)])
    nbuf[q, c] = norm[...]
    rows.start()
    loads = []
    for t in range(tiles):
        for i in range(3):
            j = i * tiles + t
            loads.append((t, pltpu.make_async_copy(w_hbm.at[j], w.at[j], wsem.at[j])))
    loads.insert(2, (0, pltpu.make_async_copy(mg_hbm, mg, msem)))
    for _, cp in loads:
        cp.start()

    def row(k, carry):
        pq, _ = rows.at(k)
        rows.arrive(k)

        def first(t, carry):
            @pl.when(k == 0)
            def _():
                for j, cp in loads:

                    @pl.when(t == j)
                    def _():
                        cp.wait()

            a = nbuf[pq].reshape(2 * half, width)
            gate = mm(a, w[t].reshape(width, blk))
            up = mm(a, w[tiles + t].reshape(width, blk))
            grad = mm(mg[pq].reshape(2 * half, width), w[2 * tiles + t].reshape(width, blk))
            act, der = gelu_parts(gate)
            o_hid[t, pq] = (act * up).astype(BF)
            hg[t, pq] = (grad * up * der).astype(BF)
            hu[t, pq] = (grad * act).astype(BF)
            return carry

        lax.fori_loop(0, tiles, first, 0)

        @pl.when(k < 3)
        def _():
            rows.forward(k + 1)

        @pl.when(k > 1)
        def _():
            sums.pass_on(k - 1)

        def second(d, carry):
            total = jnp.zeros((2 * half, blk), F32)
            for t in range(tiles):
                total = total + mm_t(hg[t, pq], w[t, pl.ds(d * per, per)].reshape(blk, blk))
                total = total + mm_t(hu[t, pq], w[tiles + t, pl.ds(d * per, per)].reshape(blk, blk))
            lanes = pl.ds(pl.multiple_of(d * blk, 128), blk)
            part[pq, 0, :, lanes] = total[:half].astype(BF)
            part[pq, 1, :, lanes] = total[half:].astype(BF)
            return carry

        lax.fori_loop(0, steps, second, 0)
        sums.push(k)
        return carry

    def rows_from(k, carry):
        return row(k, carry)

    lax.fori_loop(0, 4, rows_from, 0)
    sums.pass_on(3)

    def out_tile(d):
        at = pl.ds(d * per, per)
        return pltpu.make_async_copy(gbuf.at[:, at], g_hbm.at[:, at], gsem.at[d])

    def grads(d, carry):
        lanes = pl.ds(pl.multiple_of(d * blk, 128), blk)
        nt_ = nbuf[:, :, :, lanes].reshape(8 * half, blk).T
        mt_ = mg[:, :, :, lanes].reshape(8 * half, blk).T
        for i, (left, right) in enumerate(((nt_, hg), (nt_, hu), (mt_, o_hid))):
            for t in range(tiles):
                tile = mm(left, right[t].reshape(8 * half, blk))
                gbuf[i * tiles + t, pl.ds(d * per, per)] = tile.astype(BF).reshape(per, rr, blk)
        out_tile(d).start()
        return carry

    lax.fori_loop(0, steps, grads, 0)
    sums.ready()
    e3 = ends[q][0:1, 3:4]

    def finish(i, acc):
        at = pl.ds(pl.multiple_of(i * 32, 32), 32)
        total, r = sums.own(at), resid[at, :]
        scale = lax.rsqrt(jnp.mean(r * r, axis=-1, keepdims=True) + EPS)
        unit = r * scale
        g2 = total * gain[1:2, :]
        back = scale * (g2 - unit * jnp.mean(g2 * unit, axis=-1, keepdims=True))
        spot = lax.broadcasted_iota(jnp.int32, (32, 1), 0) + (c * half + i * 32)
        back = back + jnp.where(spot.astype(F32) < e3, cot[at, :], 0.0)
        o_rgrad[at, :] = back
        o_rec[at, :] = back.astype(BF)
        return acc + jnp.sum(total * unit, axis=0, keepdims=True)

    gsum = lax.fori_loop(0, half // 32, finish, jnp.zeros((1, width), F32))
    o_gain[...] = jnp.broadcast_to(gsum, o_gain.shape)
    for d in range(steps):
        out_tile(d).wait()
    rows.finish()
    sums.finish()


def mlp_block(norm, resid, gain, cot, ends, mlp_w, mlp_grad, cid):
    half, width = norm.shape
    nt, n, rr, blk = mlp_w.shape
    tiles = nt // 3
    vm = pl.BlockSpec(memory_space=pltpu.VMEM)
    hb = pl.BlockSpec(memory_space=pl.ANY)
    hid = (tiles, 4, 2 * half, blk)
    return pl.pallas_call(
        mlp_kernel,
        out_shape=(
            jax.ShapeDtypeStruct(mlp_w.shape, BF),
            jax.ShapeDtypeStruct((half, width), BF),
            jax.ShapeDtypeStruct((half, width), F32),
            jax.ShapeDtypeStruct(hid, BF),
            jax.ShapeDtypeStruct((8, width), F32),
        ),
        in_specs=[vm] * 5 + [hb] * 2,
        out_specs=[hb] + [vm] * 4,
        scratch_shapes=[
            pltpu.VMEM(mlp_w.shape, BF),
            pltpu.VMEM((4, 2, half, width), BF),
            pltpu.VMEM((4, 2, half, width), BF),
            pltpu.VMEM(hid, BF),
            pltpu.VMEM(hid, BF),
            pltpu.VMEM(mlp_w.shape, BF),
            pltpu.VMEM((4, 2, half, width), BF),
            pltpu.VMEM((4, half, width), BF),
            pltpu.VMEM((4, half, width), BF),
            pltpu.SemaphoreType.DMA((nt,)),
            pltpu.SemaphoreType.DMA,
            pltpu.SemaphoreType.DMA((width // blk,)),
        ]
        + row_sems() * 2,
        compiler_params=pltpu.CompilerParams(
            collective_id=cid, has_side_effects=True, vmem_limit_bytes=VMEM_LIMIT
        ),
        name="mlp_block",
    )(norm, resid, gain, cot, ends, mlp_w, mlp_grad)


class Scatter:
    def __init__(self, away, mine, pair, landed, sems, here, there, core):
        self.away, self.mine, self.pair, self.landed = away, mine, pair, landed
        self.ysend, self.yrecv, self.send, self.recv = sems
        zh, zl, y, x = here
        self.core = core
        self.own = zh * 4 + zl * 2 + x
        self.places = [
            (h * 4 + z * 2 + w, dp_at(h, z, y, w), dp_at(h, z, 1 - y, w)) for h, z, w in (*there[1:], there[0])
        ]
        self.other = dev(dp_at(zh, zl, 1 - y, x), core)

    def start(self):
        for j, _, far in self.places:
            remote(self.away(far), self.pair(j), self.ysend.at[j], self.yrecv.at[j], self.other).start()

    def pass_on(self):
        last = len(self.places) - 1
        for i, (j, near, _) in enumerate(self.places):
            slot = self.pair(j)
            remote(slot, slot, self.ysend.at[j], self.yrecv.at[j], self.other).wait_recv()
            slot[...] = (self.mine(near).astype(F32) + slot[...].astype(F32)).astype(slot.dtype)
            if i == last:
                pltpu.make_async_copy(slot, self.landed(self.own), self.send.at[j]).start()
            else:
                remote(
                    slot, self.landed(self.own), self.send.at[j], self.recv.at[self.own], dev(near, self.core)
                ).start()

    def collect(self):
        last = len(self.places) - 1
        for i, (j, _, _) in enumerate(self.places):
            slot, land = self.pair(j), self.landed(j)
            remote(slot, slot, self.ysend.at[j], self.yrecv.at[j], self.other).wait_send()
            if i == last:
                pltpu.make_async_copy(land, land, self.send.at[j]).wait()
            else:
                remote(land, land, self.send.at[j], self.recv.at[j], self.other).wait_recv()
                remote(slot, slot, self.send.at[j], self.recv.at[j], self.other).wait_send()


def scatter_sems(high):
    return [pltpu.SemaphoreType.DMA((high * 4,))] * 4


def rec_gates(taps, conv_in, vec, gates, ends):
    length, blk = conv_in.shape
    same = segments(ends, length, blk, taps)
    conv = conv_in * vec[4:5] + vec[4 + taps : 5 + taps]
    for k in range(1, taps):
        conv = conv + pltpu.roll(conv_in, k, 0) * same[k - 1] * vec[4 + k : 5 + k]
    pre = jnp.dot(conv.astype(BF), gates, preferred_element_type=F32)
    r = jax.nn.sigmoid(pre[:, :blk] + vec[0:1])
    gate = jax.nn.sigmoid(pre[:, blk:] + vec[1:2])
    return same, conv, r, gate


def rec_unit_back(taps, branch, conv_in, vec, gates, ends, state, mg, carry_ref, a_ref):
    length, blk = branch.shape
    same, conv, r, gate = rec_gates(taps, conv_in, vec, gates, ends)
    start = same[0] == 0.0
    act, der = gelu_parts(branch)
    branch_low = (mg * state * der).astype(BF)
    log_a = (-DECAY * r) * vec[2:3]
    a = jnp.exp(log_a)
    a_eff = jnp.where(start, 0.0, a)
    row = lax.broadcasted_iota(jnp.int32, (length, blk), 0)
    a_next = jnp.where(row < length - 1, pltpu.roll(a_eff, length - 1, 0), 0.0)
    full_scan(a_next, mg * act, carry_ref, a_ref, True)
    carry = carry_ref[...]
    prev = jnp.where(row > 0, pltpu.roll(state, 1, 0), 0.0)
    raw = jnp.sqrt(-jnp.tanh(log_a) * (1.0 + a * a))
    mult = jnp.where(start, 1.0, raw)
    log_grad = jnp.where(start, 0.0, carry * prev * a - carry * gate * conv * (a * a) / raw)
    r_grad = log_grad * (-DECAY * vec[2:3]) * (r * (1.0 - r))
    i_grad = carry * mult * conv * (gate * (1.0 - gate))
    pre_low = jnp.concatenate([r_grad.astype(BF), i_grad.astype(BF)], axis=1)
    conv_grad = carry * mult * gate + mm_t(pre_low, gates)
    gate_grads = t_mm(conv.astype(BF), pre_low)

    def total(v):
        return jnp.sum(v, axis=0, keepdims=True)

    sums = [total(r_grad), total(i_grad), total(log_grad * (DECAY * r) * vec[3:4]), total(conv_grad)]
    inp = conv_grad * vec[4:5]
    sums.append(total(conv_grad * conv_in))
    for k in range(1, taps):
        masked = conv_grad * same[k - 1]
        sums.append(total(masked * pltpu.roll(conv_in, k, 0)))
        inp = inp + pltpu.roll(masked, length - k, 0) * vec[4 + k : 5 + k]
    return branch_low, inp.astype(BF), gate_grads, jnp.concatenate(sums, axis=0)


def backward_kernel(n, taps, *refs):
    (tok, rgrad, resid, gain, gsum2, ends, vec, gates, pre, state, mixed) = refs[:11]
    (rec_own, hid, g_hbm, rec_hbm, mlp_hbm, u_hbm) = refs[11:17]
    (o_res, o_tok, l_mlp, l_rec, l_sh, l_gate, l_small) = refs[17:24]
    (rec, ub, rg, part, sib1, got1, sib2, got2, low, grec, gsh, gshin, g_own, y_mlp, y_rec, y_sh, a_scr, c_scr,
     gg, vg, ggl, y_gate, sml, sml_sib, y_sml) = refs[24:49]
    sems = refs[49:]
    zh, zl, y, x, c = place()
    here = (zh, zl, y, x)
    q, me = zl * 2 + x, dp_at(zh, zl, y, x)
    high = n // 8
    there = plane(zh, zl, y, x, high)
    half, width = tok.shape
    length = 2 * half
    blk = mixed.shape[2]
    rr = width // n
    rb = blk // n
    nt = y_mlp.shape[0]
    per, steps = blk // rr, width // blk
    taken = [0]

    def some(k):
        taken[0] += k
        return sems[taken[0] - k : taken[0]]

    rows = Rows(rg, some(4), here, c)
    sums1 = Sums(part, sib1, got1, some(4), rows)
    sums2 = Sums(part, sib2, got2, some(4), rows)
    (loads,) = some(1)
    greet(
        [dev(dp_at(h, z, y, w), c) for h, z, w in there[1:]]
        + [dev(dp_at(zh, zl, 1 - y, x), c), dev(me, 1 - c)]
    )
    first = pltpu.make_async_copy(rec_own, rg.at[q, c], loads.at[0])
    first.start()
    first.wait()
    rows.start()
    grab = [
        pltpu.make_async_copy(rec_hbm, rec, loads.at[0]),
        pltpu.make_async_copy(u_hbm, ub, loads.at[1]),
    ]
    for cp in grab:
        cp.start()

    def own_part(i):
        return pltpu.make_async_copy(g_hbm.at[i, :, y], g_own.at[i % 2], loads.at[2 + i % 2])

    own_part(0).start()

    def reduce_chunk(i):
        own_part(i).wait()
        if i + 1 < nt:
            own_part(i + 1).start()
        mlps[i].pass_on()

    def chunk(i, sem):
        return Scatter(
            lambda s: g_hbm.at[i, s // 4, (s // 2) % 2, s % 2],
            lambda s: g_own[i % 2, s // 4, s % 2],
            lambda j: y_mlp.at[i, j],
            lambda j: l_mlp.at[i, j],
            sem, here, there, c,
        )

    mlps = [chunk(i, some(4)) for i in range(nt)]
    for a in mlps:
        a.start()
    recs = [
        Scatter(
            lambda s, i=i: grec.at[i, s],
            lambda s, i=i: grec[i, s],
            lambda j, i=i: y_rec.at[i, j],
            lambda j, i=i: l_rec.at[i, j],
            some(4), here, there, c,
        )
        for i in range(3)
    ]
    part_rows = rr // 2

    def region(ref, h):
        return ref.at[:, :, pl.ds(pl.multiple_of(h * part_rows, 8), part_rows), :]

    shared = Scatter(
        lambda s: gshin.at[:, s],
        lambda s: gshin[:, s],
        lambda j: y_sh.at[j],
        lambda j: l_sh.at[j],
        some(4), here, there, c,
    )
    gate_sc = Scatter(
        lambda s: ggl.at[:, s],
        lambda s: ggl[:, s],
        lambda j: y_gate.at[j],
        lambda j: l_gate.at[j],
        some(4), here, there, c,
    )
    h_send, h_recv, s_send, s_recv, z_send, z_recv, m_send, m_recv = some(8)
    gg[...] = jnp.zeros_like(gg)
    vg[...] = jnp.zeros_like(vg)
    grab[0].wait()

    def step(i, carry):
        h = jnp.where(i == 1, 1, 0)
        k = jnp.maximum(i - 1, 0)
        pq, _ = rows.at(k)
        at = pq + h * (4 - pq)

        @pl.when(i != 1)
        def _():
            rows.arrive(k)

        mg = mm(rg[pq].reshape(length, width), rec[h, 2].reshape(width, blk))

        @pl.when((i > 0) & (i < 4))
        def _():
            rows.forward(k + 1)

        b_low, i_low, g_add, v_add = rec_unit_back(
            taps, pre[at, :, :blk], pre[at, :, blk:], vec[h], gates[h], ends[pq][0:1, :], state[at], mg, c_scr, a_scr,
        )
        low[at, :, :blk], low[at, :, blk:] = b_low, i_low
        gg[h] += g_add
        vg[h] += v_add

        @pl.when(i > 2)
        def _():
            sums1.pass_on(k - 1)

        def cols_out(t, carry):
            cut = pl.ds(t * per, per)
            lanes = pl.ds(pl.multiple_of(t * blk, 128), blk)

            def tile_of(left, head):
                return sum(
                    mm_t(left[:, j * blk : (j + 1) * blk], rec[head, j, cut].reshape(blk, blk)) for j in range(2)
                )

            def emit(tile):
                part[pq, 0, :, lanes] = tile[:half].astype(BF)
                part[pq, 1, :, lanes] = tile[half:].astype(BF)

            @pl.when(i == 1)
            def _():
                emit(tile_of(low[4], 1) + tile_of(low[pq], 0))

            @pl.when(i > 1)
            def _():
                emit(tile_of(low[pq], 0))

            return carry

        @pl.when(i > 0)
        def _():
            lax.fori_loop(0, steps, cols_out, 0)

        @pl.when(i > 0)
        def _():
            sums1.push(k)

        for j in range(5):

            @pl.when(i == j)
            def _():
                reduce_chunk(j)

        return carry

    lax.fori_loop(0, 5, step, 0)
    sums1.pass_on(3)
    grab[1].wait()

    def grads(d, carry):
        lanes = pl.ds(pl.multiple_of(d * blk, 128), blk)
        at = pl.ds(d * per, per)
        ut = ub[:, :, :, lanes].reshape(4 * length, blk).T
        rt = rg[:, :, :, lanes].reshape(4 * length, blk).T
        uo = ub[q, :, :, lanes].reshape(length, blk).T
        ro = rg[q, :, :, lanes].reshape(length, blk).T
        for i in range(3):
            if i < 2:
                right = low[0:4, :, i * blk : (i + 1) * blk].reshape(4 * length, blk)
                own = low[4, :, i * blk : (i + 1) * blk]
            else:
                right, own = mixed[0:4].reshape(4 * length, blk), mixed[4]
            grec[i, at] = mm(ut if i < 2 else rt, right).astype(BF).reshape(per, rr, blk)
            gsh[i, at] = mm(uo if i < 2 else ro, own).astype(BF).reshape(per, rr, blk)
        return carry

    lax.fori_loop(0, steps, grads, 0)
    _, beside = rows.at(1)
    exchange = remote(region(gsh, 1 - x), gshin, h_send, h_recv, beside)
    exchange.start()
    for a in recs:
        a.start()
    for h in range(2):
        for s in range(n):
            ggl[h, s] = gg[h, s * rb : (s + 1) * rb, :].astype(BF)
    gate_sc.start()

    sums1.ready()

    def finish(i, acc):
        at = pl.ds(pl.multiple_of(i * 32, 32), 32)
        total, xin = sums1.own(at), tok[at, :].astype(F32)
        scale = lax.rsqrt(jnp.mean(xin * xin, axis=-1, keepdims=True) + EPS)
        unit = xin * scale
        g1 = total * gain[0:1, :]
        o_tok[at, :] = rgrad[at, :] + scale * (g1 - unit * jnp.mean(g1 * unit, axis=-1, keepdims=True))
        return acc + jnp.sum(total * unit, axis=0, keepdims=True)

    gsum1 = lax.fori_loop(0, half // 32, finish, jnp.zeros((1, width), F32))
    sums1.finish()
    for h in range(2):
        sml[8 * h : 8 * h + 8, :] = vg[h]
    for i in range(steps):
        sml[16 + i : 17 + i, :] = gsum1[:, i * blk : (i + 1) * blk]
        sml[16 + steps + i : 17 + steps + i, :] = gsum2[0:1, i * blk : (i + 1) * blk]
    gain_rows = sml.at[pl.ds(16, 2 * steps)]
    with_sib = remote(gain_rows, sml_sib, s_send, s_recv, rows.sib)
    with_sib.start()
    reduce_chunk(5)
    exchange.wait()
    for s in range(n):
        gshin[:, s] = (
            gshin[:, s].astype(F32)
            + gsh[:, s, pl.ds(pl.multiple_of(x * part_rows, 8), part_rows), :].astype(F32)
        ).astype(BF)
    shared.start()
    reduce_chunk(6)
    with_sib.wait()
    sml[16 : 16 + 2 * steps, :] += sml_sib[...]
    with_y = remote(sml, y_sml, z_send, z_recv, dev(dp_at(zh, zl, 1 - y, x), c))
    with_y.start()

    fetch = pltpu.make_async_copy(mlp_hbm.at[pl.ds(2 * (nt // 3), nt // 3)], rec.at[0], loads.at[0])
    fetch.start()
    per_row = length // rr
    fetch_hid = pltpu.make_async_copy(hid, gsh.at[:, pl.ds(0, 4 * per_row)], loads.at[1])
    fetch_hid.start()
    reduce_chunk(7)
    fetch.wait()
    fetch_hid.wait()

    def out_rows(i, carry):
        k = (i + 1) % 4
        pq, _ = rows.at(k)

        def cols_out(d, carry):
            tile = jnp.zeros((length, blk), F32)
            for t in range(nt // 3):
                left = gsh[t, pl.ds(pq * per_row, per_row)].reshape(length, blk)
                tile = tile + mm_t(left, rec[0, t, pl.ds(d * per, per)].reshape(blk, blk))
            lanes = pl.ds(pl.multiple_of(d * blk, 128), blk)
            part[pq, 0, :, lanes] = tile[:half].astype(BF)
            part[pq, 1, :, lanes] = tile[half:].astype(BF)
            return carry

        lax.fori_loop(0, steps, cols_out, 0)
        sums2.push(k)

        @pl.when(i > 0)
        def _():
            sums2.pass_on(i)

        return carry

    lax.fori_loop(0, 4, out_rows, 0)
    reduce_chunk(8)
    with_y.wait()
    sml[...] = sml[...] + y_sml[...]
    mine = zh * 4 + q
    small_out = []
    for i, (h, z, w) in enumerate(there):
        if i == 0:
            cp = pltpu.make_async_copy(sml, l_small.at[mine], m_send.at[i])
        else:
            cp = remote(sml, l_small.at[mine], m_send.at[i], m_recv.at[mine], dev(dp_at(h, z, y, w), c))
        cp.start()
        small_out.append(cp)
    for a in recs:
        a.pass_on()
    gate_sc.pass_on()
    shared.pass_on()
    sums2.ready()
    e3 = ends[q][0:1, 3:4]

    def result(i, carry):
        at = pl.ds(pl.multiple_of(i * 32, 32), 32)
        spot = lax.broadcasted_iota(jnp.int32, (32, 1), 0) + (c * half + i * 32)
        o_res[at, :] = jnp.where(spot.astype(F32) < e3, resid[at, :] + sums2.own(at), 0.0).astype(BF)
        return carry

    lax.fori_loop(0, half // 32, result, 0)
    sums2.finish()
    rows.finish()
    for a in mlps + recs + [gate_sc, shared]:
        a.collect()
    for i, (h, z, w) in enumerate(there):
        if i == 0:
            small_out[i].wait()
        else:
            j = h * 4 + z * 2 + w
            land = l_small.at[j]
            remote(land, land, m_send.at[i], m_recv.at[j], rows.sib).wait_recv()
            small_out[i].wait_send()


def backward(tok, rec_own, rgrad, resid, gain, gsum2, ends, vec, gates, saved, hid, g_mlp, rec_w, mlp_w, u, n, taps, cid):
    half, width = tok.shape
    pre, state, mixed = saved
    blk = mixed.shape[2]
    length = 2 * half
    rr, rb, high = width // n, blk // n, n // 8
    nt = g_mlp.shape[0]
    slots = high * 4
    vm = pl.BlockSpec(memory_space=pltpu.VMEM)
    hb = pl.BlockSpec(memory_space=pl.ANY)
    g_view = g_mlp.reshape(nt, n // 4, 2, 2, rr, blk)
    hid = hid.reshape(nt // 3, 4 * length // rr, rr, blk)
    small_rows = 16 + 2 * (width // blk)

    def sds(*shape, t=BF):
        return jax.ShapeDtypeStruct(shape, t)

    def v(*shape, t=BF):
        return pltpu.VMEM(shape, t)

    dma = pltpu.SemaphoreType.DMA
    return pl.pallas_call(
        functools.partial(backward_kernel, n, taps),
        out_shape=(
            sds(half, width),
            sds(half, width, t=F32),
            sds(nt, slots, rr, blk),
            sds(3, slots, rr, blk),
            sds(slots, 3, rr // 2, blk),
            sds(slots, 2, rb, 2 * blk),
            sds(slots, small_rows, blk, t=F32),
        ),
        in_specs=[vm] * 11 + [hb] * 6,
        out_specs=[vm, vm] + [hb] * 5,
        scratch_shapes=[
            v(2, 3, n, rr, blk),
            v(4, 2, half, width),
            v(4, 2, half, width),
            v(4, 2, half, width),
            v(4, half, width),
            v(4, half, width),
            v(4, half, width),
            v(4, half, width),
            v(5, length, 2 * blk),
            v(3, n, rr, blk),
            v(3, n, rr, blk),
            v(3, n, rr // 2, blk),
            v(2, n // 4, 2, rr, blk),
            v(nt, slots, rr, blk),
            v(3, slots, rr, blk),
            v(slots, 3, rr // 2, blk),
            v(length, blk, t=F32),
            v(length, blk, t=F32),
            v(2, blk, 2 * blk, t=F32),
            v(2, 4 + taps, blk, t=F32),
            v(2, n, rb, 2 * blk),
            v(slots, 2, rb, 2 * blk),
            v(small_rows, blk, t=F32),
            v(small_rows - 16, blk, t=F32),
            v(small_rows, blk, t=F32),
        ]
        + row_sems() * 3
        + [dma((4,))]
        + scatter_sems(high) * (nt + 5)
        + [dma, dma, dma, dma, dma, dma, dma((slots,)), dma((slots,))],
        compiler_params=pltpu.CompilerParams(
            collective_id=cid, has_side_effects=True, vmem_limit_bytes=VMEM_LIMIT
        ),
        name="backward",
    )(tok, rgrad, resid, gain, gsum2, ends, vec, gates, *saved, rec_own, hid, g_view, rec_w, mlp_w, u)


def mm(a, b):
    return jnp.dot(a, b, preferred_element_type=F32)


def mm_t(a, b):
    return lax.dot_general(a, b, (((1,), (1,)), ((), ())), preferred_element_type=F32)


def t_mm(a, b):
    return lax.dot_general(a, b, (((0,), (0,)), ((), ())), preferred_element_type=F32)


def local(
    tokens, doc_lengths, rec_gain, w_branch, w_input, w_rgate, w_igate, rgate_bias, igate_bias,
    decay_param, conv_weight, conv_bias, w_output, mlp_gain, w_gate, w_up, w_down, cotangent,
):
    n = lax.axis_size("dp")
    zh, zl, y, x, c = place()
    q = zl * 2 + x
    _, half, width = tokens.shape
    length = half * 2
    heads, rb, blk = w_rgate.shape
    taps = conv_weight.shape[0]
    rows = w_branch.shape[0]
    ff = w_gate.shape[1] // 4

    dp = lax.axis_index("dp")

    def lanes(v, per):
        v = v.astype(BF).reshape(-1, per)
        at = (dp * per) % 128
        return lax.dynamic_update_slice(jnp.zeros((v.shape[0], 128), BF), v, (0, at))

    params = jnp.concatenate(
        [rgate_bias[:, None], igate_bias[:, None], decay_param[:, None], conv_weight.transpose(1, 0, 2), conv_bias[:, None]],
        axis=1,
    )
    params = jnp.pad(params, ((0, 0), (0, 16 - params.shape[1]), (0, 0))).reshape(heads * 16, rb)
    lens = doc_lengths.reshape(4).astype(F32)
    e0 = lens[0]
    e1 = e0 + lens[1]
    e2 = e1 + lens[2]
    e3 = e2 + lens[3]
    ends_own = jnp.pad(jnp.stack([e0, e1, e2, e3]).astype(BF)[None], ((0, 13), (0, 124)))
    small = jnp.concatenate([lanes(params, rb), lanes(jnp.stack([rec_gain, mlp_gain]), rows), ends_own], axis=0)
    (
        rec_w, mlp_w, gates, vec, gains_all, group_ends, u, mlp_grad, pre, state, mixed, resid, norm_own,
    ) = forward(
        tokens[0], cotangent[0], w_branch, w_input, w_output.T, w_gate, w_up, w_down.T, w_rgate, w_igate, small, n, taps, 1,
    )
    g_mlp, rec_own, resid_grad, hid, gain2_sum = mlp_block(
        norm_own, resid, gains_all, cotangent[0], group_ends, mlp_w, mlp_grad, 4
    )
    result, token_grad, l_mlp, l_rec, l_sh, l_gate, l_small = backward(
        tokens[0], rec_own, resid_grad, resid, gains_all, gain2_sum, group_ends, vec, gates,
        (pre, state, mixed), hid, g_mlp, rec_w, mlp_w, u, n, taps, 5,
    )
    high = n // 8

    def owned(a):
        return jnp.sum(a.reshape((high, 4) + a.shape[1:]).astype(F32), axis=0)

    tiles = ff // blk
    o_mlp = jnp.sum(l_mlp.reshape(3, tiles, high, 4, rows, blk).astype(F32), axis=2)
    o_mlp = o_mlp.transpose(0, 3, 2, 1, 4).reshape(3, rows, 4 * ff)
    o_q = jnp.sum(l_rec.reshape(3, high, 4, rows, blk).astype(F32), axis=1)
    o_sh = jnp.sum(l_sh.reshape(high * 2, 2, 3, rows // 2, blk).astype(F32), axis=0)
    o_sh = o_sh.transpose(1, 0, 2, 3).reshape(3, 1, rows, blk)
    o_rec = jnp.concatenate([o_q, o_sh], axis=1).transpose(0, 2, 1, 3).reshape(3, rows, heads * blk)
    o_gate = owned(l_gate)
    o_gate = jnp.concatenate([o_gate[:, 0], jnp.sum(o_gate[:, 1], axis=0, keepdims=True)], axis=0)
    o_small = owned(l_small)
    at = dp * rb
    o_vec = jnp.concatenate([o_small[:, :8], jnp.sum(o_small[:, 8:16], axis=0, keepdims=True)], axis=0)
    o_vec = lax.dynamic_slice_in_dim(o_vec, at, rb, 2)
    o_gain = jnp.sum(o_small[:, 16:], axis=0).reshape(2, width)
    o_gain = lax.dynamic_slice_in_dim(o_gain, dp * rows, rows, 1)
    return (
        result[None],
        token_grad[None],
        o_gain[0],
        o_rec[0],
        o_rec[1],
        o_gate[:, :, :blk],
        o_gate[:, :, blk:],
        o_vec[:, 0],
        o_vec[:, 1],
        o_vec[:, 2],
        o_vec[:, 4 : 4 + taps].transpose(1, 0, 2),
        o_vec[:, 3],
        o_rec[2].T,
        o_gain[1],
        o_mlp[0],
        o_mlp[1],
        o_mlp[2].T,
    )


def solution(mesh):
    return jax.shard_map(
        local,
        mesh=mesh,
        in_specs=(
            P("dp", "tensor", None),
            P("dp", None),
            P("dp"),
            P("dp", "tensor"),
            P("dp", "tensor"),
            P("tensor", "dp", None),
            P("tensor", "dp", None),
            P("tensor", "dp"),
            P("tensor", "dp"),
            P("tensor", "dp"),
            P(None, "tensor", "dp"),
            P("tensor", "dp"),
            P("tensor", "dp"),
            P("dp"),
            P("dp", "tensor"),
            P("dp", "tensor"),
            P("tensor", "dp"),
            P("dp", "tensor", None),
        ),
        out_specs=(
            P("dp", "tensor", None),
            P("dp", "tensor", None),
            P("dp"),
            P("dp", "tensor"),
            P("dp", "tensor"),
            P("tensor", "dp", None),
            P("tensor", "dp", None),
            P("tensor", "dp"),
            P("tensor", "dp"),
            P("tensor", "dp"),
            P(None, "tensor", "dp"),
            P("tensor", "dp"),
            P("tensor", "dp"),
            P("dp"),
            P("dp", "tensor"),
            P("dp", "tensor"),
            P("tensor", "dp"),
        ),
        check_vma=False,
    )
```

```python
import functools

import jax
import jax.numpy as jnp
from jax import lax
from jax.experimental import pallas as pl
from jax.experimental.pallas import tpu as pltpu
from jax.sharding import PartitionSpec as P

MESH = pl.DeviceIdType.MESH
BF = jnp.bfloat16
F32 = jnp.float32
EPS = 1e-06
DECAY = 8.0
GC = 0.7978845608028654
GK = 0.044715
VMEM_LIMIT = 62 * 1024 * 1024


def dp_at(zh, zl, y, x):
    return ((zh * 2 + zl) * 2 + y) * 2 + x


def place():
    dp = lax.axis_index("dp")
    return dp // 8, (dp // 4) % 2, (dp // 2) % 2, dp % 2, lax.axis_index("tensor")


def dev(dp, core):
    return {"dp": dp, "tensor": core}


def greet(devices):
    sem = pltpu.get_barrier_semaphore()
    for d in devices:
        pl.semaphore_signal(sem, inc=1, device_id=d, device_id_type=MESH)
    pl.semaphore_wait(sem, len(devices))


def remote(src, dst, ssem, rsem, d):
    return pltpu.make_async_remote_copy(
        src_ref=src, dst_ref=dst, send_sem=ssem, recv_sem=rsem, device_id=d, device_id_type=MESH
    )


def plane(zh, zl, y, x, high):
    out = []
    for kh in range(high):
        for kl in range(2):
            for kx in range(2):
                ph, pz, px = (zh + kh) % high, (zl + kl) % 2, (x + kx) % 2
                out.append((ph, pz, px))
    return out


def gelu_parts(v):
    t = jnp.tanh(GC * (v + GK * v * v * v))
    act = 0.5 * v * (1.0 + t)
    der = 0.5 * (1.0 + t) + 0.5 * v * (1.0 - t * t) * GC * (1.0 + 3.0 * GK * v * v)
    return act, der


def segments(ends, length, width, taps):
    t = lax.broadcasted_iota(jnp.int32, (length, width), 0).astype(F32)

    def seg(at):
        total = jnp.zeros((length, width), F32)
        for j in range(4):
            total = total + jnp.where(at >= ends[:, j : j + 1], 1.0, 0.0)
        return total

    here = seg(t)
    same = []
    for k in range(1, taps):
        same.append(jnp.where((t >= float(k)) & (seg(t - float(k)) == here), 1.0, 0.0))
    return same


def scan8(a, b, reverse):
    length, width = a.shape
    row = lax.broadcasted_iota(jnp.int32, (length, width), 0) % 8
    for d in (1, 2, 4):
        if reverse:
            ash, bsh = pltpu.roll(a, length - d, 0), pltpu.roll(b, length - d, 0)
            ok = row < 8 - d
        else:
            ash, bsh = pltpu.roll(a, d, 0), pltpu.roll(b, d, 0)
            ok = row >= d
        b = b + a * jnp.where(ok, bsh, 0.0)
        a = a * jnp.where(ok, ash, 1.0)
    return a, b


def full_scan(a, b, out_ref, a_ref, reverse):
    length, width = a.shape
    a8, b8 = scan8(a, b, reverse)
    a_ref[...] = a8
    out_ref[...] = b8
    blocks = length // 8

    def step(i, carry):
        at = (blocks - 1 - i if reverse else i) * 8
        at = pl.multiple_of(at, 8)
        now = out_ref[pl.ds(at, 8), :] + a_ref[pl.ds(at, 8), :] * carry
        out_ref[pl.ds(at, 8), :] = now
        return now[0:1, :] if reverse else now[7:8, :]

    lax.fori_loop(0, blocks, step, jnp.zeros((1, width), F32))


class Gather:
    def __init__(self, slot, parts, sems, here, there, core):
        self.slot, self.parts, (self.send, self.recv, self.fsend) = slot, parts, sems
        zh, zl, y, x = here
        self.q = zl * 2 + x
        self.me = dp_at(zh, zl, y, x)
        self.near = [dp_at(h, z, y, w) for h, z, w in there]
        self.far = [dp_at(h, z, 1 - y, w) for h, z, w in there]
        self.pick = [z * 2 + w for _, z, w in there]
        self.core = core
        self.other = dev(dp_at(zh, zl, 1 - y, x), core)

    def ks(self, far):
        count = len(self.near)
        return range(4, count) if far else range(4)

    def start(self, far):
        for k in self.ks(far):
            for piece, part in self.parts:
                src = piece(self.pick[k])
                dst = part(self.slot(self.me, self.pick[k]))
                if k == 0:
                    pltpu.make_async_copy(src, dst, self.send.at[0]).start()
                else:
                    d = dev(self.near[k], self.core)
                    remote(src, dst, self.send.at[k], self.recv.at[self.me], d).start()

    def forward(self, k):
        land = self.slot(self.near[k], self.q)
        if k == 0:
            pltpu.make_async_copy(land, land, self.send.at[0]).wait()
        else:
            remote(land, land, self.send.at[k], self.recv.at[self.near[k]], self.other).wait_recv()
        remote(land, land, self.fsend.at[k], self.recv.at[self.near[k]], self.other).start()

    def forward_all(self, far):
        for k in self.ks(far):
            self.forward(k)

    def arrive_all(self):
        for k in range(len(self.far)):
            land = self.slot(self.far[k], self.q)
            remote(land, land, self.fsend.at[k], self.recv.at[self.far[k]], self.other).wait_recv()

    def finish(self):
        for k in range(len(self.near)):
            land = self.slot(self.near[k], self.q)
            remote(land, land, self.fsend.at[k], self.recv.at[self.near[k]], self.other).wait_send()
            if k:
                remote(land, land, self.send.at[k], self.recv.at[self.near[k]], self.other).wait_send()


class Rows:
    def __init__(self, buf, sems, here, core):
        self.buf, (self.send, self.recv, self.fsend, self.frecv) = buf, sems
        self.here, self.core = here, core
        zh, zl, y, x = here
        self.q = zl * 2 + x
        self.sib = dev(dp_at(zh, zl, y, x), 1 - core)

    def at(self, k):
        zh, zl, y, x = self.here
        pz, px = (zl + k // 2) % 2, (x + k % 2) % 2
        return pz * 2 + px, dev(dp_at(zh, pz, y, px), self.core)

    def start(self, piece=0, pieces=1):
        per = self.buf.shape[2] // pieces
        own = self.buf.at[self.q, self.core, pl.ds(piece * per, per)]
        for k in (1, 2):
            _, d = self.at(k)
            remote(own, own, self.send.at[k], self.recv.at[self.q], d).start()
        remote(own, own, self.fsend.at[0], self.frecv.at[self.q], self.sib).start()

    def forward(self, k):
        pq, d = self.at(k)
        land = self.buf.at[pq, self.core]
        remote(land, land, self.send.at[k], self.recv.at[pq], d).wait_recv()

        def relay():
            _, beside = self.at(1)
            remote(land, land, self.send.at[3], self.recv.at[pq], beside).start()

        if isinstance(k, int):
            if k == 2:
                relay()
        else:
            pl.when(k == 2)(relay)
        remote(land, land, self.fsend.at[k], self.frecv.at[pq], self.sib).start()

    def arrive(self, k):
        pq, _ = self.at(k)
        land = self.buf.at[pq, 1 - self.core]
        remote(land, land, self.fsend.at[k], self.frecv.at[pq], self.sib).wait_recv()

    def finish(self):
        own = self.buf.at[self.q, self.core]
        for k in range(4):
            remote(own, own, self.fsend.at[k], self.frecv.at[self.q], self.sib).wait_send()
            if k:
                remote(own, own, self.send.at[k], self.recv.at[self.q], self.sib).wait_send()


def row_sems():
    return [pltpu.SemaphoreType.DMA((4,))] * 4


class Sums:
    def __init__(self, part, sib, got, sems, rows):
        self.part, self.sib_buf, self.got = part, sib, got
        self.ssend, self.srecv, self.send, self.recv = sems
        self.rows = rows

    def push(self, k):
        r = self.rows
        pq, _ = r.at(k)
        remote(
            self.part.at[pq, 1 - r.core], self.sib_buf.at[pq], self.ssend.at[k], self.srecv.at[pq], r.sib
        ).start()

    def pair(self, k):
        r = self.rows
        pq, _ = r.at(k)
        land = self.sib_buf.at[pq]
        remote(land, land, self.ssend.at[k], self.srecv.at[pq], r.sib).wait_recv()
        return self.part[pq, r.core].astype(F32) + self.sib_buf[pq].astype(F32)

    def pass_on(self, k):
        r = self.rows
        pq, d = r.at(k)
        self.part[pq, r.core] = self.pair(k).astype(BF)
        remote(self.part.at[pq, r.core], self.got.at[r.q], self.send.at[k], self.recv.at[r.q], d).start()

    def take(self, k):
        r = self.rows
        pq, _ = r.at(k)
        land = self.got.at[pq]
        remote(land, land, self.send.at[k], self.recv.at[pq], r.sib).wait_recv()
        return self.got[pq].astype(F32)

    def ready(self):
        r = self.rows
        land = self.sib_buf.at[r.q]
        remote(land, land, self.ssend.at[0], self.srecv.at[r.q], r.sib).wait_recv()
        for k in (1, 2, 3):
            pq, _ = r.at(k)
            land = self.got.at[pq]
            remote(land, land, self.send.at[k], self.recv.at[pq], r.sib).wait_recv()

    def own(self, at):
        r = self.rows
        total = self.part[r.q, r.core, at].astype(F32) + self.sib_buf[r.q, at].astype(F32)
        for k in (1, 2, 3):
            total = total + self.got[r.at(k)[0], at].astype(F32)
        return total

    def finish(self):
        r = self.rows
        land = self.got.at[r.q]
        for k in range(4):
            remote(land, land, self.ssend.at[k], self.srecv.at[r.q], r.sib).wait_send()
            if k:
                remote(land, land, self.send.at[k], self.recv.at[r.q], r.sib).wait_send()


def rec_unit(taps, branch, conv_in, vec, gates, ends, state_ref, a_ref):
    same, conv, r, gate = rec_gates(taps, conv_in, vec, gates, ends)
    log_a = (-DECAY * r) * vec[2:3]
    a = jnp.exp(log_a)
    start = same[0] == 0.0
    a_eff = jnp.where(start, 0.0, a)
    mult = jnp.where(start, 1.0, jnp.sqrt(-jnp.tanh(log_a) * (1.0 + a * a)))
    full_scan(a_eff, mult * gate * conv, state_ref, a_ref, False)
    act, _ = gelu_parts(branch)
    return (state_ref[...] * act).astype(BF)


SMALL_ROWS = 96


def forward_kernel(n, taps, heads, *refs):
    (tok, cot, wb, wi, wo, wg, wu, wd, wr, wig, small) = refs[:11]
    (o_rec, o_mlp, o_gate, o_vec, o_gain, o_ends, o_u, o_grad, pre, state, mixed, resid, o_norm) = refs[11:24]
    (rec, gat, sml, u_buf, og, part, sibb, got, extra, a_scr, gfull) = refs[24:35]
    sems = refs[35:]
    g_sems, r1, r2, s1, (fin, h_send, h_recv) = sems[:48], sems[48:52], sems[52:56], sems[56:60], sems[60:]
    zh, zl, y, x, c = place()
    here = (zh, zl, y, x)
    q, me = zl * 2 + x, dp_at(zh, zl, y, x)
    high = n // 8
    there = plane(zh, zl, y, x, high)
    half, width = tok.shape
    length, blk = pre.shape[1], pre.shape[2] // 2
    ff = wg.shape[1] // 4
    rb, rr = wr.shape[1], wb.shape[0]
    greet(
        [dev(dp_at(h, z, y, w), c) for h, z, w in there[1:]]
        + [dev(dp_at(zh, zl, 1 - y, x), c), dev(me, 1 - c)]
    )

    def whole(ref):
        return ref

    def head_cols(ref):
        return lambda p: ref.at[:, pl.ds(pl.multiple_of(p * blk, 128), blk)]

    def make(i, slot, parts):
        return Gather(slot, parts, g_sems[3 * i : 3 * i + 3], here, there, c)

    smalls = make(0, lambda s, g: sml.at[s], [(lambda p: small, whole)])
    gats, recs, mlps = [], [], []
    for h in range(2):
        pick = (lambda ref: lambda p: ref.at[p]) if h == 0 else (lambda ref: lambda p: ref.at[heads - 1])
        gats.append(
            make(
                1 + h,
                lambda s, g, h=h: gat.at[h, s],
                [
                    (pick(w), lambda r, i=i: r.at[:, pl.ds(i * blk, blk)])
                    for i, w in enumerate((wr, wig))
                ],
            )
        )
    for i, w in enumerate((wb, wi, wo)):
        recs.append(make(3 + i, lambda s, g, i=i: rec.at[0, i, s], [(head_cols(w), whole)]))
    part_rows = rr // 2

    def shared_piece(ref):
        return lambda p: ref.at[
            pl.ds(pl.multiple_of((p % 2) * part_rows, 8), part_rows), pl.ds((heads - 1) * blk, blk)
        ]

    def shared_rows(s, g):
        return rec.at[1, :, s, pl.ds(pl.multiple_of((g % 2) * part_rows, 8), part_rows), :]

    shared = make(
        6, shared_rows, [(shared_piece(w), lambda r, i=i: r.at[i]) for i, w in enumerate((wb, wi, wo))]
    )
    for i, w in enumerate((wg, wu, wd)):
        for t in range(ff // blk):
            piece = lambda p, w=w, t=t: w.at[:, pl.ds(pl.multiple_of(p * ff + t * blk, 128), blk)]
            j = i * (ff // blk) + t
            mlps.append(make(7 + j, lambda s, g, j=j: o_mlp.at[j, s], [(piece, whole)]))
    count = len(there)
    order = [recs[0], gats[0], recs[1], gats[1], shared, recs[2]] + mlps
    ahead = 2

    def pump(j):
        if j + ahead < len(order):
            order[j + ahead].forward_all(False)
        order[j].forward_all(True)
        for _ in range(2 if j < 4 else 1):
            if trickle:
                trickle.pop(0)()
        if j + ahead < len(order):
            order[j + ahead].start(True)
        if j + 2 * ahead < len(order):
            order[j + 2 * ahead].start(False)

    smalls.start(True)
    smalls.start(False)
    for j in range(2 * ahead):
        if j < ahead:
            order[j].start(True)
        order[j].start(False)

    xin = tok[...].astype(F32)
    unit = xin * lax.rsqrt(jnp.mean(xin * xin, axis=-1, keepdims=True) + EPS)
    resid[...] = unit
    smalls.forward_all(False)
    smalls.forward_all(True)
    for j in range(ahead):
        order[j].forward_all(False)
    smalls.arrive_all()
    per_vec, per_gain = blk // 128, width // 128
    base = (heads - 1) * 16
    for h in range(2):
        at = pl.multiple_of(q * 16, 16) if h == 0 else base
        groups = [jnp.zeros((16, 128), F32)] * per_vec
        for s in range(n):
            g = s * rb // 128
            groups[g] = groups[g] + sml[s, pl.ds(at, 16), :].astype(F32)
        raw = jnp.concatenate(groups, axis=1)
        decay = raw[2:3]
        o_vec[h, 0:2, :] = raw[0:2]
        o_vec[h, 2:3, :] = jnp.log1p(jnp.exp(-decay))
        o_vec[h, 3:4, :] = jax.nn.sigmoid(-decay)
        o_vec[h, 4 : 5 + taps, :] = raw[3 : 4 + taps]
    groups = [None] * per_gain
    for s in range(n):
        g = s * rr // 128
        v = sml[s, SMALL_ROWS - 16 : SMALL_ROWS, :].astype(F32)
        groups[g] = v if groups[g] is None else groups[g] + v
    for g in range(per_gain):
        o_gain[:, g * 128 : (g + 1) * 128] = groups[g][0:8]
    for j in range(4):
        v = sml[dp_at(zh, j // 2, y, j % 2), SMALL_ROWS - 16 : SMALL_ROWS, :].astype(F32)
        o_ends[j] = jnp.broadcast_to(v[2:3], (8, 128))
    u_rows = Rows(u_buf, r1, here, c)
    g_rows = Rows(o_grad, r2, here, c)
    u_buf[q, c] = (resid[...] * o_gain[0:1, :]).astype(BF)
    trickle = [functools.partial(r.start, p, 8) for r in (u_rows, g_rows) for p in range(8)]
    e3 = o_ends[q][0:1, 3:4]
    spot = lax.broadcasted_iota(jnp.int32, (half, 1), 0).astype(F32) + (c * half).astype(F32)
    og[...] = jnp.where(spot < e3, cot[...], 0.0).astype(BF)
    own_grad = o_grad.at[q, c]
    place_grad = pltpu.make_async_copy(og, own_grad, fin.at[0])
    place_grad.start()
    place_grad.wait()
    for j in range(5):
        pump(j)
    for k in (1, 2):
        u_rows.forward(k)
    pump(5)
    u_rows.forward(3)

    _, beside = u_rows.at(1)

    def exchange(g, first, many):
        rows = rec.at[
            1, :, pl.ds(first, many), pl.ds(pl.multiple_of((g % 2) * part_rows, 8), part_rows), :
        ]
        return remote(rows, rows, h_send, h_recv, beside)

    shared.arrive_all()
    eighth = n // 8
    for p in range(4):
        exchange(q, p * eighth, eighth).start()
    trickle[:0] = [exchange(q, p * eighth, eighth).start for p in range(4, 8)]
    for a in gats + recs:
        a.arrive_all()
    for h in range(2):
        if rb % 16 == 0:
            o_gate[h] = gat[h].reshape(blk, 2 * blk)
        else:
            for s in range(n):
                gfull[s * rb : (s + 1) * rb, :] = gat[h, s].astype(F32)
            o_gate[h] = gfull[...].astype(BF)
    for k in range(4):
        u_rows.arrive(k)
    keep = [pltpu.make_async_copy(rec, o_rec, fin.at[1]), pltpu.make_async_copy(u_buf, o_u, fin.at[2])]
    keep[1].start()

    sums = Sums(part, sibb, got, s1, u_rows)

    def step(i, carry):
        h = i // 4
        k = ((i + 1) % 4) * ((7 - i) // 4)
        pq, _ = u_rows.at(k)
        at = pq + h * (4 - pq)

        @pl.when(i == 4)
        def _():
            exchange(q + 1, 0, n).wait_recv()
            keep[0].start()

        rows = u_buf[pq].reshape(2 * half, width)
        for j in range(2):
            w = rec[h, j].reshape(width, blk)
            pre[at, :, j * blk : (j + 1) * blk] = mm(rows, w)
        mx = rec_unit(
            taps, pre[at, :, :blk], pre[at, :, blk:], o_vec[h], o_gate[h], o_ends[pq][0:1, :], state.at[at], a_scr
        )
        mixed[at] = mx
        per = 512 // rr if rr <= 512 else 1

        def cols_out(t, carry):
            w = rec[h, 2, pl.ds(t * per, per)].reshape(per * rr, blk)
            tile = mm_t(mx, w)
            lanes = pl.ds(pl.multiple_of(t * (per * rr), 128), per * rr)
            tile = tile + jnp.where(i == 4, extra[:, lanes], 0.0)

            @pl.when(i == 3)
            def _():
                extra[:, lanes] = tile

            @pl.when(i != 3)
            def _():
                part[pq, 0, :, lanes] = tile[:half].astype(BF)
                part[pq, 1, :, lanes] = tile[half:].astype(BF)

            return carry

        lax.fori_loop(0, width // (per * rr), cols_out, 0)

        @pl.when(i != 3)
        def _():
            sums.push(k)

        @pl.when((i > 0) & (i < 4))
        def _():
            sums.pass_on(i)

        for j in range(4):

            @pl.when(i == j)
            def _():
                pump(6 + j)

        return carry

    extra[...] = jnp.zeros_like(extra)
    lax.fori_loop(0, 5, step, 0)
    sums.ready()

    def finish(i, carry):
        at = pl.ds(pl.multiple_of(i * 32, 32), 32)
        total = tok[at, :].astype(F32) + sums.own(at)
        resid[at, :] = total
        unit = total * lax.rsqrt(jnp.mean(total * total, axis=-1, keepdims=True) + EPS)
        o_norm[at, :] = (unit * o_gain[1:2, :]).astype(BF)
        return carry

    pump(10)
    lax.fori_loop(0, half // 32, finish, 0)
    pump(11)
    while trickle:
        trickle.pop(0)()
    pump(12)
    for k in (1, 2):
        g_rows.forward(k)
    pump(13)
    g_rows.forward(3)
    for j in range(14, len(order)):
        pump(j)
    for a in mlps:
        a.arrive_all()
    for k in range(4):
        g_rows.arrive(k)
    exchange(q, 0, n).wait_send()
    for a in [smalls, shared] + mlps + gats + recs + [u_rows, g_rows, sums]:
        a.finish()
    for cp in keep:
        cp.wait()


def forward(tok, cot, wb, wi, wo, wg, wu, wd, wr, wig, small, n, taps, cid):
    half, width = tok.shape
    heads, rb, blk = wr.shape
    rr = wb.shape[0]
    length = 2 * half
    ff = wg.shape[1] // 4
    vm = pl.BlockSpec(memory_space=pltpu.VMEM)
    hb = pl.BlockSpec(memory_space=pl.ANY)

    def sds(*shape, t=F32):
        return jax.ShapeDtypeStruct(shape, t)

    unit = sds(5, length, blk)
    outs = (
        (sds(2, 3, n, rr, blk, t=BF), hb),
        (sds(3 * ff // blk, n, rr, blk, t=BF), hb),
        (sds(2, blk, 2 * blk, t=BF), vm),
        (sds(2, 16, blk), vm),
        (sds(8, width), vm),
        (sds(4, 8, 128), vm),
        (sds(4, 2, half, width, t=BF), hb),
        (sds(4, 2, half, width, t=BF), hb),
        (sds(5, length, 2 * blk), vm),
        (unit, vm),
        (sds(5, length, blk, t=BF), vm),
        (sds(half, width), vm),
        (sds(half, width, t=BF), vm),
    )
    count = n // 2
    return pl.pallas_call(
        functools.partial(forward_kernel, n, taps, heads),
        out_shape=tuple(o for o, _ in outs),
        in_specs=[vm, vm] + [hb] * 9,
        out_specs=[s for _, s in outs],
        scratch_shapes=[
            pltpu.VMEM((2, 3, n, rr, blk), BF),
            pltpu.VMEM((2, n, rb, 2 * blk), BF),
            pltpu.VMEM((n, SMALL_ROWS, 128), BF),
            pltpu.VMEM((4, 2, half, width), BF),
            pltpu.VMEM((half, width), BF),
            pltpu.VMEM((4, 2, half, width), BF),
            pltpu.VMEM((4, half, width), BF),
            pltpu.VMEM((4, half, width), BF),
            pltpu.VMEM((length, width), F32),
            pltpu.VMEM((length, blk), F32),
            pltpu.VMEM((blk, 2 * blk), F32),
        ]
        + [
            pltpu.SemaphoreType.DMA((count,)),
            pltpu.SemaphoreType.DMA((n,)),
            pltpu.SemaphoreType.DMA((count,)),
        ]
        * 16
        + row_sems() * 3
        + [pltpu.SemaphoreType.DMA((3,)), pltpu.SemaphoreType.DMA, pltpu.SemaphoreType.DMA],
        compiler_params=pltpu.CompilerParams(
            collective_id=cid, has_side_effects=True, vmem_limit_bytes=VMEM_LIMIT
        ),
        name="forward",
    )(tok, cot, wb, wi, wo, wg, wu, wd, wr, wig, small)


def mlp_kernel(norm, resid, gain, cot, ends, w_hbm, mg_hbm, g_hbm, o_rec, o_rgrad, o_hid, o_gain,
               w, nbuf, mg, hg, hu, gbuf, part, sibb, got, wsem, msem, gsem, *sems):
    zh, zl, y, x, c = place()
    here = (zh, zl, y, x)
    q, me = zl * 2 + x, dp_at(zh, zl, y, x)
    half, width = norm.shape
    nt, n, rr, blk = w.shape
    tiles, steps, per = nt // 3, width // blk, blk // rr
    rows = Rows(nbuf, sems[:4], here, c)
    sums = Sums(part, sibb, got, sems[4:8], rows)
    greet([dev(me, 1 - c)] + [rows.at(k)[1] for k in (1, 2, 3)])
    nbuf[q, c] = norm[...]
    rows.start()
    loads = []
    for t in range(tiles):
        for i in range(3):
            j = i * tiles + t
            loads.append((t, pltpu.make_async_copy(w_hbm.at[j], w.at[j], wsem.at[j])))
    loads.insert(2, (0, pltpu.make_async_copy(mg_hbm, mg, msem)))
    for _, cp in loads:
        cp.start()

    def row(k, carry):
        pq, _ = rows.at(k)
        rows.arrive(k)

        def first(t, carry):
            @pl.when(k == 0)
            def _():
                for j, cp in loads:

                    @pl.when(t == j)
                    def _():
                        cp.wait()

            a = nbuf[pq].reshape(2 * half, width)
            gate = mm(a, w[t].reshape(width, blk))
            up = mm(a, w[tiles + t].reshape(width, blk))
            grad = mm(mg[pq].reshape(2 * half, width), w[2 * tiles + t].reshape(width, blk))
            act, der = gelu_parts(gate)
            o_hid[t, pq] = (act * up).astype(BF)
            hg[t, pq] = (grad * up * der).astype(BF)
            hu[t, pq] = (grad * act).astype(BF)
            return carry

        lax.fori_loop(0, tiles, first, 0)

        @pl.when(k < 3)
        def _():
            rows.forward(k + 1)

        @pl.when(k > 1)
        def _():
            sums.pass_on(k - 1)

        def second(d, carry):
            total = jnp.zeros((2 * half, blk), F32)
            for t in range(tiles):
                total = total + mm_t(hg[t, pq], w[t, pl.ds(d * per, per)].reshape(blk, blk))
                total = total + mm_t(hu[t, pq], w[tiles + t, pl.ds(d * per, per)].reshape(blk, blk))
            lanes = pl.ds(pl.multiple_of(d * blk, 128), blk)
            part[pq, 0, :, lanes] = total[:half].astype(BF)
            part[pq, 1, :, lanes] = total[half:].astype(BF)
            return carry

        lax.fori_loop(0, steps, second, 0)
        sums.push(k)
        return carry

    def rows_from(k, carry):
        return row(k, carry)

    lax.fori_loop(0, 4, rows_from, 0)
    sums.pass_on(3)

    def out_tile(d):
        at = pl.ds(d * per, per)
        return pltpu.make_async_copy(gbuf.at[:, at], g_hbm.at[:, at], gsem.at[d])

    def grads(d, carry):
        lanes = pl.ds(pl.multiple_of(d * blk, 128), blk)
        nt_ = nbuf[:, :, :, lanes].reshape(8 * half, blk).T
        mt_ = mg[:, :, :, lanes].reshape(8 * half, blk).T
        for i, (left, right) in enumerate(((nt_, hg), (nt_, hu), (mt_, o_hid))):
            for t in range(tiles):
                tile = mm(left, right[t].reshape(8 * half, blk))
                gbuf[i * tiles + t, pl.ds(d * per, per)] = tile.astype(BF).reshape(per, rr, blk)
        out_tile(d).start()
        return carry

    lax.fori_loop(0, steps, grads, 0)
    sums.ready()
    e3 = ends[q][0:1, 3:4]

    def finish(i, acc):
        at = pl.ds(pl.multiple_of(i * 32, 32), 32)
        total, r = sums.own(at), resid[at, :]
        scale = lax.rsqrt(jnp.mean(r * r, axis=-1, keepdims=True) + EPS)
        unit = r * scale
        g2 = total * gain[1:2, :]
        back = scale * (g2 - unit * jnp.mean(g2 * unit, axis=-1, keepdims=True))
        spot = lax.broadcasted_iota(jnp.int32, (32, 1), 0) + (c * half + i * 32)
        back = back + jnp.where(spot.astype(F32) < e3, cot[at, :], 0.0)
        o_rgrad[at, :] = back
        o_rec[at, :] = back.astype(BF)
        return acc + jnp.sum(total * unit, axis=0, keepdims=True)

    gsum = lax.fori_loop(0, half // 32, finish, jnp.zeros((1, width), F32))
    o_gain[...] = jnp.broadcast_to(gsum, o_gain.shape)
    for d in range(steps):
        out_tile(d).wait()
    rows.finish()
    sums.finish()


def mlp_block(norm, resid, gain, cot, ends, mlp_w, mlp_grad, cid):
    half, width = norm.shape
    nt, n, rr, blk = mlp_w.shape
    tiles = nt // 3
    vm = pl.BlockSpec(memory_space=pltpu.VMEM)
    hb = pl.BlockSpec(memory_space=pl.ANY)
    hid = (tiles, 4, 2 * half, blk)
    return pl.pallas_call(
        mlp_kernel,
        out_shape=(
            jax.ShapeDtypeStruct(mlp_w.shape, BF),
            jax.ShapeDtypeStruct((half, width), BF),
            jax.ShapeDtypeStruct((half, width), F32),
            jax.ShapeDtypeStruct(hid, BF),
            jax.ShapeDtypeStruct((8, width), F32),
        ),
        in_specs=[vm] * 5 + [hb] * 2,
        out_specs=[hb] + [vm] * 4,
        scratch_shapes=[
            pltpu.VMEM(mlp_w.shape, BF),
            pltpu.VMEM((4, 2, half, width), BF),
            pltpu.VMEM((4, 2, half, width), BF),
            pltpu.VMEM(hid, BF),
            pltpu.VMEM(hid, BF),
            pltpu.VMEM(mlp_w.shape, BF),
            pltpu.VMEM((4, 2, half, width), BF),
            pltpu.VMEM((4, half, width), BF),
            pltpu.VMEM((4, half, width), BF),
            pltpu.SemaphoreType.DMA((nt,)),
            pltpu.SemaphoreType.DMA,
            pltpu.SemaphoreType.DMA((width // blk,)),
        ]
        + row_sems() * 2,
        compiler_params=pltpu.CompilerParams(
            collective_id=cid, has_side_effects=True, vmem_limit_bytes=VMEM_LIMIT
        ),
        name="mlp_block",
    )(norm, resid, gain, cot, ends, mlp_w, mlp_grad)


class Scatter:
    def __init__(self, away, mine, pair, landed, sems, here, there, core):
        self.away, self.mine, self.pair, self.landed = away, mine, pair, landed
        self.ysend, self.yrecv, self.send, self.recv = sems
        zh, zl, y, x = here
        self.core = core
        self.own = zh * 4 + zl * 2 + x
        self.places = [
            (h * 4 + z * 2 + w, dp_at(h, z, y, w), dp_at(h, z, 1 - y, w)) for h, z, w in (*there[1:], there[0])
        ]
        self.other = dev(dp_at(zh, zl, 1 - y, x), core)

    def start(self):
        for j, _, far in self.places:
            remote(self.away(far), self.pair(j), self.ysend.at[j], self.yrecv.at[j], self.other).start()

    def pass_on(self):
        last = len(self.places) - 1
        for i, (j, near, _) in enumerate(self.places):
            slot = self.pair(j)
            remote(slot, slot, self.ysend.at[j], self.yrecv.at[j], self.other).wait_recv()
            slot[...] = (self.mine(near).astype(F32) + slot[...].astype(F32)).astype(slot.dtype)
            if i == last:
                pltpu.make_async_copy(slot, self.landed(self.own), self.send.at[j]).start()
            else:
                remote(
                    slot, self.landed(self.own), self.send.at[j], self.recv.at[self.own], dev(near, self.core)
                ).start()

    def collect(self):
        last = len(self.places) - 1
        for i, (j, _, _) in enumerate(self.places):
            slot, land = self.pair(j), self.landed(j)
            remote(slot, slot, self.ysend.at[j], self.yrecv.at[j], self.other).wait_send()
            if i == last:
                pltpu.make_async_copy(land, land, self.send.at[j]).wait()
            else:
                remote(land, land, self.send.at[j], self.recv.at[j], self.other).wait_recv()
                remote(slot, slot, self.send.at[j], self.recv.at[j], self.other).wait_send()


def scatter_sems(high):
    return [pltpu.SemaphoreType.DMA((high * 4,))] * 4


def rec_gates(taps, conv_in, vec, gates, ends):
    length, blk = conv_in.shape
    same = segments(ends, length, blk, taps)
    conv = conv_in * vec[4:5] + vec[4 + taps : 5 + taps]
    for k in range(1, taps):
        conv = conv + pltpu.roll(conv_in, k, 0) * same[k - 1] * vec[4 + k : 5 + k]
    pre = jnp.dot(conv.astype(BF), gates, preferred_element_type=F32)
    r = jax.nn.sigmoid(pre[:, :blk] + vec[0:1])
    gate = jax.nn.sigmoid(pre[:, blk:] + vec[1:2])
    return same, conv, r, gate


def rec_unit_back(taps, branch, conv_in, vec, gates, ends, state, mg, carry_ref, a_ref):
    length, blk = branch.shape
    same, conv, r, gate = rec_gates(taps, conv_in, vec, gates, ends)
    start = same[0] == 0.0
    act, der = gelu_parts(branch)
    branch_low = (mg * state * der).astype(BF)
    log_a = (-DECAY * r) * vec[2:3]
    a = jnp.exp(log_a)
    a_eff = jnp.where(start, 0.0, a)
    row = lax.broadcasted_iota(jnp.int32, (length, blk), 0)
    a_next = jnp.where(row < length - 1, pltpu.roll(a_eff, length - 1, 0), 0.0)
    full_scan(a_next, mg * act, carry_ref, a_ref, True)
    carry = carry_ref[...]
    prev = jnp.where(row > 0, pltpu.roll(state, 1, 0), 0.0)
    raw = jnp.sqrt(-jnp.tanh(log_a) * (1.0 + a * a))
    mult = jnp.where(start, 1.0, raw)
    log_grad = jnp.where(start, 0.0, carry * prev * a - carry * gate * conv * (a * a) / raw)
    r_grad = log_grad * (-DECAY * vec[2:3]) * (r * (1.0 - r))
    i_grad = carry * mult * conv * (gate * (1.0 - gate))
    pre_low = jnp.concatenate([r_grad.astype(BF), i_grad.astype(BF)], axis=1)
    conv_grad = carry * mult * gate + mm_t(pre_low, gates)
    gate_grads = t_mm(conv.astype(BF), pre_low)

    def total(v):
        return jnp.sum(v, axis=0, keepdims=True)

    sums = [total(r_grad), total(i_grad), total(log_grad * (DECAY * r) * vec[3:4]), total(conv_grad)]
    inp = conv_grad * vec[4:5]
    sums.append(total(conv_grad * conv_in))
    for k in range(1, taps):
        masked = conv_grad * same[k - 1]
        sums.append(total(masked * pltpu.roll(conv_in, k, 0)))
        inp = inp + pltpu.roll(masked, length - k, 0) * vec[4 + k : 5 + k]
    return branch_low, inp.astype(BF), gate_grads, jnp.concatenate(sums, axis=0)


def backward_kernel(n, taps, *refs):
    (tok, rgrad, resid, gain, gsum2, ends, vec, gates, pre, state, mixed) = refs[:11]
    (rec_own, hid, g_hbm, rec_hbm, mlp_hbm, u_hbm) = refs[11:17]
    (o_res, o_tok, l_mlp, l_rec, l_sh, l_gate, l_small) = refs[17:24]
    (rec, ub, rg, part, sib1, got1, sib2, got2, low, grec, gsh, gshin, g_own, y_mlp, y_rec, y_sh, a_scr, c_scr,
     gg, vg, ggl, y_gate, sml, sml_sib, y_sml) = refs[24:49]
    sems = refs[49:]
    zh, zl, y, x, c = place()
    here = (zh, zl, y, x)
    q, me = zl * 2 + x, dp_at(zh, zl, y, x)
    high = n // 8
    there = plane(zh, zl, y, x, high)
    half, width = tok.shape
    length = 2 * half
    blk = mixed.shape[2]
    rr = width // n
    rb = blk // n
    nt = y_mlp.shape[0]
    per, steps = blk // rr, width // blk
    taken = [0]

    def some(k):
        taken[0] += k
        return sems[taken[0] - k : taken[0]]

    rows = Rows(rg, some(4), here, c)
    sums1 = Sums(part, sib1, got1, some(4), rows)
    sums2 = Sums(part, sib2, got2, some(4), rows)
    (loads,) = some(1)
    greet(
        [dev(dp_at(h, z, y, w), c) for h, z, w in there[1:]]
        + [dev(dp_at(zh, zl, 1 - y, x), c), dev(me, 1 - c)]
    )
    first = pltpu.make_async_copy(rec_own, rg.at[q, c], loads.at[0])
    first.start()
    first.wait()
    rows.start()
    grab = [
        pltpu.make_async_copy(rec_hbm, rec, loads.at[0]),
        pltpu.make_async_copy(u_hbm, ub, loads.at[1]),
    ]
    for cp in grab:
        cp.start()

    tiles = nt // 3

    def cols_at(i):
        return pl.ds(pl.multiple_of(i * blk, 128), blk)

    def own_part(i):
        return pltpu.make_async_copy(g_hbm.at[i, :, y], g_own.at[i % 2], loads.at[2 + i % 2])

    own_part(0).start()

    def chunk(i, sem):
        return Scatter(
            lambda s: g_hbm.at[i, s // 4, (s // 2) % 2, s % 2],
            lambda s: g_own[i % 2, s // 4, s % 2],
            lambda j: y_mlp.at[i, j],
            lambda j: l_mlp.at[j // 4, i // tiles, :, cols_at((j % 4) * tiles + i % tiles)],
            sem, here, there, c,
        )

    mlps = [chunk(i, some(4)) for i in range(nt)]
    for a in mlps[:3]:
        a.start()
    recs = [
        Scatter(
            lambda s, i=i: grec.at[i, s],
            lambda s, i=i: grec[i, s],
            lambda j, i=i: y_rec.at[i, j],
            lambda j, i=i: l_rec.at[j // 4, i, :, cols_at(j % 4)],
            some(4), here, there, c,
        )
        for i in range(3)
    ]
    part_rows = rr // 2

    shared = Scatter(
        lambda s: gshin.at[:, s],
        lambda s: gshin[:, s],
        lambda j: y_sh.at[j],
        lambda j: l_sh.at[j // 2, :, pl.ds(pl.multiple_of((j % 2) * part_rows, 8), part_rows), :],
        some(4), here, there, c,
    )
    gate_sc = Scatter(
        lambda s: ggl.at[:, s],
        lambda s: ggl[:, s],
        lambda j: y_gate.at[j],
        lambda j: l_gate.at[j],
        some(4), here, there, c,
    )
    h_send, h_recv, s_send, s_recv, z_send, z_recv, m_send, m_recv = some(8)
    order = mlps + recs + [gate_sc]
    trickle = []

    def pump(j):
        if j < nt:
            own_part(j).wait()
            if j + 1 < nt:
                own_part(j + 1).start()
        order[j].pass_on()
        for _ in range(2):
            if trickle:
                trickle.pop(0)()
        if j + 3 < len(order):
            order[j + 3].start()

    gg[...] = jnp.zeros_like(gg)
    vg[...] = jnp.zeros_like(vg)
    grab[0].wait()

    def step(i, carry):
        h = jnp.where(i == 1, 1, 0)
        k = jnp.maximum(i - 1, 0)
        pq, _ = rows.at(k)
        at = pq + h * (4 - pq)

        @pl.when(i != 1)
        def _():
            rows.arrive(k)

        mg = mm(rg[pq].reshape(length, width), rec[h, 2].reshape(width, blk))

        @pl.when((i > 0) & (i < 4))
        def _():
            rows.forward(k + 1)

        b_low, i_low, g_add, v_add = rec_unit_back(
            taps, pre[at, :, :blk], pre[at, :, blk:], vec[h], gates[h], ends[pq][0:1, :], state[at], mg, c_scr, a_scr,
        )
        low[at, :, :blk], low[at, :, blk:] = b_low, i_low
        gg[h] += g_add
        vg[h] += v_add

        @pl.when(i > 2)
        def _():
            sums1.pass_on(k - 1)

        def cols_out(t, carry):
            cut = pl.ds(t * per, per)
            lanes = pl.ds(pl.multiple_of(t * blk, 128), blk)

            def tile_of(left, head):
                return sum(
                    mm_t(left[:, j * blk : (j + 1) * blk], rec[head, j, cut].reshape(blk, blk)) for j in range(2)
                )

            def emit(tile):
                part[pq, 0, :, lanes] = tile[:half].astype(BF)
                part[pq, 1, :, lanes] = tile[half:].astype(BF)

            @pl.when(i == 1)
            def _():
                emit(tile_of(low[4], 1) + tile_of(low[pq], 0))

            @pl.when(i > 1)
            def _():
                emit(tile_of(low[pq], 0))

            return carry

        @pl.when(i > 0)
        def _():
            lax.fori_loop(0, steps, cols_out, 0)

        @pl.when(i > 0)
        def _():
            sums1.push(k)

        for j in range(5):

            @pl.when(i == j)
            def _():
                pump(j)

        return carry

    lax.fori_loop(0, 5, step, 0)
    sums1.pass_on(3)
    for h in range(2):
        for s in range(n):
            ggl[h, s] = gg[h, s * rb : (s + 1) * rb, :].astype(BF)
    pump(5)
    grab[1].wait()

    def grads(d, carry):
        lanes = pl.ds(pl.multiple_of(d * blk, 128), blk)
        at = pl.ds(d * per, per)
        ut = ub[:, :, :, lanes].reshape(4 * length, blk).T
        rt = rg[:, :, :, lanes].reshape(4 * length, blk).T
        uo = ub[q, :, :, lanes].reshape(length, blk).T
        ro = rg[q, :, :, lanes].reshape(length, blk).T
        for i in range(3):
            if i < 2:
                right = low[0:4, :, i * blk : (i + 1) * blk].reshape(4 * length, blk)
                own = low[4, :, i * blk : (i + 1) * blk]
            else:
                right, own = mixed[0:4].reshape(4 * length, blk), mixed[4]
            grec[i, at] = mm(ut if i < 2 else rt, right).astype(BF).reshape(per, rr, blk)
            gsh[i, at] = mm(uo if i < 2 else ro, own).astype(BF).reshape(per, rr, blk)
        return carry

    lax.fori_loop(0, steps, grads, 0)
    _, beside = rows.at(1)

    def exchange(first, many):
        there_rows = pl.ds(pl.multiple_of((1 - x) * part_rows, 8), part_rows)
        cut = pl.ds(first, many)
        return remote(gsh.at[:, cut, there_rows, :], gshin.at[:, cut], h_send, h_recv, beside)

    eighth = n // 8
    trickle += [exchange(p * eighth, eighth).start for p in range(8)]
    pump(6)

    sums1.ready()

    def finish(i, acc):
        at = pl.ds(pl.multiple_of(i * 32, 32), 32)
        total, xin = sums1.own(at), tok[at, :].astype(F32)
        scale = lax.rsqrt(jnp.mean(xin * xin, axis=-1, keepdims=True) + EPS)
        unit = xin * scale
        g1 = total * gain[0:1, :]
        o_tok[at, :] = rgrad[at, :] + scale * (g1 - unit * jnp.mean(g1 * unit, axis=-1, keepdims=True))
        return acc + jnp.sum(total * unit, axis=0, keepdims=True)

    gsum1 = lax.fori_loop(0, half // 32, finish, jnp.zeros((1, width), F32))
    sums1.finish()
    for h in range(2):
        sml[8 * h : 8 * h + 8, :] = vg[h]
    for i in range(steps):
        sml[16 + i : 17 + i, :] = gsum1[:, i * blk : (i + 1) * blk]
        sml[16 + steps + i : 17 + steps + i, :] = gsum2[0:1, i * blk : (i + 1) * blk]
    gain_rows = sml.at[pl.ds(16, 2 * steps)]
    with_sib = remote(gain_rows, sml_sib, s_send, s_recv, rows.sib)
    with_sib.start()
    pump(7)
    with_sib.wait()
    sml[16 : 16 + 2 * steps, :] += sml_sib[...]
    with_y = remote(sml, y_sml, z_send, z_recv, dev(dp_at(zh, zl, 1 - y, x), c))
    with_y.start()
    pump(8)
    pump(9)
    exchange(0, n).wait()
    for s in range(n):
        gshin[:, s] = (
            gshin[:, s].astype(F32)
            + gsh[:, s, pl.ds(pl.multiple_of(x * part_rows, 8), part_rows), :].astype(F32)
        ).astype(BF)
    shared.start()
    fetch = pltpu.make_async_copy(mlp_hbm.at[pl.ds(2 * (nt // 3), nt // 3)], rec.at[0], loads.at[0])
    fetch.start()
    per_row = length // rr
    fetch_hid = pltpu.make_async_copy(hid, gsh.at[:, pl.ds(0, 4 * per_row)], loads.at[1])
    fetch_hid.start()
    pump(10)
    fetch.wait()
    fetch_hid.wait()

    def out_rows(i, carry):
        k = (i + 1) % 4
        pq, _ = rows.at(k)

        def cols_out(d, carry):
            tile = jnp.zeros((length, blk), F32)
            for t in range(nt // 3):
                left = gsh[t, pl.ds(pq * per_row, per_row)].reshape(length, blk)
                tile = tile + mm_t(left, rec[0, t, pl.ds(d * per, per)].reshape(blk, blk))
            lanes = pl.ds(pl.multiple_of(d * blk, 128), blk)
            part[pq, 0, :, lanes] = tile[:half].astype(BF)
            part[pq, 1, :, lanes] = tile[half:].astype(BF)
            return carry

        lax.fori_loop(0, steps, cols_out, 0)
        sums2.push(k)

        @pl.when(i > 0)
        def _():
            sums2.pass_on(i)

        for j in range(2):

            @pl.when(i == 1 + 2 * j)
            def _():
                pump(11 + j)

        return carry

    lax.fori_loop(0, 4, out_rows, 0)
    with_y.wait()
    sml[...] = sml[...] + y_sml[...]
    mine = zh * 4 + q
    small_out = []
    for i, (h, z, w) in enumerate(there):
        if i == 0:
            cp = pltpu.make_async_copy(sml, l_small.at[mine], m_send.at[i])
        else:
            cp = remote(sml, l_small.at[mine], m_send.at[i], m_recv.at[mine], dev(dp_at(h, z, y, w), c))
        cp.start()
        small_out.append(cp)
    shared.pass_on()
    sums2.ready()
    e3 = ends[q][0:1, 3:4]

    def result(i, carry):
        at = pl.ds(pl.multiple_of(i * 32, 32), 32)
        spot = lax.broadcasted_iota(jnp.int32, (32, 1), 0) + (c * half + i * 32)
        o_res[at, :] = jnp.where(spot.astype(F32) < e3, resid[at, :] + sums2.own(at), 0.0).astype(BF)
        return carry

    lax.fori_loop(0, half // 32, result, 0)
    sums2.finish()
    rows.finish()
    for a in mlps + recs + [gate_sc, shared]:
        a.collect()
    for i, (h, z, w) in enumerate(there):
        if i == 0:
            small_out[i].wait()
        else:
            j = h * 4 + z * 2 + w
            land = l_small.at[j]
            remote(land, land, m_send.at[i], m_recv.at[j], rows.sib).wait_recv()
            small_out[i].wait_send()


def backward(tok, rec_own, rgrad, resid, gain, gsum2, ends, vec, gates, saved, hid, g_mlp, rec_w, mlp_w, u, n, taps, cid):
    half, width = tok.shape
    pre, state, mixed = saved
    blk = mixed.shape[2]
    length = 2 * half
    rr, rb, high = width // n, blk // n, n // 8
    nt = g_mlp.shape[0]
    slots = high * 4
    vm = pl.BlockSpec(memory_space=pltpu.VMEM)
    hb = pl.BlockSpec(memory_space=pl.ANY)
    g_view = g_mlp.reshape(nt, n // 4, 2, 2, rr, blk)
    hid = hid.reshape(nt // 3, 4 * length // rr, rr, blk)
    small_rows = 16 + 2 * (width // blk)

    def sds(*shape, t=BF):
        return jax.ShapeDtypeStruct(shape, t)

    def v(*shape, t=BF):
        return pltpu.VMEM(shape, t)

    dma = pltpu.SemaphoreType.DMA
    return pl.pallas_call(
        functools.partial(backward_kernel, n, taps),
        out_shape=(
            sds(half, width),
            sds(half, width, t=F32),
            sds(high, 3, rr, 4 * (nt // 3) * blk),
            sds(high, 3, rr, 4 * blk),
            sds(slots // 2, 3, rr, blk),
            sds(slots, 2, rb, 2 * blk),
            sds(slots, small_rows, blk, t=F32),
        ),
        in_specs=[vm] * 11 + [hb] * 6,
        out_specs=[vm, vm] + [hb] * 5,
        scratch_shapes=[
            v(2, 3, n, rr, blk),
            v(4, 2, half, width),
            v(4, 2, half, width),
            v(4, 2, half, width),
            v(4, half, width),
            v(4, half, width),
            v(4, half, width),
            v(4, half, width),
            v(5, length, 2 * blk),
            v(3, n, rr, blk),
            v(3, n, rr, blk),
            v(3, n, rr // 2, blk),
            v(2, n // 4, 2, rr, blk),
            v(nt, slots, rr, blk),
            v(3, slots, rr, blk),
            v(slots, 3, rr // 2, blk),
            v(length, blk, t=F32),
            v(length, blk, t=F32),
            v(2, blk, 2 * blk, t=F32),
            v(2, 4 + taps, blk, t=F32),
            v(2, n, rb, 2 * blk),
            v(slots, 2, rb, 2 * blk),
            v(small_rows, blk, t=F32),
            v(small_rows - 16, blk, t=F32),
            v(small_rows, blk, t=F32),
        ]
        + row_sems() * 3
        + [dma((4,))]
        + scatter_sems(high) * (nt + 5)
        + [dma, dma, dma, dma, dma, dma, dma((slots,)), dma((slots,))],
        compiler_params=pltpu.CompilerParams(
            collective_id=cid, has_side_effects=True, vmem_limit_bytes=VMEM_LIMIT
        ),
        name="backward",
    )(tok, rgrad, resid, gain, gsum2, ends, vec, gates, *saved, rec_own, hid, g_view, rec_w, mlp_w, u)


def mm(a, b):
    return jnp.dot(a, b, preferred_element_type=F32)


def mm_t(a, b):
    return lax.dot_general(a, b, (((1,), (1,)), ((), ())), preferred_element_type=F32)


def t_mm(a, b):
    return lax.dot_general(a, b, (((0,), (0,)), ((), ())), preferred_element_type=F32)


def local(
    tokens, doc_lengths, rec_gain, w_branch, w_input, w_rgate, w_igate, rgate_bias, igate_bias,
    decay_param, conv_weight, conv_bias, w_output, mlp_gain, w_gate, w_up, w_down, cotangent,
):
    n = lax.axis_size("dp")
    zh, zl, y, x, c = place()
    q = zl * 2 + x
    _, half, width = tokens.shape
    length = half * 2
    heads, rb, blk = w_rgate.shape
    taps = conv_weight.shape[0]
    rows = w_branch.shape[0]
    ff = w_gate.shape[1] // 4

    dp = lax.axis_index("dp")

    def lanes(v, per):
        v = v.astype(BF).reshape(-1, per)
        at = (dp * per) % 128
        return lax.dynamic_update_slice(jnp.zeros((v.shape[0], 128), BF), v, (0, at))

    params = jnp.concatenate(
        [rgate_bias[:, None], igate_bias[:, None], decay_param[:, None], conv_weight.transpose(1, 0, 2), conv_bias[:, None]],
        axis=1,
    )
    params = jnp.pad(params, ((0, 0), (0, 16 - params.shape[1]), (0, 0))).reshape(heads * 16, rb)
    lens = doc_lengths.reshape(4).astype(F32)
    e0 = lens[0]
    e1 = e0 + lens[1]
    e2 = e1 + lens[2]
    e3 = e2 + lens[3]
    ends_own = jnp.pad(jnp.stack([e0, e1, e2, e3]).astype(BF)[None], ((0, 13), (0, 124)))
    small = jnp.concatenate([lanes(params, rb), lanes(jnp.stack([rec_gain, mlp_gain]), rows), ends_own], axis=0)
    (
        rec_w, mlp_w, gates, vec, gains_all, group_ends, u, mlp_grad, pre, state, mixed, resid, norm_own,
    ) = forward(
        tokens[0], cotangent[0], w_branch, w_input, w_output.T, w_gate, w_up, w_down.T, w_rgate, w_igate, small, n, taps, 1,
    )
    g_mlp, rec_own, resid_grad, hid, gain2_sum = mlp_block(
        norm_own, resid, gains_all, cotangent[0], group_ends, mlp_w, mlp_grad, 4
    )
    result, token_grad, l_mlp, l_rec, l_sh, l_gate, l_small = backward(
        tokens[0], rec_own, resid_grad, resid, gains_all, gain2_sum, group_ends, vec, gates,
        (pre, state, mixed), hid, g_mlp, rec_w, mlp_w, u, n, taps, 5,
    )
    high = n // 8

    def owned(a):
        return jnp.sum(a.reshape((high, 4) + a.shape[1:]).astype(F32), axis=0)

    def add(a):
        return jnp.sum(a.astype(F32), axis=0)

    o_mlp = [add(l_mlp[:, i]) for i in range(3)]
    o_rec = [jnp.concatenate([add(l_rec[:, i]), add(l_sh[:, i])], axis=1) for i in range(3)]
    o_gate = owned(l_gate)
    o_gate = jnp.concatenate([o_gate[:, 0], jnp.sum(o_gate[:, 1], axis=0, keepdims=True)], axis=0)
    o_small = owned(l_small)
    at = dp * rb
    o_vec = jnp.concatenate([o_small[:, :8], jnp.sum(o_small[:, 8:16], axis=0, keepdims=True)], axis=0)
    o_vec = lax.dynamic_slice_in_dim(o_vec, at, rb, 2)
    o_gain = jnp.sum(o_small[:, 16:], axis=0).reshape(2, width)
    o_gain = lax.dynamic_slice_in_dim(o_gain, dp * rows, rows, 1)
    return (
        result[None],
        token_grad[None],
        o_gain[0],
        o_rec[0],
        o_rec[1],
        o_gate[:, :, :blk],
        o_gate[:, :, blk:],
        o_vec[:, 0],
        o_vec[:, 1],
        o_vec[:, 2],
        o_vec[:, 4 : 4 + taps].transpose(1, 0, 2),
        o_vec[:, 3],
        o_rec[2].T,
        o_gain[1],
        o_mlp[0],
        o_mlp[1],
        o_mlp[2].T,
    )


def solution(mesh):
    return jax.shard_map(
        local,
        mesh=mesh,
        in_specs=(
            P("dp", "tensor", None),
            P("dp", None),
            P("dp"),
            P("dp", "tensor"),
            P("dp", "tensor"),
            P("tensor", "dp", None),
            P("tensor", "dp", None),
            P("tensor", "dp"),
            P("tensor", "dp"),
            P("tensor", "dp"),
            P(None, "tensor", "dp"),
            P("tensor", "dp"),
            P("tensor", "dp"),
            P("dp"),
            P("dp", "tensor"),
            P("dp", "tensor"),
            P("tensor", "dp"),
            P("dp", "tensor", None),
        ),
        out_specs=(
            P("dp", "tensor", None),
            P("dp", "tensor", None),
            P("dp"),
            P("dp", "tensor"),
            P("dp", "tensor"),
            P("tensor", "dp", None),
            P("tensor", "dp", None),
            P("tensor", "dp"),
            P("tensor", "dp"),
            P("tensor", "dp"),
            P(None, "tensor", "dp"),
            P("tensor", "dp"),
            P("tensor", "dp"),
            P("dp"),
            P("dp", "tensor"),
            P("dp", "tensor"),
            P("tensor", "dp"),
        ),
        check_vma=False,
    )
```

```python
import functools

import jax
import jax.numpy as jnp
from jax import lax
from jax.experimental import pallas as pl
from jax.experimental.pallas import tpu as pltpu
from jax.sharding import PartitionSpec as P

MESH = pl.DeviceIdType.MESH
BF = jnp.bfloat16
F32 = jnp.float32
EPS = 1e-06
DECAY = 8.0
GC = 0.7978845608028654
GK = 0.044715
VMEM_LIMIT = 62 * 1024 * 1024


def dp_at(zh, zl, y, x):
    return ((zh * 2 + zl) * 2 + y) * 2 + x


def place():
    dp = lax.axis_index("dp")
    return dp // 8, (dp // 4) % 2, (dp // 2) % 2, dp % 2, lax.axis_index("tensor")


def dev(dp, core):
    return {"dp": dp, "tensor": core}


def greet(devices):
    sem = pltpu.get_barrier_semaphore()
    for d in devices:
        pl.semaphore_signal(sem, inc=1, device_id=d, device_id_type=MESH)
    pl.semaphore_wait(sem, len(devices))


def remote(src, dst, ssem, rsem, d):
    return pltpu.make_async_remote_copy(
        src_ref=src, dst_ref=dst, send_sem=ssem, recv_sem=rsem, device_id=d, device_id_type=MESH
    )


def plane(zh, zl, y, x, high):
    out = []
    for kh in range(high):
        for kl in range(2):
            for kx in range(2):
                ph, pz, px = (zh + kh) % high, (zl + kl) % 2, (x + kx) % 2
                out.append((ph, pz, px))
    return out


def gelu_parts(v):
    t = jnp.tanh(GC * (v + GK * v * v * v))
    act = 0.5 * v * (1.0 + t)
    der = 0.5 * (1.0 + t) + 0.5 * v * (1.0 - t * t) * GC * (1.0 + 3.0 * GK * v * v)
    return act, der


def segments(ends, length, width, taps):
    t = lax.broadcasted_iota(jnp.int32, (length, width), 0).astype(F32)

    def seg(at):
        total = jnp.zeros((length, width), F32)
        for j in range(4):
            total = total + jnp.where(at >= ends[:, j : j + 1], 1.0, 0.0)
        return total

    here = seg(t)
    same = []
    for k in range(1, taps):
        same.append(jnp.where((t >= float(k)) & (seg(t - float(k)) == here), 1.0, 0.0))
    return same


def scan8(a, b, reverse):
    length, width = a.shape
    row = lax.broadcasted_iota(jnp.int32, (length, width), 0) % 8
    for d in (1, 2, 4):
        if reverse:
            ash, bsh = pltpu.roll(a, length - d, 0), pltpu.roll(b, length - d, 0)
            ok = row < 8 - d
        else:
            ash, bsh = pltpu.roll(a, d, 0), pltpu.roll(b, d, 0)
            ok = row >= d
        b = b + a * jnp.where(ok, bsh, 0.0)
        a = a * jnp.where(ok, ash, 1.0)
    return a, b


def full_scan(a, b, out_ref, a_ref, reverse):
    length, width = a.shape
    a8, b8 = scan8(a, b, reverse)
    a_ref[...] = a8
    out_ref[...] = b8
    blocks = length // 8

    def step(i, carry):
        at = (blocks - 1 - i if reverse else i) * 8
        at = pl.multiple_of(at, 8)
        now = out_ref[pl.ds(at, 8), :] + a_ref[pl.ds(at, 8), :] * carry
        out_ref[pl.ds(at, 8), :] = now
        return now[0:1, :] if reverse else now[7:8, :]

    lax.fori_loop(0, blocks, step, jnp.zeros((1, width), F32))


class Gather:
    def __init__(self, slot, parts, sems, here, there, core):
        self.slot, self.parts, (self.send, self.recv, self.fsend) = slot, parts, sems
        zh, zl, y, x = here
        self.q = zl * 2 + x
        self.me = dp_at(zh, zl, y, x)
        self.near = [dp_at(h, z, y, w) for h, z, w in there]
        self.far = [dp_at(h, z, 1 - y, w) for h, z, w in there]
        self.pick = [z * 2 + w for _, z, w in there]
        self.core = core
        self.other = dev(dp_at(zh, zl, 1 - y, x), core)

    def ks(self, far):
        count = len(self.near)
        return range(4, count) if far else range(4)

    def start(self, far):
        for k in self.ks(far):
            for piece, part in self.parts:
                src = piece(self.pick[k])
                dst = part(self.slot(self.me, self.pick[k]))
                if k == 0:
                    pltpu.make_async_copy(src, dst, self.send.at[0]).start()
                else:
                    d = dev(self.near[k], self.core)
                    remote(src, dst, self.send.at[k], self.recv.at[self.me], d).start()

    def forward(self, k):
        land = self.slot(self.near[k], self.q)
        if k == 0:
            pltpu.make_async_copy(land, land, self.send.at[0]).wait()
        else:
            remote(land, land, self.send.at[k], self.recv.at[self.near[k]], self.other).wait_recv()
        remote(land, land, self.fsend.at[k], self.recv.at[self.near[k]], self.other).start()

    def forward_all(self, far):
        for k in self.ks(far):
            self.forward(k)

    def arrive_all(self):
        for k in range(len(self.far)):
            land = self.slot(self.far[k], self.q)
            remote(land, land, self.fsend.at[k], self.recv.at[self.far[k]], self.other).wait_recv()

    def finish(self):
        for k in range(len(self.near)):
            land = self.slot(self.near[k], self.q)
            remote(land, land, self.fsend.at[k], self.recv.at[self.near[k]], self.other).wait_send()
            if k:
                remote(land, land, self.send.at[k], self.recv.at[self.near[k]], self.other).wait_send()


class Rows:
    def __init__(self, buf, sems, here, core):
        self.buf, (self.send, self.recv, self.fsend, self.frecv) = buf, sems
        self.here, self.core = here, core
        zh, zl, y, x = here
        self.q = zl * 2 + x
        self.sib = dev(dp_at(zh, zl, y, x), 1 - core)

    def at(self, k):
        zh, zl, y, x = self.here
        pz, px = (zl + k // 2) % 2, (x + k % 2) % 2
        return pz * 2 + px, dev(dp_at(zh, pz, y, px), self.core)

    def start(self, piece=0, pieces=1):
        per = self.buf.shape[2] // pieces
        own = self.buf.at[self.q, self.core, pl.ds(piece * per, per)]
        for k in (1, 2):
            _, d = self.at(k)
            remote(own, own, self.send.at[k], self.recv.at[self.q], d).start()
        remote(own, own, self.fsend.at[0], self.frecv.at[self.q], self.sib).start()

    def forward(self, k):
        pq, d = self.at(k)
        land = self.buf.at[pq, self.core]
        remote(land, land, self.send.at[k], self.recv.at[pq], d).wait_recv()

        def relay():
            _, beside = self.at(1)
            remote(land, land, self.send.at[3], self.recv.at[pq], beside).start()

        if isinstance(k, int):
            if k == 2:
                relay()
        else:
            pl.when(k == 2)(relay)
        remote(land, land, self.fsend.at[k], self.frecv.at[pq], self.sib).start()

    def arrive(self, k):
        pq, _ = self.at(k)
        land = self.buf.at[pq, 1 - self.core]
        remote(land, land, self.fsend.at[k], self.frecv.at[pq], self.sib).wait_recv()

    def finish(self):
        own = self.buf.at[self.q, self.core]
        for k in range(4):
            remote(own, own, self.fsend.at[k], self.frecv.at[self.q], self.sib).wait_send()
            if k:
                remote(own, own, self.send.at[k], self.recv.at[self.q], self.sib).wait_send()


def row_sems():
    return [pltpu.SemaphoreType.DMA((4,))] * 4


class Sums:
    def __init__(self, part, sib, got, sems, rows):
        self.part, self.sib_buf, self.got = part, sib, got
        self.ssend, self.srecv, self.send, self.recv = sems
        self.rows = rows

    def push(self, k):
        r = self.rows
        pq, _ = r.at(k)
        remote(
            self.part.at[pq, 1 - r.core], self.sib_buf.at[pq], self.ssend.at[k], self.srecv.at[pq], r.sib
        ).start()

    def pair(self, k):
        r = self.rows
        pq, _ = r.at(k)
        land = self.sib_buf.at[pq]
        remote(land, land, self.ssend.at[k], self.srecv.at[pq], r.sib).wait_recv()
        return self.part[pq, r.core].astype(F32) + self.sib_buf[pq].astype(F32)

    def pass_on(self, k):
        r = self.rows
        pq, d = r.at(k)
        self.part[pq, r.core] = self.pair(k).astype(BF)
        remote(self.part.at[pq, r.core], self.got.at[r.q], self.send.at[k], self.recv.at[r.q], d).start()

    def take(self, k):
        r = self.rows
        pq, _ = r.at(k)
        land = self.got.at[pq]
        remote(land, land, self.send.at[k], self.recv.at[pq], r.sib).wait_recv()
        return self.got[pq].astype(F32)

    def ready(self):
        r = self.rows
        land = self.sib_buf.at[r.q]
        remote(land, land, self.ssend.at[0], self.srecv.at[r.q], r.sib).wait_recv()
        for k in (1, 2, 3):
            pq, _ = r.at(k)
            land = self.got.at[pq]
            remote(land, land, self.send.at[k], self.recv.at[pq], r.sib).wait_recv()

    def own(self, at):
        r = self.rows
        total = self.part[r.q, r.core, at].astype(F32) + self.sib_buf[r.q, at].astype(F32)
        for k in (1, 2, 3):
            total = total + self.got[r.at(k)[0], at].astype(F32)
        return total

    def finish(self):
        r = self.rows
        land = self.got.at[r.q]
        for k in range(4):
            remote(land, land, self.ssend.at[k], self.srecv.at[r.q], r.sib).wait_send()
            if k:
                remote(land, land, self.send.at[k], self.recv.at[r.q], r.sib).wait_send()


def rec_unit(taps, branch, conv_in, vec, gates, ends, state_ref, a_ref):
    same, conv, r, gate = rec_gates(taps, conv_in, vec, gates, ends)
    log_a = (-DECAY * r) * vec[2:3]
    a = jnp.exp(log_a)
    start = same[0] == 0.0
    a_eff = jnp.where(start, 0.0, a)
    mult = jnp.where(start, 1.0, jnp.sqrt(-jnp.tanh(log_a) * (1.0 + a * a)))
    full_scan(a_eff, mult * gate * conv, state_ref, a_ref, False)
    act, _ = gelu_parts(branch)
    return (state_ref[...] * act).astype(BF)


SMALL_ROWS = 96


def forward_kernel(n, taps, heads, *refs):
    (tok, cot, wb, wi, wo, wg, wu, wd, wr, wig, small) = refs[:11]
    (o_rec, o_mlp, o_gate, o_vec, o_gain, o_ends, o_u, o_grad, pre, state, mixed, resid, o_norm) = refs[11:24]
    (rec, gat, sml, u_buf, og, part, sibb, got, extra, a_scr, gfull) = refs[24:35]
    sems = refs[35:]
    g_sems, r1, r2, s1, (fin, h_send, h_recv) = sems[:48], sems[48:52], sems[52:56], sems[56:60], sems[60:]
    zh, zl, y, x, c = place()
    here = (zh, zl, y, x)
    q, me = zl * 2 + x, dp_at(zh, zl, y, x)
    high = n // 8
    there = plane(zh, zl, y, x, high)
    half, width = tok.shape
    length, blk = pre.shape[1], pre.shape[2] // 2
    ff = wg.shape[1] // 4
    rb, rr = wr.shape[1], wb.shape[0]
    greet(
        [dev(dp_at(h, z, y, w), c) for h, z, w in there[1:]]
        + [dev(dp_at(zh, zl, 1 - y, x), c), dev(me, 1 - c)]
    )

    def whole(ref):
        return ref

    def head_cols(ref):
        return lambda p: ref.at[:, pl.ds(pl.multiple_of(p * blk, 128), blk)]

    def make(i, slot, parts):
        return Gather(slot, parts, g_sems[3 * i : 3 * i + 3], here, there, c)

    smalls = make(0, lambda s, g: sml.at[s], [(lambda p: small, whole)])
    gats, recs, mlps = [], [], []
    for h in range(2):
        pick = (lambda ref: lambda p: ref.at[p]) if h == 0 else (lambda ref: lambda p: ref.at[heads - 1])
        gats.append(
            make(
                1 + h,
                lambda s, g, h=h: gat.at[h, s],
                [
                    (pick(w), lambda r, i=i: r.at[:, pl.ds(i * blk, blk)])
                    for i, w in enumerate((wr, wig))
                ],
            )
        )
    for i, w in enumerate((wb, wi, wo)):
        recs.append(make(3 + i, lambda s, g, i=i: rec.at[0, i, s], [(head_cols(w), whole)]))
    part_rows = rr // 2

    def shared_piece(ref):
        return lambda p: ref.at[
            pl.ds(pl.multiple_of((p % 2) * part_rows, 8), part_rows), pl.ds((heads - 1) * blk, blk)
        ]

    def shared_rows(s, g):
        return rec.at[1, :, s, pl.ds(pl.multiple_of((g % 2) * part_rows, 8), part_rows), :]

    shared = make(
        6, shared_rows, [(shared_piece(w), lambda r, i=i: r.at[i]) for i, w in enumerate((wb, wi, wo))]
    )
    for i, w in enumerate((wg, wu, wd)):
        for t in range(ff // blk):
            piece = lambda p, w=w, t=t: w.at[:, pl.ds(pl.multiple_of(p * ff + t * blk, 128), blk)]
            j = i * (ff // blk) + t
            mlps.append(make(7 + j, lambda s, g, j=j: o_mlp.at[j, s], [(piece, whole)]))
    count = len(there)
    order = [shared, recs[0], gats[0], recs[1], gats[1], recs[2]] + mlps
    ahead = 3
    trickle = []

    def pump(j):
        if j + ahead < len(order):
            order[j + ahead].forward_all(False)
        order[j].forward_all(True)
        for _ in range(3 if j < 6 else 2):
            if trickle:
                trickle.pop(0)()
        if j + ahead < len(order):
            order[j + ahead].start(True)
        if j + 2 * ahead < len(order):
            order[j + 2 * ahead].start(False)

    smalls.start(True)
    smalls.start(False)
    for j in range(2 * ahead):
        if j < ahead:
            order[j].start(True)
        order[j].start(False)

    xin = tok[...].astype(F32)
    unit = xin * lax.rsqrt(jnp.mean(xin * xin, axis=-1, keepdims=True) + EPS)
    resid[...] = unit
    smalls.forward_all(False)
    for j in range(ahead):
        order[j].forward_all(False)
    smalls.forward_all(True)
    pump(0)
    smalls.arrive_all()
    per_vec, per_gain = blk // 128, width // 128
    base = (heads - 1) * 16
    for h in range(2):
        at = pl.multiple_of(q * 16, 16) if h == 0 else base
        groups = [jnp.zeros((16, 128), F32)] * per_vec
        for s in range(n):
            g = s * rb // 128
            groups[g] = groups[g] + sml[s, pl.ds(at, 16), :].astype(F32)
        raw = jnp.concatenate(groups, axis=1)
        decay = raw[2:3]
        o_vec[h, 0:2, :] = raw[0:2]
        o_vec[h, 2:3, :] = jnp.log1p(jnp.exp(-decay))
        o_vec[h, 3:4, :] = jax.nn.sigmoid(-decay)
        o_vec[h, 4 : 5 + taps, :] = raw[3 : 4 + taps]
    groups = [None] * per_gain
    for s in range(n):
        g = s * rr // 128
        v = sml[s, SMALL_ROWS - 16 : SMALL_ROWS, :].astype(F32)
        groups[g] = v if groups[g] is None else groups[g] + v
    for g in range(per_gain):
        o_gain[:, g * 128 : (g + 1) * 128] = groups[g][0:8]
    for j in range(4):
        v = sml[dp_at(zh, j // 2, y, j % 2), SMALL_ROWS - 16 : SMALL_ROWS, :].astype(F32)
        row = jnp.broadcast_to(v[2:3], (8, 128))
        lane = lax.broadcasted_iota(jnp.int32, (8, 128), 1)
        ends = jnp.zeros((8, 128), F32)
        for i in range(4):
            ends = ends + jnp.where(lane >= i, row[:, i : i + 1], 0.0)
        o_ends[j] = ends
    u_rows = Rows(u_buf, r1, here, c)
    g_rows = Rows(o_grad, r2, here, c)
    u_buf[q, c] = (resid[...] * o_gain[0:1, :]).astype(BF)
    trickle += [functools.partial(u_rows.start, p, 8) for p in range(8)]
    e3 = o_ends[q][0:1, 3:4]
    spot = lax.broadcasted_iota(jnp.int32, (half, 1), 0).astype(F32) + (c * half).astype(F32)
    og[...] = jnp.where(spot < e3, cot[...], 0.0).astype(BF)
    own_grad = o_grad.at[q, c]
    place_grad = pltpu.make_async_copy(og, own_grad, fin.at[0])
    place_grad.start()
    place_grad.wait()
    _, beside = u_rows.at(1)

    def exchange(g, first, many):
        rows = rec.at[
            1, :, pl.ds(first, many), pl.ds(pl.multiple_of((g % 2) * part_rows, 8), part_rows), :
        ]
        return remote(rows, rows, h_send, h_recv, beside)

    pump(1)
    shared.arrive_all()
    eighth = n // 8
    trickle += [exchange(q, p * eighth, eighth).start for p in range(8)]
    for j in range(2, 5):
        pump(j)
    for k in (1, 2):
        u_rows.forward(k)
    pump(5)
    while trickle:
        trickle.pop(0)()
    trickle += [functools.partial(g_rows.start, p, 8) for p in range(8)]
    u_rows.forward(3)
    for a in gats + recs:
        a.arrive_all()
    for h in range(2):
        if rb % 16 == 0:
            o_gate[h] = gat[h].reshape(blk, 2 * blk)
        else:
            for s in range(n):
                gfull[s * rb : (s + 1) * rb, :] = gat[h, s].astype(F32)
            o_gate[h] = gfull[...].astype(BF)
    for k in range(4):
        u_rows.arrive(k)
    keep = [pltpu.make_async_copy(rec, o_rec, fin.at[1]), pltpu.make_async_copy(u_buf, o_u, fin.at[2])]
    keep[1].start()

    sums = Sums(part, sibb, got, s1, u_rows)

    def step(i, carry):
        h = i // 4
        k = ((i + 1) % 4) * ((7 - i) // 4)
        pq, _ = u_rows.at(k)
        at = pq + h * (4 - pq)

        @pl.when(i == 4)
        def _():
            exchange(q + 1, 0, n).wait_recv()
            keep[0].start()

        rows = u_buf[pq].reshape(2 * half, width)
        for j in range(2):
            w = rec[h, j].reshape(width, blk)
            pre[at, :, j * blk : (j + 1) * blk] = mm(rows, w)
        mx = rec_unit(
            taps, pre[at, :, :blk], pre[at, :, blk:], o_vec[h], o_gate[h], o_ends[pq][0:1, :], state.at[at], a_scr
        )
        mixed[at] = mx
        per = 512 // rr if rr <= 512 else 1

        def cols_out(t, carry):
            w = rec[h, 2, pl.ds(t * per, per)].reshape(per * rr, blk)
            tile = mm_t(mx, w)
            lanes = pl.ds(pl.multiple_of(t * (per * rr), 128), per * rr)
            tile = tile + jnp.where(i == 4, extra[:, lanes], 0.0)

            @pl.when(i == 3)
            def _():
                extra[:, lanes] = tile

            @pl.when(i != 3)
            def _():
                part[pq, 0, :, lanes] = tile[:half].astype(BF)
                part[pq, 1, :, lanes] = tile[half:].astype(BF)

            return carry

        lax.fori_loop(0, width // (per * rr), cols_out, 0)

        @pl.when(i != 3)
        def _():
            sums.push(k)

        @pl.when((i > 0) & (i < 4))
        def _():
            sums.pass_on(i)

        for j in range(4):

            @pl.when(i == j)
            def _():
                pump(6 + j)

        return carry

    extra[...] = jnp.zeros_like(extra)
    lax.fori_loop(0, 5, step, 0)
    pump(10)
    pump(11)
    for k in (1, 2):
        g_rows.forward(k)
    sums.ready()

    def finish(i, carry):
        at = pl.ds(pl.multiple_of(i * 32, 32), 32)
        total = tok[at, :].astype(F32) + sums.own(at)
        resid[at, :] = total
        unit = total * lax.rsqrt(jnp.mean(total * total, axis=-1, keepdims=True) + EPS)
        o_norm[at, :] = (unit * o_gain[1:2, :]).astype(BF)
        return carry

    lax.fori_loop(0, half // 32, finish, 0)
    pump(12)
    pump(13)
    g_rows.forward(3)
    for j in range(14, len(order)):
        pump(j)
    for a in mlps:
        a.arrive_all()
    for k in range(4):
        g_rows.arrive(k)
    exchange(q, 0, n).wait_send()
    for a in [smalls, shared] + mlps + gats + recs + [u_rows, g_rows, sums]:
        a.finish()
    for cp in keep:
        cp.wait()


def forward(tok, cot, wb, wi, wo, wg, wu, wd, wr, wig, small, n, taps, cid):
    half, width = tok.shape
    heads, rb, blk = wr.shape
    rr = wb.shape[0]
    length = 2 * half
    ff = wg.shape[1] // 4
    vm = pl.BlockSpec(memory_space=pltpu.VMEM)
    hb = pl.BlockSpec(memory_space=pl.ANY)

    def sds(*shape, t=F32):
        return jax.ShapeDtypeStruct(shape, t)

    unit = sds(5, length, blk)
    outs = (
        (sds(2, 3, n, rr, blk, t=BF), hb),
        (sds(3 * ff // blk, n, rr, blk, t=BF), hb),
        (sds(2, blk, 2 * blk, t=BF), vm),
        (sds(2, 16, blk), vm),
        (sds(8, width), vm),
        (sds(4, 8, 128), vm),
        (sds(4, 2, half, width, t=BF), hb),
        (sds(4, 2, half, width, t=BF), hb),
        (sds(5, length, 2 * blk), vm),
        (unit, vm),
        (sds(5, length, blk, t=BF), vm),
        (sds(half, width), vm),
        (sds(half, width, t=BF), vm),
    )
    count = n // 2
    return pl.pallas_call(
        functools.partial(forward_kernel, n, taps, heads),
        out_shape=tuple(o for o, _ in outs),
        in_specs=[vm, vm] + [hb] * 9,
        out_specs=[s for _, s in outs],
        scratch_shapes=[
            pltpu.VMEM((2, 3, n, rr, blk), BF),
            pltpu.VMEM((2, n, rb, 2 * blk), BF),
            pltpu.VMEM((n, SMALL_ROWS, 128), BF),
            pltpu.VMEM((4, 2, half, width), BF),
            pltpu.VMEM((half, width), BF),
            pltpu.VMEM((4, 2, half, width), BF),
            pltpu.VMEM((4, half, width), BF),
            pltpu.VMEM((4, half, width), BF),
            pltpu.VMEM((length, width), F32),
            pltpu.VMEM((length, blk), F32),
            pltpu.VMEM((blk, 2 * blk), F32),
        ]
        + [
            pltpu.SemaphoreType.DMA((count,)),
            pltpu.SemaphoreType.DMA((n,)),
            pltpu.SemaphoreType.DMA((count,)),
        ]
        * 16
        + row_sems() * 3
        + [pltpu.SemaphoreType.DMA((3,)), pltpu.SemaphoreType.DMA, pltpu.SemaphoreType.DMA],
        compiler_params=pltpu.CompilerParams(
            collective_id=cid, has_side_effects=True, vmem_limit_bytes=VMEM_LIMIT
        ),
        name="forward",
    )(tok, cot, wb, wi, wo, wg, wu, wd, wr, wig, small)


def mlp_kernel(norm, resid, gain, cot, ends, w_hbm, mg_hbm, g_hbm, o_rec, o_rgrad, o_hid, o_gain,
               w, nbuf, mg, hg, hu, gbuf, part, sibb, got, wsem, msem, gsem, *sems):
    zh, zl, y, x, c = place()
    here = (zh, zl, y, x)
    q, me = zl * 2 + x, dp_at(zh, zl, y, x)
    half, width = norm.shape
    nt, n, rr, blk = w.shape
    tiles, steps, per = nt // 3, width // blk, blk // rr
    rows = Rows(nbuf, sems[:4], here, c)
    sums = Sums(part, sibb, got, sems[4:8], rows)
    greet([dev(me, 1 - c)] + [rows.at(k)[1] for k in (1, 2, 3)])
    nbuf[q, c] = norm[...]
    rows.start()
    loads = []
    for t in range(tiles):
        for i in range(3):
            j = i * tiles + t
            loads.append((t, pltpu.make_async_copy(w_hbm.at[j], w.at[j], wsem.at[j])))
    loads.insert(2, (0, pltpu.make_async_copy(mg_hbm, mg, msem)))
    for _, cp in loads:
        cp.start()

    def row(k, carry):
        pq, _ = rows.at(k)
        rows.arrive(k)

        def first(t, carry):
            @pl.when(k == 0)
            def _():
                for j, cp in loads:

                    @pl.when(t == j)
                    def _():
                        cp.wait()

            a = nbuf[pq].reshape(2 * half, width)
            gate = mm(a, w[t].reshape(width, blk))
            up = mm(a, w[tiles + t].reshape(width, blk))
            grad = mm(mg[pq].reshape(2 * half, width), w[2 * tiles + t].reshape(width, blk))
            act, der = gelu_parts(gate)
            o_hid[t, pq] = (act * up).astype(BF)
            hg[t, pq] = (grad * up * der).astype(BF)
            hu[t, pq] = (grad * act).astype(BF)
            return carry

        lax.fori_loop(0, tiles, first, 0)

        @pl.when(k < 3)
        def _():
            rows.forward(k + 1)

        @pl.when(k > 1)
        def _():
            sums.pass_on(k - 1)

        def second(d, carry):
            total = jnp.zeros((2 * half, blk), F32)
            for t in range(tiles):
                total = total + mm_t(hg[t, pq], w[t, pl.ds(d * per, per)].reshape(blk, blk))
                total = total + mm_t(hu[t, pq], w[tiles + t, pl.ds(d * per, per)].reshape(blk, blk))
            lanes = pl.ds(pl.multiple_of(d * blk, 128), blk)
            part[pq, 0, :, lanes] = total[:half].astype(BF)
            part[pq, 1, :, lanes] = total[half:].astype(BF)
            return carry

        lax.fori_loop(0, steps, second, 0)
        sums.push(k)
        return carry

    def rows_from(k, carry):
        return row(k, carry)

    lax.fori_loop(0, 4, rows_from, 0)
    sums.pass_on(3)

    def out_tile(d):
        at = pl.ds(d * per, per)
        return pltpu.make_async_copy(gbuf.at[:, at], g_hbm.at[:, at], gsem.at[d])

    def grads(d, carry):
        lanes = pl.ds(pl.multiple_of(d * blk, 128), blk)
        nt_ = nbuf[:, :, :, lanes].reshape(8 * half, blk).T
        mt_ = mg[:, :, :, lanes].reshape(8 * half, blk).T
        for i, (left, right) in enumerate(((nt_, hg), (nt_, hu), (mt_, o_hid))):
            for t in range(tiles):
                tile = mm(left, right[t].reshape(8 * half, blk))
                gbuf[i * tiles + t, pl.ds(d * per, per)] = tile.astype(BF).reshape(per, rr, blk)
        out_tile(d).start()
        return carry

    lax.fori_loop(0, steps, grads, 0)
    sums.ready()
    e3 = ends[q][0:1, 3:4]

    def finish(i, acc):
        at = pl.ds(pl.multiple_of(i * 32, 32), 32)
        total, r = sums.own(at), resid[at, :]
        scale = lax.rsqrt(jnp.mean(r * r, axis=-1, keepdims=True) + EPS)
        unit = r * scale
        g2 = total * gain[1:2, :]
        back = scale * (g2 - unit * jnp.mean(g2 * unit, axis=-1, keepdims=True))
        spot = lax.broadcasted_iota(jnp.int32, (32, 1), 0) + (c * half + i * 32)
        back = back + jnp.where(spot.astype(F32) < e3, cot[at, :], 0.0)
        o_rgrad[at, :] = back
        o_rec[at, :] = back.astype(BF)
        return acc + jnp.sum(total * unit, axis=0, keepdims=True)

    gsum = lax.fori_loop(0, half // 32, finish, jnp.zeros((1, width), F32))
    o_gain[...] = jnp.broadcast_to(gsum, o_gain.shape)
    for d in range(steps):
        out_tile(d).wait()
    rows.finish()
    sums.finish()


def mlp_block(norm, resid, gain, cot, ends, mlp_w, mlp_grad, cid):
    half, width = norm.shape
    nt, n, rr, blk = mlp_w.shape
    tiles = nt // 3
    vm = pl.BlockSpec(memory_space=pltpu.VMEM)
    hb = pl.BlockSpec(memory_space=pl.ANY)
    hid = (tiles, 4, 2 * half, blk)
    return pl.pallas_call(
        mlp_kernel,
        out_shape=(
            jax.ShapeDtypeStruct(mlp_w.shape, BF),
            jax.ShapeDtypeStruct((half, width), BF),
            jax.ShapeDtypeStruct((half, width), F32),
            jax.ShapeDtypeStruct(hid, BF),
            jax.ShapeDtypeStruct((8, width), F32),
        ),
        in_specs=[vm] * 5 + [hb] * 2,
        out_specs=[hb] + [vm] * 4,
        scratch_shapes=[
            pltpu.VMEM(mlp_w.shape, BF),
            pltpu.VMEM((4, 2, half, width), BF),
            pltpu.VMEM((4, 2, half, width), BF),
            pltpu.VMEM(hid, BF),
            pltpu.VMEM(hid, BF),
            pltpu.VMEM(mlp_w.shape, BF),
            pltpu.VMEM((4, 2, half, width), BF),
            pltpu.VMEM((4, half, width), BF),
            pltpu.VMEM((4, half, width), BF),
            pltpu.SemaphoreType.DMA((nt,)),
            pltpu.SemaphoreType.DMA,
            pltpu.SemaphoreType.DMA((width // blk,)),
        ]
        + row_sems() * 2,
        compiler_params=pltpu.CompilerParams(
            collective_id=cid, has_side_effects=True, vmem_limit_bytes=VMEM_LIMIT
        ),
        name="mlp_block",
    )(norm, resid, gain, cot, ends, mlp_w, mlp_grad)


class Scatter:
    def __init__(self, away, both, mine, pair, landed, sems, here, there, core):
        self.away, self.both, self.mine, self.pair, self.landed = away, both, mine, pair, landed
        self.ysend, self.yrecv, self.send, self.recv = sems
        zh, zl, y, x = here
        self.core = core
        self.own = zh * 4 + zl * 2 + x
        self.places = [(h * 4 + z * 2 + w, dp_at(h, z, y, w)) for h, z, w in (*there[4:], *there[1:4], there[0])]
        self.other = dev(dp_at(zh, zl, 1 - y, x), core)

    def start(self):
        remote(self.away, self.both, self.ysend, self.yrecv, self.other).start()

    def pass_on(self):
        last = len(self.places) - 1
        remote(self.away, self.both, self.ysend, self.yrecv, self.other).wait_recv()
        for i, (j, near) in enumerate(self.places):
            slot = self.pair(j)
            slot[...] = (self.mine(near).astype(F32) + slot[...].astype(F32)).astype(slot.dtype)
            if i == last:
                pltpu.make_async_copy(slot, self.landed(self.own), self.send.at[j]).start()
            else:
                remote(
                    slot, self.landed(self.own), self.send.at[j], self.recv.at[self.own], dev(near, self.core)
                ).start()

    def collect(self):
        last = len(self.places) - 1
        remote(self.away, self.both, self.ysend, self.yrecv, self.other).wait_send()
        for i, (j, _) in enumerate(self.places):
            slot, land = self.pair(j), self.landed(j)
            if i == last:
                pltpu.make_async_copy(land, land, self.send.at[j]).wait()
            else:
                remote(land, land, self.send.at[j], self.recv.at[j], self.other).wait_recv()
                remote(slot, slot, self.send.at[j], self.recv.at[j], self.other).wait_send()


def scatter_sems(high):
    return [pltpu.SemaphoreType.DMA, pltpu.SemaphoreType.DMA] + [pltpu.SemaphoreType.DMA((high * 4,))] * 2


def rec_gates(taps, conv_in, vec, gates, ends):
    length, blk = conv_in.shape
    same = segments(ends, length, blk, taps)
    conv = conv_in * vec[4:5] + vec[4 + taps : 5 + taps]
    for k in range(1, taps):
        conv = conv + pltpu.roll(conv_in, k, 0) * same[k - 1] * vec[4 + k : 5 + k]
    pre = jnp.dot(conv.astype(BF), gates, preferred_element_type=F32)
    r = jax.nn.sigmoid(pre[:, :blk] + vec[0:1])
    gate = jax.nn.sigmoid(pre[:, blk:] + vec[1:2])
    return same, conv, r, gate


def rec_unit_back(taps, branch, conv_in, vec, gates, ends, state, mg, carry_ref, a_ref):
    length, blk = branch.shape
    same, conv, r, gate = rec_gates(taps, conv_in, vec, gates, ends)
    start = same[0] == 0.0
    act, der = gelu_parts(branch)
    branch_low = (mg * state * der).astype(BF)
    log_a = (-DECAY * r) * vec[2:3]
    a = jnp.exp(log_a)
    a_eff = jnp.where(start, 0.0, a)
    row = lax.broadcasted_iota(jnp.int32, (length, blk), 0)
    a_next = jnp.where(row < length - 1, pltpu.roll(a_eff, length - 1, 0), 0.0)
    full_scan(a_next, mg * act, carry_ref, a_ref, True)
    carry = carry_ref[...]
    prev = jnp.where(row > 0, pltpu.roll(state, 1, 0), 0.0)
    raw = jnp.sqrt(-jnp.tanh(log_a) * (1.0 + a * a))
    mult = jnp.where(start, 1.0, raw)
    log_grad = jnp.where(start, 0.0, carry * prev * a - carry * gate * conv * (a * a) / raw)
    r_grad = log_grad * (-DECAY * vec[2:3]) * (r * (1.0 - r))
    i_grad = carry * mult * conv * (gate * (1.0 - gate))
    pre_low = jnp.concatenate([r_grad.astype(BF), i_grad.astype(BF)], axis=1)
    conv_grad = carry * mult * gate + mm_t(pre_low, gates)
    gate_grads = t_mm(conv.astype(BF), pre_low)

    def total(v):
        return jnp.sum(v, axis=0, keepdims=True)

    sums = [total(r_grad), total(i_grad), total(log_grad * (DECAY * r) * vec[3:4]), total(conv_grad)]
    inp = conv_grad * vec[4:5]
    sums.append(total(conv_grad * conv_in))
    for k in range(1, taps):
        masked = conv_grad * same[k - 1]
        sums.append(total(masked * pltpu.roll(conv_in, k, 0)))
        inp = inp + pltpu.roll(masked, length - k, 0) * vec[4 + k : 5 + k]
    return branch_low, inp.astype(BF), gate_grads, jnp.concatenate(sums, axis=0)


def backward_kernel(n, taps, *refs):
    (tok, rgrad, resid, gain, gsum2, ends, vec, gates, pre, state, mixed) = refs[:11]
    (rec_own, hid, g_hbm, rec_hbm, mlp_hbm, u_hbm) = refs[11:17]
    (o_res, o_tok, l_mlp, l_rec, l_sh, l_gate, l_small) = refs[17:24]
    (rec, ub, rg, part, sib1, got1, low, grec, gsh, gshin, g_own, y_mlp, y_rec, y_sh, a_scr, c_scr,
     gg, vg, ggl, y_gate, sml, sml_sib, y_sml) = refs[24:47]
    sems = refs[47:]
    zh, zl, y, x, c = place()
    here = (zh, zl, y, x)
    q, me = zl * 2 + x, dp_at(zh, zl, y, x)
    high = n // 8
    there = plane(zh, zl, y, x, high)
    half, width = tok.shape
    length = 2 * half
    blk = mixed.shape[2]
    rr = width // n
    rb = blk // n
    nt = g_own.shape[0]
    per, steps = blk // rr, width // blk
    taken = [0]

    def some(k):
        taken[0] += k
        return sems[taken[0] - k : taken[0]]

    rows = Rows(rg, some(4), here, c)
    sums1 = Sums(part, sib1, got1, some(4), rows)
    sums2 = Sums(part, sib1, got1, some(4), rows)
    (loads,) = some(1)
    greet(
        [dev(dp_at(h, z, y, w), c) for h, z, w in there[1:]]
        + [dev(dp_at(zh, zl, 1 - y, x), c), dev(me, 1 - c)]
    )
    first = pltpu.make_async_copy(rec_own, rg.at[q, c], loads.at[0])
    first.start()
    first.wait()
    rows.start()
    grab = [
        pltpu.make_async_copy(rec_hbm, rec, loads.at[0]),
        pltpu.make_async_copy(u_hbm, ub, loads.at[1]),
        pltpu.make_async_copy(g_hbm.at[:, :, y], g_own, loads.at[2]),
    ]
    for cp in grab:
        cp.start()

    tiles = nt // 3

    def cols_at(i):
        return pl.ds(pl.multiple_of(i * blk, 128), blk)

    def chunk(i, sem):
        return Scatter(
            g_hbm.at[i, :, 1 - y],
            y_mlp.at[i],
            lambda s: g_own[i, s // 4, s % 2],
            lambda j: y_mlp.at[i, j // 2, j % 2],
            lambda j: l_mlp.at[j // 4, i // tiles, :, cols_at((j % 4) * tiles + i % tiles)],
            sem, here, there, c,
        )

    mlps = [chunk(i, some(4)) for i in range(nt)]
    for a in mlps[:3]:
        a.start()
    recs = [
        Scatter(
            grec.at[i, :, 1 - y],
            y_rec.at[i],
            lambda s, i=i: grec[i, s // 4, (s // 2) % 2, s % 2],
            lambda j, i=i: y_rec.at[i, j // 2, j % 2],
            lambda j, i=i: l_rec.at[j // 4, i, :, cols_at(j % 4)],
            some(4), here, there, c,
        )
        for i in range(3)
    ]
    part_rows = rr // 2

    shared = Scatter(
        gshin.at[:, :, 1 - y],
        y_sh,
        lambda s: gshin[:, s // 4, (s // 2) % 2, s % 2],
        lambda j: y_sh.at[:, j // 2, j % 2],
        lambda j: l_sh.at[j // 2, :, pl.ds(pl.multiple_of((j % 2) * part_rows, 8), part_rows), :],
        some(4), here, there, c,
    )
    gate_sc = Scatter(
        ggl.at[:, :, 1 - y],
        y_gate,
        lambda s: ggl[:, s // 4, (s // 2) % 2, s % 2],
        lambda j: y_gate.at[:, j // 2, j % 2],
        lambda j: l_gate.at[j],
        some(4), here, there, c,
    )
    h_send, h_recv, s_send, s_recv, z_send, z_recv, m_send, m_recv, again = some(9)
    order = mlps + [shared] + recs + [gate_sc]
    trickle = []
    _, beside = rows.at(1)
    eighth = n // 16

    def pump(j):
        order[j].pass_on()
        for _ in range(2 if j else 0):
            if trickle:
                trickle.pop(0)()
        if j + 3 < len(order):
            order[j + 3].start()

    gg[...] = jnp.zeros_like(gg)
    vg[...] = jnp.zeros_like(vg)
    grab[0].wait()

    def exchange(first, many):
        there_rows = pl.ds(pl.multiple_of((1 - x) * part_rows, 8), part_rows)
        cut = pl.ds(first, many)
        return remote(gsh.at[:, cut, :, :, there_rows, :], gshin.at[:, cut], h_send, h_recv, beside)

    def store(ref, i, d, tile):
        tile = tile.astype(BF)
        if per == 2:
            ref[i, d // 2, d % 2] = tile.reshape(2, rr, blk)
        else:
            ref[i, pl.ds(d * (per // 4), per // 4)] = tile.reshape(per // 4, 2, 2, rr, blk)

    def shared_grads(d, carry):
        lanes = pl.ds(pl.multiple_of(d * blk, 128), blk)
        uo = ub[q, :, :, lanes].reshape(length, blk).T
        ro = rg[q, :, :, lanes].reshape(length, blk).T
        for i in range(3):
            own = low[4, :, i * blk : (i + 1) * blk] if i < 2 else mixed[4]
            store(gsh, i, d, mm(uo if i < 2 else ro, own))
        return carry

    trickle += [exchange(p * eighth, eighth).start for p in range(4)]

    def step(i, carry):
        h = jnp.where(i == 1, 1, 0)
        k = jnp.maximum(i - 1, 0)
        pq, _ = rows.at(k)
        at = pq + h * (4 - pq)

        @pl.when(i != 1)
        def _():
            rows.arrive(k)

        mg = mm(rg[pq].reshape(length, width), rec[h, 2].reshape(width, blk))

        @pl.when((i > 0) & (i < 4))
        def _():
            rows.forward(k + 1)

        b_low, i_low, g_add, v_add = rec_unit_back(
            taps, pre[at, :, :blk], pre[at, :, blk:], vec[h], gates[h], ends[pq][0:1, :], state[at], mg, c_scr, a_scr,
        )
        low[at, :, :blk], low[at, :, blk:] = b_low, i_low
        gg[h] += g_add
        vg[h] += v_add

        @pl.when(i > 2)
        def _():
            sums1.pass_on(k - 1)

        def cols_out(t, carry):
            cut = pl.ds(t * per, per)
            lanes = pl.ds(pl.multiple_of(t * blk, 128), blk)

            def tile_of(left, head):
                return sum(
                    mm_t(left[:, j * blk : (j + 1) * blk], rec[head, j, cut].reshape(blk, blk)) for j in range(2)
                )

            def emit(tile):
                part[pq, 0, :, lanes] = tile[:half].astype(BF)
                part[pq, 1, :, lanes] = tile[half:].astype(BF)

            @pl.when(i == 1)
            def _():
                emit(tile_of(low[4], 1) + tile_of(low[pq], 0))

            @pl.when(i > 1)
            def _():
                emit(tile_of(low[pq], 0))

            return carry

        @pl.when(i > 0)
        def _():
            lax.fori_loop(0, steps, cols_out, 0)

        @pl.when(i > 0)
        def _():
            sums1.push(k)

        for j in range(5):

            @pl.when(i == j)
            def _():
                if j == 0:
                    grab[2].wait()
                if j == 1:
                    grab[1].wait()
                    lax.fori_loop(0, steps, shared_grads, 0)
                pump(j)

        return carry

    lax.fori_loop(0, 5, step, 0)
    sums1.pass_on(3)
    for h in range(2):
        for s in range(n):
            ggl[h, s // 4, (s // 2) % 2, s % 2] = gg[h, s * rb : (s + 1) * rb, :].astype(BF)
    fetch = pltpu.make_async_copy(mlp_hbm.at[pl.ds(2 * (nt // 3), nt // 3)], rec.at[0], loads.at[0])
    fetch.start()
    pump(5)

    def grads(d, carry):
        lanes = pl.ds(pl.multiple_of(d * blk, 128), blk)
        ut = ub[:, :, :, lanes].reshape(4 * length, blk).T
        rt = rg[:, :, :, lanes].reshape(4 * length, blk).T
        for i in range(3):
            if i < 2:
                right = low[0:4, :, i * blk : (i + 1) * blk].reshape(4 * length, blk)
            else:
                right = mixed[0:4].reshape(4 * length, blk)
            store(grec, i, d, mm(ut if i < 2 else rt, right))
        return carry

    lax.fori_loop(0, steps, grads, 0)
    exchange(0, n // 4).wait()
    for s in range(n // 4):
        gshin[:, s] = (
            gshin[:, s].astype(F32)
            + gsh[:, s, :, :, pl.ds(pl.multiple_of(x * part_rows, 8), part_rows), :].astype(F32)
        ).astype(BF)
    per_row = length // rr
    fetch_hid = pltpu.make_async_copy(hid, gsh.at[:, pl.ds(0, per_row)], loads.at[1])
    fetch_hid.start()
    pump(6)

    sums1.ready()

    def finish(i, acc):
        at = pl.ds(pl.multiple_of(i * 32, 32), 32)
        total, xin = sums1.own(at), tok[at, :].astype(F32)
        scale = lax.rsqrt(jnp.mean(xin * xin, axis=-1, keepdims=True) + EPS)
        unit = xin * scale
        g1 = total * gain[0:1, :]
        o_tok[at, :] = rgrad[at, :] + scale * (g1 - unit * jnp.mean(g1 * unit, axis=-1, keepdims=True))
        return acc + jnp.sum(total * unit, axis=0, keepdims=True)

    gsum1 = lax.fori_loop(0, half // 32, finish, jnp.zeros((1, width), F32))
    sums1.finish()
    for d in [rows.sib] + [rows.at(k)[1] for k in (1, 2, 3)]:
        pl.semaphore_signal(again, inc=1, device_id=d, device_id_type=MESH)
    for h in range(2):
        sml[8 * h : 8 * h + 8, :] = vg[h]
    for i in range(steps):
        sml[16 + i : 17 + i, :] = gsum1[:, i * blk : (i + 1) * blk]
        sml[16 + steps + i : 17 + steps + i, :] = gsum2[0:1, i * blk : (i + 1) * blk]
    gain_rows = sml.at[pl.ds(16, 2 * steps)]
    with_sib = remote(gain_rows, sml_sib, s_send, s_recv, rows.sib)
    with_sib.start()
    pump(7)

    fetch.wait()
    fetch_hid.wait()

    pl.semaphore_wait(again, 4)

    def hid_rows(t, row):
        if per_row == 2:
            return gsh[t, row // 2, row % 2].reshape(length, blk)
        return gsh[t, pl.ds(row * (per_row // 4), per_row // 4)].reshape(length, blk)

    def out_rows(i, carry):
        k = (i + 1) % 4
        pq, _ = rows.at(k)

        def cols_out(d, carry):
            tile = jnp.zeros((length, blk), F32)
            for t in range(nt // 3):
                left = hid_rows(t, pq)
                tile = tile + mm_t(left, rec[0, t, pl.ds(d * per, per)].reshape(blk, blk))
            lanes = pl.ds(pl.multiple_of(d * blk, 128), blk)
            part[pq, 0, :, lanes] = tile[:half].astype(BF)
            part[pq, 1, :, lanes] = tile[half:].astype(BF)
            return carry

        lax.fori_loop(0, steps, cols_out, 0)
        sums2.push(k)

        @pl.when(i > 0)
        def _():
            sums2.pass_on(i)

        return carry

    lax.fori_loop(0, 4, out_rows, 0)
    pump(8)
    with_sib.wait()
    sml[16 : 16 + 2 * steps, :] += sml_sib[...]
    with_y = remote(sml, y_sml, z_send, z_recv, dev(dp_at(zh, zl, 1 - y, x), c))
    with_y.start()
    pump(9)
    pump(10)
    with_y.wait()
    sml[...] = sml[...] + y_sml[...]
    mine = zh * 4 + q
    small_out = []
    for i, (h, z, w) in enumerate(there):
        if i == 0:
            cp = pltpu.make_async_copy(sml, l_small.at[mine], m_send.at[i])
        else:
            cp = remote(sml, l_small.at[mine], m_send.at[i], m_recv.at[mine], dev(dp_at(h, z, y, w), c))
        cp.start()
        small_out.append(cp)
    pump(11)
    sums2.ready()
    e3 = ends[q][0:1, 3:4]

    def result(i, carry):
        at = pl.ds(pl.multiple_of(i * 32, 32), 32)
        spot = lax.broadcasted_iota(jnp.int32, (32, 1), 0) + (c * half + i * 32)
        o_res[at, :] = jnp.where(spot.astype(F32) < e3, resid[at, :] + sums2.own(at), 0.0).astype(BF)
        return carry

    lax.fori_loop(0, half // 32, result, 0)
    sums2.finish()
    pump(12)
    pump(13)
    rows.finish()
    for a in mlps + recs + [gate_sc, shared]:
        a.collect()
    for i, (h, z, w) in enumerate(there):
        if i == 0:
            small_out[i].wait()
        else:
            j = h * 4 + z * 2 + w
            land = l_small.at[j]
            remote(land, land, m_send.at[i], m_recv.at[j], rows.sib).wait_recv()
            small_out[i].wait_send()


def backward(tok, rec_own, rgrad, resid, gain, gsum2, ends, vec, gates, saved, hid, g_mlp, rec_w, mlp_w, u, n, taps, cid):
    half, width = tok.shape
    pre, state, mixed = saved
    blk = mixed.shape[2]
    length = 2 * half
    rr, rb, high = width // n, blk // n, n // 8
    nt = g_mlp.shape[0]
    slots = high * 4
    vm = pl.BlockSpec(memory_space=pltpu.VMEM)
    hb = pl.BlockSpec(memory_space=pl.ANY)
    g_view = g_mlp.reshape(nt, n // 4, 2, 2, rr, blk)
    hid = hid.reshape(nt // 3, length // rr, 2, 2, rr, blk)
    small_rows = 16 + 2 * (width // blk)

    def sds(*shape, t=BF):
        return jax.ShapeDtypeStruct(shape, t)

    def v(*shape, t=BF):
        return pltpu.VMEM(shape, t)

    dma = pltpu.SemaphoreType.DMA
    return pl.pallas_call(
        functools.partial(backward_kernel, n, taps),
        out_shape=(
            sds(half, width),
            sds(half, width, t=F32),
            sds(high, 3, rr, 4 * (nt // 3) * blk),
            sds(high, 3, rr, 4 * blk),
            sds(slots // 2, 3, rr, blk),
            sds(slots, 2, rb, 2 * blk),
            sds(slots, small_rows, blk, t=F32),
        ),
        in_specs=[vm] * 11 + [hb] * 6,
        out_specs=[vm, vm] + [hb] * 5,
        scratch_shapes=[
            v(2, 3, n, rr, blk),
            v(4, 2, half, width),
            v(4, 2, half, width),
            v(4, 2, half, width),
            v(4, half, width),
            v(4, half, width),
            v(5, length, 2 * blk),
            v(3, n // 4, 2, 2, rr, blk),
            v(3, n // 4, 2, 2, rr, blk),
            v(3, n // 4, 2, 2, rr // 2, blk),
            v(nt, n // 4, 2, rr, blk),
            v(nt, n // 4, 2, rr, blk),
            v(3, n // 4, 2, rr, blk),
            v(3, n // 4, 2, rr // 2, blk),
            v(length, blk, t=F32),
            v(length, blk, t=F32),
            v(2, blk, 2 * blk, t=F32),
            v(2, 4 + taps, blk, t=F32),
            v(2, n // 4, 2, 2, rb, 2 * blk),
            v(2, n // 4, 2, rb, 2 * blk),
            v(small_rows, blk, t=F32),
            v(small_rows - 16, blk, t=F32),
            v(small_rows, blk, t=F32),
        ]
        + row_sems() * 3
        + [dma((4,))]
        + scatter_sems(high) * (nt + 5)
        + [dma, dma, dma, dma, dma, dma, dma((slots,)), dma((slots,)), pltpu.SemaphoreType.REGULAR],
        compiler_params=pltpu.CompilerParams(
            collective_id=cid, has_side_effects=True, vmem_limit_bytes=VMEM_LIMIT
        ),
        name="backward",
    )(tok, rgrad, resid, gain, gsum2, ends, vec, gates, *saved, rec_own, hid, g_view, rec_w, mlp_w, u)


def mm(a, b):
    return jnp.dot(a, b, preferred_element_type=F32)


def mm_t(a, b):
    return lax.dot_general(a, b, (((1,), (1,)), ((), ())), preferred_element_type=F32)


def t_mm(a, b):
    return lax.dot_general(a, b, (((0,), (0,)), ((), ())), preferred_element_type=F32)


def local(
    tokens, doc_lengths, rec_gain, w_branch, w_input, w_rgate, w_igate, rgate_bias, igate_bias,
    decay_param, conv_weight, conv_bias, w_output, mlp_gain, w_gate, w_up, w_down, cotangent,
):
    n = lax.axis_size("dp")
    zh, zl, y, x, c = place()
    q = zl * 2 + x
    _, half, width = tokens.shape
    length = half * 2
    heads, rb, blk = w_rgate.shape
    taps = conv_weight.shape[0]
    rows = w_branch.shape[0]
    ff = w_gate.shape[1] // 4

    dp = lax.axis_index("dp")

    def lanes(v, per):
        v = v.astype(BF).reshape(-1, per)
        at = (dp * per) % 128
        return lax.dynamic_update_slice(jnp.zeros((v.shape[0], 128), BF), v, (0, at))

    params = jnp.concatenate(
        [rgate_bias[None], igate_bias[None], decay_param[None], conv_weight, conv_bias[None]], axis=0
    ).transpose(1, 0, 2)
    params = jnp.pad(params, ((0, 0), (0, 16 - params.shape[1]), (0, 0))).reshape(heads * 16, rb)
    lens_own = jnp.pad(doc_lengths.astype(BF), ((0, 13), (0, 124)))
    small = jnp.concatenate([lanes(params, rb), lanes(jnp.stack([rec_gain, mlp_gain]), rows), lens_own], axis=0)
    (
        rec_w, mlp_w, gates, vec, gains_all, group_ends, u, mlp_grad, pre, state, mixed, resid, norm_own,
    ) = forward(
        tokens[0], cotangent[0], w_branch, w_input, w_output.T, w_gate, w_up, w_down.T, w_rgate, w_igate, small, n, taps, 1,
    )
    g_mlp, rec_own, resid_grad, hid, gain2_sum = mlp_block(
        norm_own, resid, gains_all, cotangent[0], group_ends, mlp_w, mlp_grad, 4
    )
    result, token_grad, l_mlp, l_rec, l_sh, l_gate, l_small = backward(
        tokens[0], rec_own, resid_grad, resid, gains_all, gain2_sum, group_ends, vec, gates,
        (pre, state, mixed), hid, g_mlp, rec_w, mlp_w, u, n, taps, 5,
    )
    high = n // 8

    def owned(a):
        return jnp.sum(a.reshape((high, 4) + a.shape[1:]).astype(F32), axis=0)

    def add(a):
        return jnp.sum(a.astype(F32), axis=0)

    o_mlp = [add(l_mlp[:, i]) for i in range(3)]
    o_rec = [jnp.concatenate([add(l_rec[:, i]), add(l_sh[:, i])], axis=1) for i in range(3)]
    o_gate = owned(l_gate)
    o_gate = jnp.concatenate([o_gate[:, 0], jnp.sum(o_gate[:, 1], axis=0, keepdims=True)], axis=0)
    o_small = owned(l_small)
    at = dp * rb
    o_vec = jnp.concatenate([o_small[:, :8], jnp.sum(o_small[:, 8:16], axis=0, keepdims=True)], axis=0)
    o_vec = lax.dynamic_slice_in_dim(o_vec, at, rb, 2)
    o_gain = jnp.sum(o_small[:, 16:], axis=0).reshape(2, width)
    o_gain = lax.dynamic_slice_in_dim(o_gain, dp * rows, rows, 1)
    return (
        result[None],
        token_grad[None],
        o_gain[0],
        o_rec[0],
        o_rec[1],
        o_gate[:, :, :blk],
        o_gate[:, :, blk:],
        o_vec[:, 0],
        o_vec[:, 1],
        o_vec[:, 2],
        o_vec[:, 4 : 4 + taps].transpose(1, 0, 2),
        o_vec[:, 3],
        o_rec[2].T,
        o_gain[1],
        o_mlp[0],
        o_mlp[1],
        o_mlp[2].T,
    )


def solution(mesh):
    return jax.shard_map(
        local,
        mesh=mesh,
        in_specs=(
            P("dp", "tensor", None),
            P("dp", None),
            P("dp"),
            P("dp", "tensor"),
            P("dp", "tensor"),
            P("tensor", "dp", None),
            P("tensor", "dp", None),
            P("tensor", "dp"),
            P("tensor", "dp"),
            P("tensor", "dp"),
            P(None, "tensor", "dp"),
            P("tensor", "dp"),
            P("tensor", "dp"),
            P("dp"),
            P("dp", "tensor"),
            P("dp", "tensor"),
            P("tensor", "dp"),
            P("dp", "tensor", None),
        ),
        out_specs=(
            P("dp", "tensor", None),
            P("dp", "tensor", None),
            P("dp"),
            P("dp", "tensor"),
            P("dp", "tensor"),
            P("tensor", "dp", None),
            P("tensor", "dp", None),
            P("tensor", "dp"),
            P("tensor", "dp"),
            P("tensor", "dp"),
            P(None, "tensor", "dp"),
            P("tensor", "dp"),
            P("tensor", "dp"),
            P("dp"),
            P("dp", "tensor"),
            P("dp", "tensor"),
            P("tensor", "dp"),
        ),
        check_vma=False,
    )
```

```python
import functools

import jax
import jax.numpy as jnp
from jax import lax
from jax.experimental import pallas as pl
from jax.experimental.pallas import tpu as pltpu
from jax.sharding import PartitionSpec as P

MESH = pl.DeviceIdType.MESH
BF = jnp.bfloat16
F32 = jnp.float32
EPS = 1e-06
DECAY = 8.0
GC = 0.7978845608028654
GK = 0.044715
VMEM_LIMIT = 62 * 1024 * 1024


def dp_at(zh, zl, y, x):
    return ((zh * 2 + zl) * 2 + y) * 2 + x


def place():
    dp = lax.axis_index("dp")
    return dp // 8, (dp // 4) % 2, (dp // 2) % 2, dp % 2, lax.axis_index("tensor")


def dev(dp, core):
    return {"dp": dp, "tensor": core}


def greet(devices):
    sem = pltpu.get_barrier_semaphore()
    for d in devices:
        pl.semaphore_signal(sem, inc=1, device_id=d, device_id_type=MESH)
    pl.semaphore_wait(sem, len(devices))


def remote(src, dst, ssem, rsem, d):
    return pltpu.make_async_remote_copy(
        src_ref=src, dst_ref=dst, send_sem=ssem, recv_sem=rsem, device_id=d, device_id_type=MESH
    )


def plane(zh, zl, y, x, high):
    out = []
    for kh in range(high):
        for kl in range(2):
            for kx in range(2):
                ph, pz, px = (zh + kh) % high, (zl + kl) % 2, (x + kx) % 2
                out.append((ph, pz, px))
    return out


def gelu_parts(v):
    t = jnp.tanh(GC * (v + GK * v * v * v))
    act = 0.5 * v * (1.0 + t)
    der = 0.5 * (1.0 + t) + 0.5 * v * (1.0 - t * t) * GC * (1.0 + 3.0 * GK * v * v)
    return act, der


def segments(ends, length, width, taps):
    t = lax.broadcasted_iota(jnp.int32, (length, width), 0).astype(F32)

    def seg(at):
        total = jnp.zeros((length, width), F32)
        for j in range(4):
            total = total + jnp.where(at >= ends[:, j : j + 1], 1.0, 0.0)
        return total

    here = seg(t)
    same = []
    for k in range(1, taps):
        same.append(jnp.where((t >= float(k)) & (seg(t - float(k)) == here), 1.0, 0.0))
    return same


def scan8(a, b, reverse):
    length, width = a.shape
    row = lax.broadcasted_iota(jnp.int32, (length, width), 0) % 8
    for d in (1, 2, 4):
        if reverse:
            ash, bsh = pltpu.roll(a, length - d, 0), pltpu.roll(b, length - d, 0)
            ok = row < 8 - d
        else:
            ash, bsh = pltpu.roll(a, d, 0), pltpu.roll(b, d, 0)
            ok = row >= d
        b = b + a * jnp.where(ok, bsh, 0.0)
        a = a * jnp.where(ok, ash, 1.0)
    return a, b


def full_scan(a, b, out_ref, a_ref, reverse):
    length, width = a.shape
    a8, b8 = scan8(a, b, reverse)
    a_ref[...] = a8
    out_ref[...] = b8
    blocks = length // 8

    def step(i, carry):
        at = (blocks - 1 - i if reverse else i) * 8
        at = pl.multiple_of(at, 8)
        now = out_ref[pl.ds(at, 8), :] + a_ref[pl.ds(at, 8), :] * carry
        out_ref[pl.ds(at, 8), :] = now
        return now[0:1, :] if reverse else now[7:8, :]

    lax.fori_loop(0, blocks, step, jnp.zeros((1, width), F32))


class Gather:
    def __init__(self, slot, parts, sems, here, there, core):
        self.slot, self.parts, (self.send, self.recv, self.fsend) = slot, parts, sems
        zh, zl, y, x = here
        self.q = zl * 2 + x
        self.me = dp_at(zh, zl, y, x)
        self.near = [dp_at(h, z, y, w) for h, z, w in there]
        self.far = [dp_at(h, z, 1 - y, w) for h, z, w in there]
        self.pick = [z * 2 + w for _, z, w in there]
        self.core = core
        self.other = dev(dp_at(zh, zl, 1 - y, x), core)

    def ks(self, far):
        count = len(self.near)
        return range(4, count) if far else range(4)

    def start(self, far):
        for k in self.ks(far):
            for piece, part in self.parts:
                src = piece(self.pick[k])
                dst = part(self.slot(self.me, self.pick[k]))
                if k == 0:
                    pltpu.make_async_copy(src, dst, self.send.at[0]).start()
                else:
                    d = dev(self.near[k], self.core)
                    remote(src, dst, self.send.at[k], self.recv.at[self.me], d).start()

    def forward(self, k):
        land = self.slot(self.near[k], self.q)
        if k == 0:
            pltpu.make_async_copy(land, land, self.send.at[0]).wait()
        else:
            remote(land, land, self.send.at[k], self.recv.at[self.near[k]], self.other).wait_recv()
        remote(land, land, self.fsend.at[k], self.recv.at[self.near[k]], self.other).start()

    def forward_all(self, far):
        for k in self.ks(far):
            self.forward(k)

    def arrive_all(self):
        for k in range(len(self.far)):
            land = self.slot(self.far[k], self.q)
            remote(land, land, self.fsend.at[k], self.recv.at[self.far[k]], self.other).wait_recv()

    def finish(self):
        for k in range(len(self.near)):
            land = self.slot(self.near[k], self.q)
            remote(land, land, self.fsend.at[k], self.recv.at[self.near[k]], self.other).wait_send()
            if k:
                remote(land, land, self.send.at[k], self.recv.at[self.near[k]], self.other).wait_send()


class Rows:
    def __init__(self, buf, sems, here, core):
        self.buf, (self.send, self.recv, self.fsend, self.frecv) = buf, sems
        self.here, self.core = here, core
        zh, zl, y, x = here
        self.q = zl * 2 + x
        self.sib = dev(dp_at(zh, zl, y, x), 1 - core)

    def at(self, k):
        zh, zl, y, x = self.here
        pz, px = (zl + k // 2) % 2, (x + k % 2) % 2
        return pz * 2 + px, dev(dp_at(zh, pz, y, px), self.core)

    def start(self, piece=0, pieces=1):
        per = self.buf.shape[2] // pieces
        own = self.buf.at[self.q, self.core, pl.ds(piece * per, per)]
        for k in (1, 2):
            _, d = self.at(k)
            remote(own, own, self.send.at[k], self.recv.at[self.q], d).start()
        remote(own, own, self.fsend.at[0], self.frecv.at[self.q], self.sib).start()

    def forward(self, k):
        pq, d = self.at(k)
        land = self.buf.at[pq, self.core]
        remote(land, land, self.send.at[k], self.recv.at[pq], d).wait_recv()

        def relay():
            _, beside = self.at(1)
            remote(land, land, self.send.at[3], self.recv.at[pq], beside).start()

        if isinstance(k, int):
            if k == 2:
                relay()
        else:
            pl.when(k == 2)(relay)
        remote(land, land, self.fsend.at[k], self.frecv.at[pq], self.sib).start()

    def arrive(self, k):
        pq, _ = self.at(k)
        land = self.buf.at[pq, 1 - self.core]
        remote(land, land, self.fsend.at[k], self.frecv.at[pq], self.sib).wait_recv()

    def finish(self):
        own = self.buf.at[self.q, self.core]
        for k in range(4):
            remote(own, own, self.fsend.at[k], self.frecv.at[self.q], self.sib).wait_send()
            if k:
                remote(own, own, self.send.at[k], self.recv.at[self.q], self.sib).wait_send()


def row_sems():
    return [pltpu.SemaphoreType.DMA((4,))] * 4


class Sums:
    def __init__(self, part, sib, got, sems, rows):
        self.part, self.sib_buf, self.got = part, sib, got
        self.ssend, self.srecv, self.send, self.recv = sems
        self.rows = rows

    def push(self, k):
        r = self.rows
        pq, _ = r.at(k)
        remote(
            self.part.at[pq, 1 - r.core], self.sib_buf.at[pq], self.ssend.at[k], self.srecv.at[pq], r.sib
        ).start()

    def pair(self, k):
        r = self.rows
        pq, _ = r.at(k)
        land = self.sib_buf.at[pq]
        remote(land, land, self.ssend.at[k], self.srecv.at[pq], r.sib).wait_recv()
        return self.part[pq, r.core].astype(F32) + self.sib_buf[pq].astype(F32)

    def pass_on(self, k):
        r = self.rows
        pq, d = r.at(k)
        self.part[pq, r.core] = self.pair(k).astype(BF)
        remote(self.part.at[pq, r.core], self.got.at[r.q], self.send.at[k], self.recv.at[r.q], d).start()

    def take(self, k):
        r = self.rows
        pq, _ = r.at(k)
        land = self.got.at[pq]
        remote(land, land, self.send.at[k], self.recv.at[pq], r.sib).wait_recv()
        return self.got[pq].astype(F32)

    def ready(self):
        r = self.rows
        land = self.sib_buf.at[r.q]
        remote(land, land, self.ssend.at[0], self.srecv.at[r.q], r.sib).wait_recv()
        for k in (1, 2, 3):
            pq, _ = r.at(k)
            land = self.got.at[pq]
            remote(land, land, self.send.at[k], self.recv.at[pq], r.sib).wait_recv()

    def own(self, at):
        r = self.rows
        total = self.part[r.q, r.core, at].astype(F32) + self.sib_buf[r.q, at].astype(F32)
        for k in (1, 2, 3):
            total = total + self.got[r.at(k)[0], at].astype(F32)
        return total

    def finish(self):
        r = self.rows
        land = self.got.at[r.q]
        for k in range(4):
            remote(land, land, self.ssend.at[k], self.srecv.at[r.q], r.sib).wait_send()
            if k:
                remote(land, land, self.send.at[k], self.recv.at[r.q], r.sib).wait_send()


def rec_unit(taps, branch, conv_in, vec, gates, ends, state_ref, a_ref):
    same, conv, r, gate = rec_gates(taps, conv_in, vec, gates, ends)
    log_a = (-DECAY * r) * vec[2:3]
    a = jnp.exp(log_a)
    start = same[0] == 0.0
    a_eff = jnp.where(start, 0.0, a)
    mult = jnp.where(start, 1.0, jnp.sqrt(-jnp.tanh(log_a) * (1.0 + a * a)))
    full_scan(a_eff, mult * gate * conv, state_ref, a_ref, False)
    act, _ = gelu_parts(branch)
    return (state_ref[...] * act).astype(BF)


SMALL_ROWS = 96


def forward_kernel(n, taps, heads, turn, *refs):
    (tok, cot, wb, wi, wo, wg, wu, wd, wr, wig, small) = refs[:11]
    (o_rec, o_mlp, o_gate, o_vec, o_gain, o_ends, o_u, o_grad, pre, state, mixed, resid, o_norm) = refs[11:24]
    (rec, gat, sml, u_buf, og, part, sibb, got, extra, a_scr, gfull) = refs[24:35]
    sems = refs[35:]
    if turn:
        sems, wo_in, wd_in, (wo, wd) = refs[35:-2], wo, wd, refs[-2:]
    g_sems, r1, r2, s1, (fin, h_send, h_recv) = sems[:48], sems[48:52], sems[52:56], sems[56:60], sems[60:]
    zh, zl, y, x, c = place()
    here = (zh, zl, y, x)
    q, me = zl * 2 + x, dp_at(zh, zl, y, x)
    high = n // 8
    there = plane(zh, zl, y, x, high)
    half, width = tok.shape
    length, blk = pre.shape[1], pre.shape[2] // 2
    ff = wg.shape[1] // 4
    rb, rr = wr.shape[1], wb.shape[0]
    greet(
        [dev(dp_at(h, z, y, w), c) for h, z, w in there[1:]]
        + [dev(dp_at(zh, zl, 1 - y, x), c), dev(me, 1 - c)]
    )

    def whole(ref):
        return ref

    def head_cols(ref):
        return lambda p: ref.at[:, pl.ds(pl.multiple_of(p * blk, 128), blk)]

    def make(i, slot, parts):
        return Gather(slot, parts, g_sems[3 * i : 3 * i + 3], here, there, c)

    smalls = make(0, lambda s, g: sml.at[s], [(lambda p: small, whole)])
    gats, recs, mlps = [], [], []
    for h in range(2):
        pick = (lambda ref: lambda p: ref.at[p]) if h == 0 else (lambda ref: lambda p: ref.at[heads - 1])
        gats.append(
            make(
                1 + h,
                lambda s, g, h=h: gat.at[h, s],
                [
                    (pick(w), lambda r, i=i: r.at[:, pl.ds(i * blk, blk)])
                    for i, w in enumerate((wr, wig))
                ],
            )
        )
    for i, w in enumerate((wb, wi, wo)):
        recs.append(make(3 + i, lambda s, g, i=i: rec.at[0, i, s], [(head_cols(w), whole)]))
    part_rows = rr // 2

    def shared_piece(ref):
        return lambda p: ref.at[
            pl.ds(pl.multiple_of((p % 2) * part_rows, 8), part_rows), pl.ds((heads - 1) * blk, blk)
        ]

    def shared_rows(s, g):
        return rec.at[1, :, s, pl.ds(pl.multiple_of((g % 2) * part_rows, 8), part_rows), :]

    shared = make(
        6, shared_rows, [(shared_piece(w), lambda r, i=i: r.at[i]) for i, w in enumerate((wb, wi, wo))]
    )
    for i, w in enumerate((wg, wu, wd)):
        for t in range(ff // blk):
            piece = lambda p, w=w, t=t: w.at[:, pl.ds(pl.multiple_of(p * ff + t * blk, 128), blk)]
            j = i * (ff // blk) + t
            mlps.append(make(7 + j, lambda s, g, j=j: o_mlp.at[j, s], [(piece, whole)]))
    count = len(there)
    order = [shared, recs[0], gats[0], recs[1], gats[1], recs[2]] + mlps
    ahead = 3
    trickle = []

    def pump(j):
        if j + ahead < len(order):
            order[j + ahead].forward_all(False)
        order[j].forward_all(True)
        for _ in range(3 if j < 6 else 2):
            if trickle:
                trickle.pop(0)()
        if j + ahead < len(order):
            order[j + ahead].start(True)
        if j + 2 * ahead < len(order):
            order[j + 2 * ahead].start(False)

    def turn_over(src, dst):
        for i in range(0, src.shape[0], 128):
            dst[:, i : i + 128] = src[i : i + 128, :].T

    smalls.start(True)
    smalls.start(False)
    if turn:
        turn_over(wo_in, wo)
    for j in range(2 * ahead):
        if j < ahead:
            order[j].start(True)
        order[j].start(False)

    if turn:
        turn_over(wd_in, wd)
    xin = tok[...].astype(F32)
    unit = xin * lax.rsqrt(jnp.mean(xin * xin, axis=-1, keepdims=True) + EPS)
    resid[...] = unit
    smalls.forward_all(False)
    for j in range(ahead):
        order[j].forward_all(False)
    smalls.forward_all(True)
    pump(0)
    smalls.arrive_all()
    per_vec, per_gain = blk // 128, width // 128
    base = (heads - 1) * 16
    for h in range(2):
        at = pl.multiple_of(q * 16, 16) if h == 0 else base
        groups = [jnp.zeros((16, 128), F32)] * per_vec
        for s in range(n):
            g = s * rb // 128
            groups[g] = groups[g] + sml[s, pl.ds(at, 16), :].astype(F32)
        raw = jnp.concatenate(groups, axis=1)
        decay = raw[2:3]
        o_vec[h, 0:2, :] = raw[0:2]
        o_vec[h, 2:3, :] = jnp.log1p(jnp.exp(-decay))
        o_vec[h, 3:4, :] = jax.nn.sigmoid(-decay)
        o_vec[h, 4 : 5 + taps, :] = raw[3 : 4 + taps]
    groups = [None] * per_gain
    for s in range(n):
        g = s * rr // 128
        v = sml[s, SMALL_ROWS - 16 : SMALL_ROWS, :].astype(F32)
        groups[g] = v if groups[g] is None else groups[g] + v
    for g in range(per_gain):
        o_gain[:, g * 128 : (g + 1) * 128] = groups[g][0:8]
    for j in range(4):
        v = sml[dp_at(zh, j // 2, y, j % 2), SMALL_ROWS - 16 : SMALL_ROWS, :].astype(F32)
        row = jnp.broadcast_to(v[2:3], (8, 128))
        lane = lax.broadcasted_iota(jnp.int32, (8, 128), 1)
        ends = jnp.zeros((8, 128), F32)
        for i in range(4):
            ends = ends + jnp.where(lane >= i, row[:, i : i + 1], 0.0)
        o_ends[j] = ends
    u_rows = Rows(u_buf, r1, here, c)
    g_rows = Rows(o_grad, r2, here, c)
    u_buf[q, c] = (resid[...] * o_gain[0:1, :]).astype(BF)
    trickle += [functools.partial(u_rows.start, p, 8) for p in range(8)]
    e3 = o_ends[q][0:1, 3:4]
    spot = lax.broadcasted_iota(jnp.int32, (half, 1), 0).astype(F32) + (c * half).astype(F32)
    og[...] = jnp.where(spot < e3, cot[...], 0.0).astype(BF)
    own_grad = o_grad.at[q, c]
    place_grad = pltpu.make_async_copy(og, own_grad, fin.at[0])
    place_grad.start()
    place_grad.wait()
    _, beside = u_rows.at(1)

    def exchange(g, first, many):
        rows = rec.at[
            1, :, pl.ds(first, many), pl.ds(pl.multiple_of((g % 2) * part_rows, 8), part_rows), :
        ]
        return remote(rows, rows, h_send, h_recv, beside)

    pump(1)
    shared.arrive_all()
    eighth = n // 8
    trickle += [exchange(q, p * eighth, eighth).start for p in range(8)]
    for j in range(2, 5):
        pump(j)
    for k in (1, 2):
        u_rows.forward(k)
    pump(5)
    while trickle:
        trickle.pop(0)()
    trickle += [functools.partial(g_rows.start, p, 8) for p in range(8)]
    u_rows.forward(3)
    for a in gats + recs:
        a.arrive_all()
    for h in range(2):
        if rb % 16 == 0:
            o_gate[h] = gat[h].reshape(blk, 2 * blk)
        else:
            for s in range(n):
                gfull[s * rb : (s + 1) * rb, :] = gat[h, s].astype(F32)
            o_gate[h] = gfull[...].astype(BF)
    for k in range(4):
        u_rows.arrive(k)
    keep = [pltpu.make_async_copy(rec, o_rec, fin.at[1]), pltpu.make_async_copy(u_buf, o_u, fin.at[2])]
    keep[1].start()

    sums = Sums(part, sibb, got, s1, u_rows)

    def step(i, carry):
        h = i // 4
        k = ((i + 1) % 4) * ((7 - i) // 4)
        pq, _ = u_rows.at(k)
        at = pq + h * (4 - pq)

        @pl.when(i == 4)
        def _():
            exchange(q + 1, 0, n).wait_recv()
            keep[0].start()

        rows = u_buf[pq].reshape(2 * half, width)
        for j in range(2):
            w = rec[h, j].reshape(width, blk)
            pre[at, :, j * blk : (j + 1) * blk] = mm(rows, w)
        mx = rec_unit(
            taps, pre[at, :, :blk], pre[at, :, blk:], o_vec[h], o_gate[h], o_ends[pq][0:1, :], state.at[at], a_scr
        )
        mixed[at] = mx
        per = 512 // rr if rr <= 512 else 1

        def cols_out(t, carry):
            w = rec[h, 2, pl.ds(t * per, per)].reshape(per * rr, blk)
            tile = mm_t(mx, w)
            lanes = pl.ds(pl.multiple_of(t * (per * rr), 128), per * rr)
            tile = tile + jnp.where(i == 4, extra[:, lanes], 0.0)

            @pl.when(i == 3)
            def _():
                extra[:, lanes] = tile

            @pl.when(i != 3)
            def _():
                part[pq, 0, :, lanes] = tile[:half].astype(BF)
                part[pq, 1, :, lanes] = tile[half:].astype(BF)

            return carry

        lax.fori_loop(0, width // (per * rr), cols_out, 0)

        @pl.when(i != 3)
        def _():
            sums.push(k)

        @pl.when((i > 0) & (i < 4))
        def _():
            sums.pass_on(i)

        for j in range(4):

            @pl.when(i == j)
            def _():
                pump(6 + j)

        return carry

    extra[...] = jnp.zeros_like(extra)
    lax.fori_loop(0, 5, step, 0)
    pump(10)
    pump(11)
    for k in (1, 2):
        g_rows.forward(k)
    sums.ready()

    def finish(i, carry):
        at = pl.ds(pl.multiple_of(i * 32, 32), 32)
        total = tok[at, :].astype(F32) + sums.own(at)
        resid[at, :] = total
        unit = total * lax.rsqrt(jnp.mean(total * total, axis=-1, keepdims=True) + EPS)
        o_norm[at, :] = (unit * o_gain[1:2, :]).astype(BF)
        return carry

    lax.fori_loop(0, half // 32, finish, 0)
    pump(12)
    pump(13)
    g_rows.forward(3)
    for j in range(14, len(order)):
        pump(j)
    for a in mlps:
        a.arrive_all()
    for k in range(4):
        g_rows.arrive(k)
    exchange(q, 0, n).wait_send()
    for a in [smalls, shared] + mlps + gats + recs + [u_rows, g_rows, sums]:
        a.finish()
    for cp in keep:
        cp.wait()


def forward(tok, cot, wb, wi, wo, wg, wu, wd, wr, wig, small, n, taps, cid):
    half, width = tok.shape
    heads, rb, blk = wr.shape
    rr = wb.shape[0]
    length = 2 * half
    ff = wg.shape[1] // 4
    turn = rr % 128 == 0
    if not turn:
        wo, wd = wo.T, wd.T
    vm = pl.BlockSpec(memory_space=pltpu.VMEM)
    hb = pl.BlockSpec(memory_space=pl.ANY)

    def sds(*shape, t=F32):
        return jax.ShapeDtypeStruct(shape, t)

    unit = sds(5, length, blk)
    outs = (
        (sds(2, 3, n, rr, blk, t=BF), hb),
        (sds(3 * ff // blk, n, rr, blk, t=BF), hb),
        (sds(2, blk, 2 * blk, t=BF), vm),
        (sds(2, 16, blk), vm),
        (sds(8, width), vm),
        (sds(4, 8, 128), vm),
        (sds(4, 2, half, width, t=BF), hb),
        (sds(4, 2, half, width, t=BF), hb),
        (sds(5, length, 2 * blk), vm),
        (unit, vm),
        (sds(5, length, blk, t=BF), vm),
        (sds(half, width), vm),
        (sds(half, width, t=BF), vm),
    )
    count = n // 2
    return pl.pallas_call(
        functools.partial(forward_kernel, n, taps, heads, turn),
        out_shape=tuple(o for o, _ in outs),
        in_specs=[vm, vm, hb, hb, vm if turn else hb, hb, hb, vm if turn else hb, hb, hb, hb],
        out_specs=[s for _, s in outs],
        scratch_shapes=[
            pltpu.VMEM((2, 3, n, rr, blk), BF),
            pltpu.VMEM((2, n, rb, 2 * blk), BF),
            pltpu.VMEM((n, SMALL_ROWS, 128), BF),
            pltpu.VMEM((4, 2, half, width), BF),
            pltpu.VMEM((half, width), BF),
            pltpu.VMEM((4, 2, half, width), BF),
            pltpu.VMEM((4, half, width), BF),
            pltpu.VMEM((4, half, width), BF),
            pltpu.VMEM((length, width), F32),
            pltpu.VMEM((length, blk), F32),
            pltpu.VMEM((blk, 2 * blk), F32),
        ]
        + [
            pltpu.SemaphoreType.DMA((count,)),
            pltpu.SemaphoreType.DMA((n,)),
            pltpu.SemaphoreType.DMA((count,)),
        ]
        * 16
        + row_sems() * 3
        + [pltpu.SemaphoreType.DMA((3,)), pltpu.SemaphoreType.DMA, pltpu.SemaphoreType.DMA]
        + ([pltpu.VMEM((rr, heads * blk), BF), pltpu.VMEM((rr, 4 * ff), BF)] if turn else []),
        compiler_params=pltpu.CompilerParams(
            collective_id=cid, has_side_effects=True, vmem_limit_bytes=VMEM_LIMIT
        ),
        name="forward",
    )(tok, cot, wb, wi, wo, wg, wu, wd, wr, wig, small)


def mlp_kernel(norm, resid, gain, cot, ends, w_hbm, mg_hbm, g_hbm, o_rec, o_rgrad, o_hid, o_gain,
               w, nbuf, mg, hg, hu, gbuf, part, sibb, got, wsem, msem, gsem, *sems):
    zh, zl, y, x, c = place()
    here = (zh, zl, y, x)
    q, me = zl * 2 + x, dp_at(zh, zl, y, x)
    half, width = norm.shape
    nt, n, rr, blk = w.shape
    tiles, steps, per = nt // 3, width // blk, blk // rr
    rows = Rows(nbuf, sems[:4], here, c)
    sums = Sums(part, sibb, got, sems[4:8], rows)
    greet([dev(me, 1 - c)] + [rows.at(k)[1] for k in (1, 2, 3)])
    nbuf[q, c] = norm[...]
    rows.start()
    loads = []
    for t in range(tiles):
        for i in range(3):
            j = i * tiles + t
            loads.append((t, pltpu.make_async_copy(w_hbm.at[j], w.at[j], wsem.at[j])))
    loads.insert(2, (0, pltpu.make_async_copy(mg_hbm, mg, msem)))
    for _, cp in loads:
        cp.start()

    def row(k, carry):
        pq, _ = rows.at(k)
        rows.arrive(k)

        def first(t, carry):
            @pl.when(k == 0)
            def _():
                for j, cp in loads:

                    @pl.when(t == j)
                    def _():
                        cp.wait()

            a = nbuf[pq].reshape(2 * half, width)
            gate = mm(a, w[t].reshape(width, blk))
            up = mm(a, w[tiles + t].reshape(width, blk))
            grad = mm(mg[pq].reshape(2 * half, width), w[2 * tiles + t].reshape(width, blk))
            act, der = gelu_parts(gate)
            o_hid[t, pq] = (act * up).astype(BF)
            hg[t, pq] = (grad * up * der).astype(BF)
            hu[t, pq] = (grad * act).astype(BF)
            return carry

        lax.fori_loop(0, tiles, first, 0)

        @pl.when(k < 3)
        def _():
            rows.forward(k + 1)

        @pl.when(k > 1)
        def _():
            sums.pass_on(k - 1)

        def second(d, carry):
            total = jnp.zeros((2 * half, blk), F32)
            for t in range(tiles):
                total = total + mm_t(hg[t, pq], w[t, pl.ds(d * per, per)].reshape(blk, blk))
                total = total + mm_t(hu[t, pq], w[tiles + t, pl.ds(d * per, per)].reshape(blk, blk))
            lanes = pl.ds(pl.multiple_of(d * blk, 128), blk)
            part[pq, 0, :, lanes] = total[:half].astype(BF)
            part[pq, 1, :, lanes] = total[half:].astype(BF)
            return carry

        lax.fori_loop(0, steps, second, 0)
        sums.push(k)
        return carry

    def rows_from(k, carry):
        return row(k, carry)

    lax.fori_loop(0, 4, rows_from, 0)
    sums.pass_on(3)

    def out_tile(d):
        at = pl.ds(d * per, per)
        return pltpu.make_async_copy(gbuf.at[:, at], g_hbm.at[:, at], gsem.at[d])

    def grads(d, carry):
        lanes = pl.ds(pl.multiple_of(d * blk, 128), blk)
        nt_ = nbuf[:, :, :, lanes].reshape(8 * half, blk).T
        mt_ = mg[:, :, :, lanes].reshape(8 * half, blk).T
        for i, (left, right) in enumerate(((nt_, hg), (nt_, hu), (mt_, o_hid))):
            for t in range(tiles):
                tile = mm(left, right[t].reshape(8 * half, blk))
                gbuf[i * tiles + t, pl.ds(d * per, per)] = tile.astype(BF).reshape(per, rr, blk)
        out_tile(d).start()
        return carry

    lax.fori_loop(0, steps, grads, 0)
    sums.ready()
    e3 = ends[q][0:1, 3:4]

    def finish(i, acc):
        at = pl.ds(pl.multiple_of(i * 32, 32), 32)
        total, r = sums.own(at), resid[at, :]
        scale = lax.rsqrt(jnp.mean(r * r, axis=-1, keepdims=True) + EPS)
        unit = r * scale
        g2 = total * gain[1:2, :]
        back = scale * (g2 - unit * jnp.mean(g2 * unit, axis=-1, keepdims=True))
        spot = lax.broadcasted_iota(jnp.int32, (32, 1), 0) + (c * half + i * 32)
        back = back + jnp.where(spot.astype(F32) < e3, cot[at, :], 0.0)
        o_rgrad[at, :] = back
        o_rec[at, :] = back.astype(BF)
        return acc + jnp.sum(total * unit, axis=0, keepdims=True)

    gsum = lax.fori_loop(0, half // 32, finish, jnp.zeros((1, width), F32))
    o_gain[...] = jnp.broadcast_to(gsum, o_gain.shape)
    for d in range(steps):
        out_tile(d).wait()
    rows.finish()
    sums.finish()


def mlp_block(norm, resid, gain, cot, ends, mlp_w, mlp_grad, cid):
    half, width = norm.shape
    nt, n, rr, blk = mlp_w.shape
    tiles = nt // 3
    vm = pl.BlockSpec(memory_space=pltpu.VMEM)
    hb = pl.BlockSpec(memory_space=pl.ANY)
    hid = (tiles, 4, 2 * half, blk)
    return pl.pallas_call(
        mlp_kernel,
        out_shape=(
            jax.ShapeDtypeStruct(mlp_w.shape, BF),
            jax.ShapeDtypeStruct((half, width), BF),
            jax.ShapeDtypeStruct((half, width), F32),
            jax.ShapeDtypeStruct(hid, BF),
            jax.ShapeDtypeStruct((8, width), F32),
        ),
        in_specs=[vm] * 5 + [hb] * 2,
        out_specs=[hb] + [vm] * 4,
        scratch_shapes=[
            pltpu.VMEM(mlp_w.shape, BF),
            pltpu.VMEM((4, 2, half, width), BF),
            pltpu.VMEM((4, 2, half, width), BF),
            pltpu.VMEM(hid, BF),
            pltpu.VMEM(hid, BF),
            pltpu.VMEM(mlp_w.shape, BF),
            pltpu.VMEM((4, 2, half, width), BF),
            pltpu.VMEM((4, half, width), BF),
            pltpu.VMEM((4, half, width), BF),
            pltpu.SemaphoreType.DMA((nt,)),
            pltpu.SemaphoreType.DMA,
            pltpu.SemaphoreType.DMA((width // blk,)),
        ]
        + row_sems() * 2,
        compiler_params=pltpu.CompilerParams(
            collective_id=cid, has_side_effects=True, vmem_limit_bytes=VMEM_LIMIT
        ),
        name="mlp_block",
    )(norm, resid, gain, cot, ends, mlp_w, mlp_grad)


class Scatter:
    def __init__(self, away, both, mine, pair, landed, sems, here, there, core):
        self.away, self.both, self.mine, self.pair, self.landed = away, both, mine, pair, landed
        self.ysend, self.yrecv, self.send, self.recv = sems
        zh, zl, y, x = here
        self.core = core
        self.own = zh * 4 + zl * 2 + x
        self.places = [(h * 4 + z * 2 + w, dp_at(h, z, y, w)) for h, z, w in (*there[4:], *there[1:4], there[0])]
        self.other = dev(dp_at(zh, zl, 1 - y, x), core)

    def start(self):
        remote(self.away, self.both, self.ysend, self.yrecv, self.other).start()

    def pass_on(self):
        last = len(self.places) - 1
        remote(self.away, self.both, self.ysend, self.yrecv, self.other).wait_recv()
        for i, (j, near) in enumerate(self.places):
            slot = self.pair(j)
            slot[...] = (self.mine(near).astype(F32) + slot[...].astype(F32)).astype(slot.dtype)
            if i == last:
                pltpu.make_async_copy(slot, self.landed(self.own), self.send.at[j]).start()
            else:
                remote(
                    slot, self.landed(self.own), self.send.at[j], self.recv.at[self.own], dev(near, self.core)
                ).start()

    def collect(self):
        last = len(self.places) - 1
        remote(self.away, self.both, self.ysend, self.yrecv, self.other).wait_send()
        for i, (j, _) in enumerate(self.places):
            slot, land = self.pair(j), self.landed(j)
            if i == last:
                pltpu.make_async_copy(land, land, self.send.at[j]).wait()
            else:
                remote(land, land, self.send.at[j], self.recv.at[j], self.other).wait_recv()
                remote(slot, slot, self.send.at[j], self.recv.at[j], self.other).wait_send()


def scatter_sems(high):
    return [pltpu.SemaphoreType.DMA, pltpu.SemaphoreType.DMA] + [pltpu.SemaphoreType.DMA((high * 4,))] * 2


def rec_gates(taps, conv_in, vec, gates, ends):
    length, blk = conv_in.shape
    same = segments(ends, length, blk, taps)
    conv = conv_in * vec[4:5] + vec[4 + taps : 5 + taps]
    for k in range(1, taps):
        conv = conv + pltpu.roll(conv_in, k, 0) * same[k - 1] * vec[4 + k : 5 + k]
    pre = jnp.dot(conv.astype(BF), gates, preferred_element_type=F32)
    r = jax.nn.sigmoid(pre[:, :blk] + vec[0:1])
    gate = jax.nn.sigmoid(pre[:, blk:] + vec[1:2])
    return same, conv, r, gate


def rec_unit_back(taps, branch, conv_in, vec, gates, ends, state, mg, carry_ref, a_ref):
    length, blk = branch.shape
    same, conv, r, gate = rec_gates(taps, conv_in, vec, gates, ends)
    start = same[0] == 0.0
    act, der = gelu_parts(branch)
    branch_low = (mg * state * der).astype(BF)
    log_a = (-DECAY * r) * vec[2:3]
    a = jnp.exp(log_a)
    a_eff = jnp.where(start, 0.0, a)
    row = lax.broadcasted_iota(jnp.int32, (length, blk), 0)
    a_next = jnp.where(row < length - 1, pltpu.roll(a_eff, length - 1, 0), 0.0)
    full_scan(a_next, mg * act, carry_ref, a_ref, True)
    carry = carry_ref[...]
    prev = jnp.where(row > 0, pltpu.roll(state, 1, 0), 0.0)
    raw = jnp.sqrt(-jnp.tanh(log_a) * (1.0 + a * a))
    mult = jnp.where(start, 1.0, raw)
    log_grad = jnp.where(start, 0.0, carry * prev * a - carry * gate * conv * (a * a) / raw)
    r_grad = log_grad * (-DECAY * vec[2:3]) * (r * (1.0 - r))
    i_grad = carry * mult * conv * (gate * (1.0 - gate))
    pre_low = jnp.concatenate([r_grad.astype(BF), i_grad.astype(BF)], axis=1)
    conv_grad = carry * mult * gate + mm_t(pre_low, gates)
    gate_grads = t_mm(conv.astype(BF), pre_low)

    def total(v):
        return jnp.sum(v, axis=0, keepdims=True)

    sums = [total(r_grad), total(i_grad), total(log_grad * (DECAY * r) * vec[3:4]), total(conv_grad)]
    inp = conv_grad * vec[4:5]
    sums.append(total(conv_grad * conv_in))
    for k in range(1, taps):
        masked = conv_grad * same[k - 1]
        sums.append(total(masked * pltpu.roll(conv_in, k, 0)))
        inp = inp + pltpu.roll(masked, length - k, 0) * vec[4 + k : 5 + k]
    return branch_low, inp.astype(BF), gate_grads, jnp.concatenate(sums, axis=0)


def backward_kernel(n, taps, *refs):
    (tok, rgrad, resid, gain, gsum2, ends, vec, gates, pre, state, mixed) = refs[:11]
    (rec_own, hid, g_hbm, rec_hbm, mlp_hbm, u_hbm) = refs[11:17]
    (o_res, o_tok, l_mlp, l_rec, l_sh, l_gate, l_small) = refs[17:24]
    (rec, ub, rg, part, sib1, got1, low, grec, gsh, gshin, g_own, y_mlp, y_rec, y_sh, a_scr, c_scr,
     gg, vg, ggl, y_gate, sml, sml_sib, y_sml) = refs[24:47]
    sems = refs[47:]
    zh, zl, y, x, c = place()
    here = (zh, zl, y, x)
    q, me = zl * 2 + x, dp_at(zh, zl, y, x)
    high = n // 8
    there = plane(zh, zl, y, x, high)
    half, width = tok.shape
    length = 2 * half
    blk = mixed.shape[2]
    rr = width // n
    rb = blk // n
    nt = g_own.shape[0]
    per, steps = blk // rr, width // blk
    taken = [0]

    def some(k):
        taken[0] += k
        return sems[taken[0] - k : taken[0]]

    rows = Rows(rg, some(4), here, c)
    sums1 = Sums(part, sib1, got1, some(4), rows)
    sums2 = Sums(part, sib1, got1, some(4), rows)
    (loads,) = some(1)
    greet(
        [dev(dp_at(h, z, y, w), c) for h, z, w in there[1:]]
        + [dev(dp_at(zh, zl, 1 - y, x), c), dev(me, 1 - c)]
    )
    first = pltpu.make_async_copy(rec_own, rg.at[q, c], loads.at[0])
    first.start()
    first.wait()
    rows.start()
    grab = [
        pltpu.make_async_copy(rec_hbm, rec, loads.at[0]),
        pltpu.make_async_copy(u_hbm, ub, loads.at[1]),
        pltpu.make_async_copy(g_hbm.at[:, :, y], g_own, loads.at[2]),
    ]
    for cp in grab:
        cp.start()

    tiles = nt // 3

    def cols_at(i):
        return pl.ds(pl.multiple_of(i * blk, 128), blk)

    def chunk(i, sem):
        return Scatter(
            g_hbm.at[i, :, 1 - y],
            y_mlp.at[i],
            lambda s: g_own[i, s // 4, s % 2],
            lambda j: y_mlp.at[i, j // 2, j % 2],
            lambda j: l_mlp.at[j // 4, i // tiles, :, cols_at((j % 4) * tiles + i % tiles)],
            sem, here, there, c,
        )

    mlps = [chunk(i, some(4)) for i in range(nt)]
    for a in mlps[:3]:
        a.start()
    recs = [
        Scatter(
            grec.at[i, :, 1 - y],
            y_rec.at[i],
            lambda s, i=i: grec[i, s // 4, (s // 2) % 2, s % 2],
            lambda j, i=i: y_rec.at[i, j // 2, j % 2],
            lambda j, i=i: l_rec.at[j // 4, i, :, cols_at(j % 4)],
            some(4), here, there, c,
        )
        for i in range(3)
    ]
    part_rows = rr // 2

    shared = Scatter(
        gshin.at[:, :, 1 - y],
        y_sh,
        lambda s: gshin[:, s // 4, (s // 2) % 2, s % 2],
        lambda j: y_sh.at[:, j // 2, j % 2],
        lambda j: l_sh.at[j // 2, :, pl.ds(pl.multiple_of((j % 2) * part_rows, 8), part_rows), :],
        some(4), here, there, c,
    )
    gate_sc = Scatter(
        ggl.at[:, :, 1 - y],
        y_gate,
        lambda s: ggl[:, s // 4, (s // 2) % 2, s % 2],
        lambda j: y_gate.at[:, j // 2, j % 2],
        lambda j: l_gate.at[j],
        some(4), here, there, c,
    )
    h_send, h_recv, s_send, s_recv, z_send, z_recv, m_send, m_recv, again = some(9)
    order = mlps + [shared] + recs + [gate_sc]
    trickle = []
    _, beside = rows.at(1)
    eighth = n // 16

    def pump(j):
        order[j].pass_on()
        for _ in range(2 if j else 0):
            if trickle:
                trickle.pop(0)()
        if j + 3 < len(order):
            order[j + 3].start()

    gg[...] = jnp.zeros_like(gg)
    vg[...] = jnp.zeros_like(vg)
    grab[0].wait()

    def exchange(first, many):
        there_rows = pl.ds(pl.multiple_of((1 - x) * part_rows, 8), part_rows)
        cut = pl.ds(first, many)
        return remote(gsh.at[:, cut, :, :, there_rows, :], gshin.at[:, cut], h_send, h_recv, beside)

    def store(ref, i, d, tile):
        tile = tile.astype(BF)
        if per == 2:
            ref[i, d // 2, d % 2] = tile.reshape(2, rr, blk)
        else:
            ref[i, pl.ds(d * (per // 4), per // 4)] = tile.reshape(per // 4, 2, 2, rr, blk)

    def shared_grads(d, carry):
        lanes = pl.ds(pl.multiple_of(d * blk, 128), blk)
        uo = ub[q, :, :, lanes].reshape(length, blk).T
        ro = rg[q, :, :, lanes].reshape(length, blk).T
        for i in range(3):
            own = low[4, :, i * blk : (i + 1) * blk] if i < 2 else mixed[4]
            store(gsh, i, d, mm(uo if i < 2 else ro, own))
        return carry

    trickle += [exchange(p * eighth, eighth).start for p in range(4)]

    def step(i, carry):
        h = jnp.where(i == 1, 1, 0)
        k = jnp.maximum(i - 1, 0)
        pq, _ = rows.at(k)
        at = pq + h * (4 - pq)

        @pl.when(i != 1)
        def _():
            rows.arrive(k)

        mg = mm(rg[pq].reshape(length, width), rec[h, 2].reshape(width, blk))

        @pl.when((i > 0) & (i < 4))
        def _():
            rows.forward(k + 1)

        b_low, i_low, g_add, v_add = rec_unit_back(
            taps, pre[at, :, :blk], pre[at, :, blk:], vec[h], gates[h], ends[pq][0:1, :], state[at], mg, c_scr, a_scr,
        )
        low[at, :, :blk], low[at, :, blk:] = b_low, i_low
        gg[h] += g_add
        vg[h] += v_add

        @pl.when(i > 2)
        def _():
            sums1.pass_on(k - 1)

        def cols_out(t, carry):
            cut = pl.ds(t * per, per)
            lanes = pl.ds(pl.multiple_of(t * blk, 128), blk)

            def tile_of(left, head):
                return sum(
                    mm_t(left[:, j * blk : (j + 1) * blk], rec[head, j, cut].reshape(blk, blk)) for j in range(2)
                )

            def emit(tile):
                part[pq, 0, :, lanes] = tile[:half].astype(BF)
                part[pq, 1, :, lanes] = tile[half:].astype(BF)

            @pl.when(i == 1)
            def _():
                emit(tile_of(low[4], 1) + tile_of(low[pq], 0))

            @pl.when(i > 1)
            def _():
                emit(tile_of(low[pq], 0))

            return carry

        @pl.when(i > 0)
        def _():
            lax.fori_loop(0, steps, cols_out, 0)

        @pl.when(i > 0)
        def _():
            sums1.push(k)

        for j in range(5):

            @pl.when(i == j)
            def _():
                if j == 0:
                    grab[2].wait()
                if j == 1:
                    grab[1].wait()
                    lax.fori_loop(0, steps, shared_grads, 0)
                pump(j)

        return carry

    lax.fori_loop(0, 5, step, 0)
    sums1.pass_on(3)
    for h in range(2):
        for s in range(n):
            ggl[h, s // 4, (s // 2) % 2, s % 2] = gg[h, s * rb : (s + 1) * rb, :].astype(BF)
    fetch = pltpu.make_async_copy(mlp_hbm.at[pl.ds(2 * (nt // 3), nt // 3)], rec.at[0], loads.at[0])
    fetch.start()
    pump(5)

    def grads(d, carry):
        lanes = pl.ds(pl.multiple_of(d * blk, 128), blk)
        ut = ub[:, :, :, lanes].reshape(4 * length, blk).T
        rt = rg[:, :, :, lanes].reshape(4 * length, blk).T
        for i in range(3):
            if i < 2:
                right = low[0:4, :, i * blk : (i + 1) * blk].reshape(4 * length, blk)
            else:
                right = mixed[0:4].reshape(4 * length, blk)
            store(grec, i, d, mm(ut if i < 2 else rt, right))
        return carry

    lax.fori_loop(0, steps, grads, 0)
    exchange(0, n // 4).wait()
    for s in range(n // 4):
        gshin[:, s] = (
            gshin[:, s].astype(F32)
            + gsh[:, s, :, :, pl.ds(pl.multiple_of(x * part_rows, 8), part_rows), :].astype(F32)
        ).astype(BF)
    per_row = length // rr
    fetch_hid = pltpu.make_async_copy(hid, gsh.at[:, pl.ds(0, per_row)], loads.at[1])
    fetch_hid.start()
    pump(6)

    sums1.ready()

    def finish(i, acc):
        at = pl.ds(pl.multiple_of(i * 32, 32), 32)
        total, xin = sums1.own(at), tok[at, :].astype(F32)
        scale = lax.rsqrt(jnp.mean(xin * xin, axis=-1, keepdims=True) + EPS)
        unit = xin * scale
        g1 = total * gain[0:1, :]
        o_tok[at, :] = rgrad[at, :] + scale * (g1 - unit * jnp.mean(g1 * unit, axis=-1, keepdims=True))
        return acc + jnp.sum(total * unit, axis=0, keepdims=True)

    gsum1 = lax.fori_loop(0, half // 32, finish, jnp.zeros((1, width), F32))
    sums1.finish()
    for d in [rows.sib] + [rows.at(k)[1] for k in (1, 2, 3)]:
        pl.semaphore_signal(again, inc=1, device_id=d, device_id_type=MESH)
    for h in range(2):
        sml[8 * h : 8 * h + 8, :] = vg[h]
    for i in range(steps):
        sml[16 + i : 17 + i, :] = gsum1[:, i * blk : (i + 1) * blk]
        sml[16 + steps + i : 17 + steps + i, :] = gsum2[0:1, i * blk : (i + 1) * blk]
    gain_rows = sml.at[pl.ds(16, 2 * steps)]
    with_sib = remote(gain_rows, sml_sib, s_send, s_recv, rows.sib)
    with_sib.start()
    pump(7)

    fetch.wait()
    fetch_hid.wait()

    pl.semaphore_wait(again, 4)

    def hid_rows(t, row):
        if per_row == 2:
            return gsh[t, row // 2, row % 2].reshape(length, blk)
        return gsh[t, pl.ds(row * (per_row // 4), per_row // 4)].reshape(length, blk)

    def out_rows(i, carry):
        k = (i + 1) % 4
        pq, _ = rows.at(k)

        def cols_out(d, carry):
            tile = jnp.zeros((length, blk), F32)
            for t in range(nt // 3):
                left = hid_rows(t, pq)
                tile = tile + mm_t(left, rec[0, t, pl.ds(d * per, per)].reshape(blk, blk))
            lanes = pl.ds(pl.multiple_of(d * blk, 128), blk)
            part[pq, 0, :, lanes] = tile[:half].astype(BF)
            part[pq, 1, :, lanes] = tile[half:].astype(BF)
            return carry

        lax.fori_loop(0, steps, cols_out, 0)
        sums2.push(k)

        @pl.when(i > 0)
        def _():
            sums2.pass_on(i)

        return carry

    lax.fori_loop(0, 4, out_rows, 0)
    pump(8)
    with_sib.wait()
    sml[16 : 16 + 2 * steps, :] += sml_sib[...]
    with_y = remote(sml, y_sml, z_send, z_recv, dev(dp_at(zh, zl, 1 - y, x), c))
    with_y.start()
    pump(9)
    pump(10)
    with_y.wait()
    sml[...] = sml[...] + y_sml[...]
    mine = zh * 4 + q
    small_out = []
    for i, (h, z, w) in enumerate(there):
        if i == 0:
            cp = pltpu.make_async_copy(sml, l_small.at[mine], m_send.at[i])
        else:
            cp = remote(sml, l_small.at[mine], m_send.at[i], m_recv.at[mine], dev(dp_at(h, z, y, w), c))
        cp.start()
        small_out.append(cp)
    pump(11)
    sums2.ready()
    e3 = ends[q][0:1, 3:4]

    def result(i, carry):
        at = pl.ds(pl.multiple_of(i * 32, 32), 32)
        spot = lax.broadcasted_iota(jnp.int32, (32, 1), 0) + (c * half + i * 32)
        o_res[at, :] = jnp.where(spot.astype(F32) < e3, resid[at, :] + sums2.own(at), 0.0).astype(BF)
        return carry

    lax.fori_loop(0, half // 32, result, 0)
    sums2.finish()
    pump(12)
    pump(13)
    rows.finish()
    for a in mlps + recs + [gate_sc, shared]:
        a.collect()
    for i, (h, z, w) in enumerate(there):
        if i == 0:
            small_out[i].wait()
        else:
            j = h * 4 + z * 2 + w
            land = l_small.at[j]
            remote(land, land, m_send.at[i], m_recv.at[j], rows.sib).wait_recv()
            small_out[i].wait_send()


def backward(tok, rec_own, rgrad, resid, gain, gsum2, ends, vec, gates, saved, hid, g_mlp, rec_w, mlp_w, u, n, taps, cid):
    half, width = tok.shape
    pre, state, mixed = saved
    blk = mixed.shape[2]
    length = 2 * half
    rr, rb, high = width // n, blk // n, n // 8
    nt = g_mlp.shape[0]
    slots = high * 4
    vm = pl.BlockSpec(memory_space=pltpu.VMEM)
    hb = pl.BlockSpec(memory_space=pl.ANY)
    g_view = g_mlp.reshape(nt, n // 4, 2, 2, rr, blk)
    hid = hid.reshape(nt // 3, length // rr, 2, 2, rr, blk)
    small_rows = 16 + 2 * (width // blk)

    def sds(*shape, t=BF):
        return jax.ShapeDtypeStruct(shape, t)

    def v(*shape, t=BF):
        return pltpu.VMEM(shape, t)

    dma = pltpu.SemaphoreType.DMA
    return pl.pallas_call(
        functools.partial(backward_kernel, n, taps),
        out_shape=(
            sds(half, width),
            sds(half, width, t=F32),
            sds(high, 3, rr, 4 * (nt // 3) * blk),
            sds(high, 3, rr, 4 * blk),
            sds(slots // 2, 3, rr, blk),
            sds(slots, 2, rb, 2 * blk),
            sds(slots, small_rows, blk, t=F32),
        ),
        in_specs=[vm] * 11 + [hb] * 6,
        out_specs=[vm, vm] + [hb] * 5,
        scratch_shapes=[
            v(2, 3, n, rr, blk),
            v(4, 2, half, width),
            v(4, 2, half, width),
            v(4, 2, half, width),
            v(4, half, width),
            v(4, half, width),
            v(5, length, 2 * blk),
            v(3, n // 4, 2, 2, rr, blk),
            v(3, n // 4, 2, 2, rr, blk),
            v(3, n // 4, 2, 2, rr // 2, blk),
            v(nt, n // 4, 2, rr, blk),
            v(nt, n // 4, 2, rr, blk),
            v(3, n // 4, 2, rr, blk),
            v(3, n // 4, 2, rr // 2, blk),
            v(length, blk, t=F32),
            v(length, blk, t=F32),
            v(2, blk, 2 * blk, t=F32),
            v(2, 4 + taps, blk, t=F32),
            v(2, n // 4, 2, 2, rb, 2 * blk),
            v(2, n // 4, 2, rb, 2 * blk),
            v(small_rows, blk, t=F32),
            v(small_rows - 16, blk, t=F32),
            v(small_rows, blk, t=F32),
        ]
        + row_sems() * 3
        + [dma((4,))]
        + scatter_sems(high) * (nt + 5)
        + [dma, dma, dma, dma, dma, dma, dma((slots,)), dma((slots,)), pltpu.SemaphoreType.REGULAR],
        compiler_params=pltpu.CompilerParams(
            collective_id=cid, has_side_effects=True, vmem_limit_bytes=VMEM_LIMIT
        ),
        name="backward",
    )(tok, rgrad, resid, gain, gsum2, ends, vec, gates, *saved, rec_own, hid, g_view, rec_w, mlp_w, u)


def mm(a, b):
    return jnp.dot(a, b, preferred_element_type=F32)


def mm_t(a, b):
    return lax.dot_general(a, b, (((1,), (1,)), ((), ())), preferred_element_type=F32)


def t_mm(a, b):
    return lax.dot_general(a, b, (((0,), (0,)), ((), ())), preferred_element_type=F32)


def local(
    tokens, doc_lengths, rec_gain, w_branch, w_input, w_rgate, w_igate, rgate_bias, igate_bias,
    decay_param, conv_weight, conv_bias, w_output, mlp_gain, w_gate, w_up, w_down, cotangent,
):
    n = lax.axis_size("dp")
    zh, zl, y, x, c = place()
    q = zl * 2 + x
    _, half, width = tokens.shape
    length = half * 2
    heads, rb, blk = w_rgate.shape
    taps = conv_weight.shape[0]
    rows = w_branch.shape[0]
    ff = w_gate.shape[1] // 4

    dp = lax.axis_index("dp")

    def lanes(v, per):
        v = v.astype(BF).reshape(-1, per)
        at = (dp * per) % 128
        return lax.dynamic_update_slice(jnp.zeros((v.shape[0], 128), BF), v, (0, at))

    params = jnp.concatenate(
        [rgate_bias[None], igate_bias[None], decay_param[None], conv_weight, conv_bias[None]], axis=0
    ).transpose(1, 0, 2)
    params = jnp.pad(params, ((0, 0), (0, 16 - params.shape[1]), (0, 0))).reshape(heads * 16, rb)
    lens_own = jnp.pad(doc_lengths.astype(BF), ((0, 13), (0, 124)))
    small = jnp.concatenate([lanes(params, rb), lanes(jnp.stack([rec_gain, mlp_gain]), rows), lens_own], axis=0)
    (
        rec_w, mlp_w, gates, vec, gains_all, group_ends, u, mlp_grad, pre, state, mixed, resid, norm_own,
    ) = forward(
        tokens[0], cotangent[0], w_branch, w_input, w_output, w_gate, w_up, w_down, w_rgate, w_igate, small, n, taps, 1,
    )
    g_mlp, rec_own, resid_grad, hid, gain2_sum = mlp_block(
        norm_own, resid, gains_all, cotangent[0], group_ends, mlp_w, mlp_grad, 4
    )
    result, token_grad, l_mlp, l_rec, l_sh, l_gate, l_small = backward(
        tokens[0], rec_own, resid_grad, resid, gains_all, gain2_sum, group_ends, vec, gates,
        (pre, state, mixed), hid, g_mlp, rec_w, mlp_w, u, n, taps, 5,
    )
    high = n // 8

    def owned(a):
        return jnp.sum(a.reshape((high, 4) + a.shape[1:]).astype(F32), axis=0)

    def add(a):
        return jnp.sum(a.astype(F32), axis=0)

    o_mlp = [add(l_mlp[:, i]) for i in range(3)]
    o_rec = [jnp.concatenate([add(l_rec[:, i]), add(l_sh[:, i])], axis=1) for i in range(3)]
    o_gate = owned(l_gate)
    o_gate = jnp.concatenate([o_gate[:, 0], jnp.sum(o_gate[:, 1], axis=0, keepdims=True)], axis=0)
    o_small = owned(l_small)
    at = dp * rb
    o_vec = jnp.concatenate([o_small[:, :8], jnp.sum(o_small[:, 8:16], axis=0, keepdims=True)], axis=0)
    o_vec = lax.dynamic_slice_in_dim(o_vec, at, rb, 2)
    o_gain = jnp.sum(o_small[:, 16:], axis=0).reshape(2, width)
    o_gain = lax.dynamic_slice_in_dim(o_gain, dp * rows, rows, 1)
    return (
        result[None],
        token_grad[None],
        o_gain[0],
        o_rec[0],
        o_rec[1],
        o_gate[:, :, :blk],
        o_gate[:, :, blk:],
        o_vec[:, 0],
        o_vec[:, 1],
        o_vec[:, 2],
        o_vec[:, 4 : 4 + taps].transpose(1, 0, 2),
        o_vec[:, 3],
        o_rec[2].T,
        o_gain[1],
        o_mlp[0],
        o_mlp[1],
        o_mlp[2].T,
    )


def solution(mesh):
    return jax.shard_map(
        local,
        mesh=mesh,
        in_specs=(
            P("dp", "tensor", None),
            P("dp", None),
            P("dp"),
            P("dp", "tensor"),
            P("dp", "tensor"),
            P("tensor", "dp", None),
            P("tensor", "dp", None),
            P("tensor", "dp"),
            P("tensor", "dp"),
            P("tensor", "dp"),
            P(None, "tensor", "dp"),
            P("tensor", "dp"),
            P("tensor", "dp"),
            P("dp"),
            P("dp", "tensor"),
            P("dp", "tensor"),
            P("tensor", "dp"),
            P("dp", "tensor", None),
        ),
        out_specs=(
            P("dp", "tensor", None),
            P("dp", "tensor", None),
            P("dp"),
            P("dp", "tensor"),
            P("dp", "tensor"),
            P("tensor", "dp", None),
            P("tensor", "dp", None),
            P("tensor", "dp"),
            P("tensor", "dp"),
            P("tensor", "dp"),
            P(None, "tensor", "dp"),
            P("tensor", "dp"),
            P("tensor", "dp"),
            P("dp"),
            P("dp", "tensor"),
            P("dp", "tensor"),
            P("tensor", "dp"),
        ),
        check_vma=False,
    )
```

```python
import functools

import jax
import jax.numpy as jnp
from jax import lax
from jax.experimental import pallas as pl
from jax.experimental.pallas import tpu as pltpu
from jax.sharding import PartitionSpec as P

MESH = pl.DeviceIdType.MESH
BF = jnp.bfloat16
F32 = jnp.float32
EPS = 1e-06
DECAY = 8.0
GC = 0.7978845608028654
GK = 0.044715
VMEM_LIMIT = 62 * 1024 * 1024


def dp_at(zh, zl, y, x):
    return ((zh * 2 + zl) * 2 + y) * 2 + x


def place():
    dp = lax.axis_index("dp")
    return dp // 8, (dp // 4) % 2, (dp // 2) % 2, dp % 2, lax.axis_index("tensor")


def dev(dp, core):
    return {"dp": dp, "tensor": core}


def greet(devices):
    sem = pltpu.get_barrier_semaphore()
    for d in devices:
        pl.semaphore_signal(sem, inc=1, device_id=d, device_id_type=MESH)
    pl.semaphore_wait(sem, len(devices))


def remote(src, dst, ssem, rsem, d):
    return pltpu.make_async_remote_copy(
        src_ref=src, dst_ref=dst, send_sem=ssem, recv_sem=rsem, device_id=d, device_id_type=MESH
    )


def plane(zh, zl, y, x, high):
    out = []
    for kh in range(high):
        for kl in range(2):
            for kx in range(2):
                ph, pz, px = (zh + kh) % high, (zl + kl) % 2, (x + kx) % 2
                out.append((ph, pz, px))
    return out


def gelu_parts(v):
    t = jnp.tanh(GC * (v + GK * v * v * v))
    act = 0.5 * v * (1.0 + t)
    der = 0.5 * (1.0 + t) + 0.5 * v * (1.0 - t * t) * GC * (1.0 + 3.0 * GK * v * v)
    return act, der


def segments(ends, length, width, taps):
    t = lax.broadcasted_iota(jnp.int32, (length, width), 0).astype(F32)

    def seg(at):
        total = jnp.zeros((length, width), F32)
        for j in range(4):
            total = total + jnp.where(at >= ends[:, j : j + 1], 1.0, 0.0)
        return total

    here = seg(t)
    same = []
    for k in range(1, taps):
        same.append(jnp.where((t >= float(k)) & (seg(t - float(k)) == here), 1.0, 0.0))
    return same


def scan8(a, b, reverse):
    length, width = a.shape
    row = lax.broadcasted_iota(jnp.int32, (length, width), 0) % 8
    for d in (1, 2, 4):
        if reverse:
            ash, bsh = pltpu.roll(a, length - d, 0), pltpu.roll(b, length - d, 0)
            ok = row < 8 - d
        else:
            ash, bsh = pltpu.roll(a, d, 0), pltpu.roll(b, d, 0)
            ok = row >= d
        b = b + a * jnp.where(ok, bsh, 0.0)
        a = a * jnp.where(ok, ash, 1.0)
    return a, b


def full_scan(a, b, out_ref, a_ref, reverse):
    length, width = a.shape
    a8, b8 = scan8(a, b, reverse)
    a_ref[...] = a8
    out_ref[...] = b8
    blocks = length // 8

    def step(i, carry):
        at = (blocks - 1 - i if reverse else i) * 8
        at = pl.multiple_of(at, 8)
        now = out_ref[pl.ds(at, 8), :] + a_ref[pl.ds(at, 8), :] * carry
        out_ref[pl.ds(at, 8), :] = now
        return now[0:1, :] if reverse else now[7:8, :]

    lax.fori_loop(0, blocks, step, jnp.zeros((1, width), F32))


class Gather:
    def __init__(self, slot, parts, sems, here, there, core):
        self.slot, self.parts, (self.send, self.recv, self.fsend) = slot, parts, sems
        zh, zl, y, x = here
        self.q = zl * 2 + x
        self.me = dp_at(zh, zl, y, x)
        self.near = [dp_at(h, z, y, w) for h, z, w in there]
        self.far = [dp_at(h, z, 1 - y, w) for h, z, w in there]
        self.pick = [z * 2 + w for _, z, w in there]
        self.core = core
        self.other = dev(dp_at(zh, zl, 1 - y, x), core)

    def ks(self, far):
        count = len(self.near)
        return range(4, count) if far else range(4)

    def start(self, far):
        for k in self.ks(far):
            for piece, part in self.parts:
                src = piece(self.pick[k])
                dst = part(self.slot(self.me, self.pick[k]))
                if k == 0:
                    pltpu.make_async_copy(src, dst, self.send.at[0]).start()
                else:
                    d = dev(self.near[k], self.core)
                    remote(src, dst, self.send.at[k], self.recv.at[self.me], d).start()

    def forward(self, k):
        land = self.slot(self.near[k], self.q)
        if k == 0:
            pltpu.make_async_copy(land, land, self.send.at[0]).wait()
        else:
            remote(land, land, self.send.at[k], self.recv.at[self.near[k]], self.other).wait_recv()
        remote(land, land, self.fsend.at[k], self.recv.at[self.near[k]], self.other).start()

    def forward_all(self, far):
        for k in self.ks(far):
            self.forward(k)

    def arrive_all(self):
        for k in range(len(self.far)):
            land = self.slot(self.far[k], self.q)
            remote(land, land, self.fsend.at[k], self.recv.at[self.far[k]], self.other).wait_recv()

    def finish(self):
        for k in range(len(self.near)):
            land = self.slot(self.near[k], self.q)
            remote(land, land, self.fsend.at[k], self.recv.at[self.near[k]], self.other).wait_send()
            if k:
                remote(land, land, self.send.at[k], self.recv.at[self.near[k]], self.other).wait_send()


class Rows:
    def __init__(self, buf, sems, here, core):
        self.buf, (self.send, self.recv, self.fsend, self.frecv) = buf, sems
        self.here, self.core = here, core
        zh, zl, y, x = here
        self.q = zl * 2 + x
        self.sib = dev(dp_at(zh, zl, y, x), 1 - core)

    def at(self, k):
        zh, zl, y, x = self.here
        pz, px = (zl + k // 2) % 2, (x + k % 2) % 2
        return pz * 2 + px, dev(dp_at(zh, pz, y, px), self.core)

    def start(self, piece=0, pieces=1):
        per = self.buf.shape[2] // pieces
        own = self.buf.at[self.q, self.core, pl.ds(piece * per, per)]
        for k in (1, 2):
            _, d = self.at(k)
            remote(own, own, self.send.at[k], self.recv.at[self.q], d).start()
        remote(own, own, self.fsend.at[0], self.frecv.at[self.q], self.sib).start()

    def forward(self, k):
        pq, d = self.at(k)
        land = self.buf.at[pq, self.core]
        remote(land, land, self.send.at[k], self.recv.at[pq], d).wait_recv()

        def relay():
            _, beside = self.at(1)
            remote(land, land, self.send.at[3], self.recv.at[pq], beside).start()

        if isinstance(k, int):
            if k == 2:
                relay()
        else:
            pl.when(k == 2)(relay)
        remote(land, land, self.fsend.at[k], self.frecv.at[pq], self.sib).start()

    def arrive(self, k):
        pq, _ = self.at(k)
        land = self.buf.at[pq, 1 - self.core]
        remote(land, land, self.fsend.at[k], self.frecv.at[pq], self.sib).wait_recv()

    def finish(self):
        own = self.buf.at[self.q, self.core]
        for k in range(4):
            remote(own, own, self.fsend.at[k], self.frecv.at[self.q], self.sib).wait_send()
            if k:
                remote(own, own, self.send.at[k], self.recv.at[self.q], self.sib).wait_send()


def row_sems():
    return [pltpu.SemaphoreType.DMA((4,))] * 4


class Sums:
    def __init__(self, part, sib, got, sems, rows):
        self.part, self.sib_buf, self.got = part, sib, got
        self.ssend, self.srecv, self.send, self.recv = sems
        self.rows = rows

    def push(self, k):
        r = self.rows
        pq, _ = r.at(k)
        remote(
            self.part.at[pq, 1 - r.core], self.sib_buf.at[pq], self.ssend.at[k], self.srecv.at[pq], r.sib
        ).start()

    def pair(self, k):
        r = self.rows
        pq, _ = r.at(k)
        land = self.sib_buf.at[pq]
        remote(land, land, self.ssend.at[k], self.srecv.at[pq], r.sib).wait_recv()
        return self.part[pq, r.core].astype(F32) + self.sib_buf[pq].astype(F32)

    def pass_on(self, k):
        r = self.rows
        pq, d = r.at(k)
        self.part[pq, r.core] = self.pair(k).astype(BF)
        remote(self.part.at[pq, r.core], self.got.at[r.q], self.send.at[k], self.recv.at[r.q], d).start()

    def take(self, k):
        r = self.rows
        pq, _ = r.at(k)
        land = self.got.at[pq]
        remote(land, land, self.send.at[k], self.recv.at[pq], r.sib).wait_recv()
        return self.got[pq].astype(F32)

    def ready(self):
        r = self.rows
        land = self.sib_buf.at[r.q]
        remote(land, land, self.ssend.at[0], self.srecv.at[r.q], r.sib).wait_recv()
        for k in (1, 2, 3):
            pq, _ = r.at(k)
            land = self.got.at[pq]
            remote(land, land, self.send.at[k], self.recv.at[pq], r.sib).wait_recv()

    def own(self, at):
        r = self.rows
        total = self.part[r.q, r.core, at].astype(F32) + self.sib_buf[r.q, at].astype(F32)
        for k in (1, 2, 3):
            total = total + self.got[r.at(k)[0], at].astype(F32)
        return total

    def finish(self):
        r = self.rows
        land = self.got.at[r.q]
        for k in range(4):
            remote(land, land, self.ssend.at[k], self.srecv.at[r.q], r.sib).wait_send()
            if k:
                remote(land, land, self.send.at[k], self.recv.at[r.q], r.sib).wait_send()


def rec_unit(taps, branch, conv_in, vec, gates, ends, state_ref, a_ref):
    same, conv, r, gate = rec_gates(taps, conv_in, vec, gates, ends)
    log_a = (-DECAY * r) * vec[2:3]
    a = jnp.exp(log_a)
    start = same[0] == 0.0
    a_eff = jnp.where(start, 0.0, a)
    mult = jnp.where(start, 1.0, jnp.sqrt(-jnp.tanh(log_a) * (1.0 + a * a)))
    full_scan(a_eff, mult * gate * conv, state_ref, a_ref, False)
    act, _ = gelu_parts(branch)
    return (state_ref[...] * act).astype(BF)


SMALL_ROWS = 96


def forward_kernel(n, taps, heads, turn, *refs):
    (tok, cot, wb, wi, wo, wg, wu, wd, wr, wig, small) = refs[:11]
    (o_rec, o_mlp, o_gate, o_vec, o_gain, o_ends, o_u, o_grad, pre, state, mixed, resid, o_norm) = refs[11:24]
    (rec, gat, sml, u_buf, og, part, sibb, got, extra, a_scr, gfull) = refs[24:35]
    sems = refs[35:]
    if turn:
        sems, wo_in, wd_in, (wo, wd) = refs[35:-2], wo, wd, refs[-2:]
    g_sems, r1, r2, s1, (fin, h_send, h_recv) = sems[:48], sems[48:52], sems[52:56], sems[56:60], sems[60:]
    zh, zl, y, x, c = place()
    here = (zh, zl, y, x)
    q, me = zl * 2 + x, dp_at(zh, zl, y, x)
    high = n // 8
    there = plane(zh, zl, y, x, high)
    half, width = tok.shape
    length, blk = pre.shape[1], pre.shape[2] // 2
    ff = wg.shape[1] // 4
    rb, rr = wr.shape[1], wb.shape[0]
    greet(
        [dev(dp_at(h, z, y, w), c) for h, z, w in there[1:]]
        + [dev(dp_at(zh, zl, 1 - y, x), c), dev(me, 1 - c)]
    )

    def whole(ref):
        return ref

    def head_cols(ref):
        return lambda p: ref.at[:, pl.ds(pl.multiple_of(p * blk, 128), blk)]

    def make(i, slot, parts):
        return Gather(slot, parts, g_sems[3 * i : 3 * i + 3], here, there, c)

    smalls = make(0, lambda s, g: sml.at[s], [(lambda p: small, whole)])
    gats, recs, mlps = [], [], []
    for h in range(2):
        pick = (lambda ref: lambda p: ref.at[p]) if h == 0 else (lambda ref: lambda p: ref.at[heads - 1])
        gats.append(
            make(
                1 + h,
                lambda s, g, h=h: gat.at[h, s],
                [
                    (pick(w), lambda r, i=i: r.at[:, pl.ds(i * blk, blk)])
                    for i, w in enumerate((wr, wig))
                ],
            )
        )
    for i, w in enumerate((wb, wi, wo)):
        recs.append(make(3 + i, lambda s, g, i=i: rec.at[0, i, s], [(head_cols(w), whole)]))
    part_rows = rr // 2

    def shared_piece(ref):
        return lambda p: ref.at[
            pl.ds(pl.multiple_of((p % 2) * part_rows, 8), part_rows), pl.ds((heads - 1) * blk, blk)
        ]

    def shared_rows(s, g):
        return rec.at[1, :, s, pl.ds(pl.multiple_of((g % 2) * part_rows, 8), part_rows), :]

    shared = make(
        6, shared_rows, [(shared_piece(w), lambda r, i=i: r.at[i]) for i, w in enumerate((wb, wi, wo))]
    )
    for i, w in enumerate((wg, wu, wd)):
        for t in range(ff // blk):
            piece = lambda p, w=w, t=t: w.at[:, pl.ds(pl.multiple_of(p * ff + t * blk, 128), blk)]
            j = i * (ff // blk) + t
            mlps.append(make(7 + j, lambda s, g, j=j: o_mlp.at[j, s], [(piece, whole)]))
    count = len(there)
    order = [shared, recs[0], gats[0], recs[1], gats[1], recs[2]] + mlps
    ahead = 3
    trickle = []

    def pump(j):
        if j + ahead < len(order):
            order[j + ahead].forward_all(False)
        order[j].forward_all(True)
        for _ in range(3 if j < 6 else 2):
            if trickle:
                trickle.pop(0)()
        if j + ahead < len(order):
            order[j + ahead].start(True)
        if j + 2 * ahead < len(order):
            order[j + 2 * ahead].start(False)

    def turn_over(src, dst):
        for i in range(0, src.shape[0], 128):
            dst[:, i : i + 128] = src[i : i + 128, :].T

    smalls.start(True)
    smalls.start(False)
    if turn:
        turn_over(wo_in, wo)
    for j in range(2 * ahead):
        if j < ahead:
            order[j].start(True)
        order[j].start(False)

    if turn:
        turn_over(wd_in, wd)
    xin = tok[...].astype(F32)
    unit = xin * lax.rsqrt(jnp.mean(xin * xin, axis=-1, keepdims=True) + EPS)
    resid[...] = unit
    smalls.forward_all(False)
    for j in range(ahead):
        order[j].forward_all(False)
    smalls.forward_all(True)
    pump(0)
    smalls.arrive_all()
    per_vec, per_gain = blk // 128, width // 128
    base = (heads - 1) * 16
    for h in range(2):
        at = pl.multiple_of(q * 16, 16) if h == 0 else base
        groups = [jnp.zeros((16, 128), F32)] * per_vec
        for s in range(n):
            g = s * rb // 128
            groups[g] = groups[g] + sml[s, pl.ds(at, 16), :].astype(F32)
        raw = jnp.concatenate(groups, axis=1)
        decay = raw[2:3]
        o_vec[h, 0:2, :] = raw[0:2]
        o_vec[h, 2:3, :] = jnp.log1p(jnp.exp(-decay))
        o_vec[h, 3:4, :] = jax.nn.sigmoid(-decay)
        o_vec[h, 4 : 5 + taps, :] = raw[3 : 4 + taps]
    groups = [None] * per_gain
    for s in range(n):
        g = s * rr // 128
        v = sml[s, SMALL_ROWS - 16 : SMALL_ROWS, :].astype(F32)
        groups[g] = v if groups[g] is None else groups[g] + v
    for g in range(per_gain):
        o_gain[:, g * 128 : (g + 1) * 128] = groups[g][0:8]
    for j in range(4):
        v = sml[dp_at(zh, j // 2, y, j % 2), SMALL_ROWS - 16 : SMALL_ROWS, :].astype(F32)
        row = jnp.broadcast_to(v[2:3], (8, 128))
        lane = lax.broadcasted_iota(jnp.int32, (8, 128), 1)
        ends = jnp.zeros((8, 128), F32)
        for i in range(4):
            ends = ends + jnp.where(lane >= i, row[:, i : i + 1], 0.0)
        o_ends[j] = ends
    u_rows = Rows(u_buf, r1, here, c)
    g_rows = Rows(o_grad, r2, here, c)
    u_buf[q, c] = (resid[...] * o_gain[0:1, :]).astype(BF)
    trickle += [functools.partial(u_rows.start, p, 8) for p in range(8)]
    e3 = o_ends[q][0:1, 3:4]
    spot = lax.broadcasted_iota(jnp.int32, (half, 1), 0).astype(F32) + (c * half).astype(F32)
    og[...] = jnp.where(spot < e3, cot[...], 0.0).astype(BF)
    own_grad = o_grad.at[q, c]
    place_grad = pltpu.make_async_copy(og, own_grad, fin.at[0])
    place_grad.start()
    place_grad.wait()
    _, beside = u_rows.at(1)

    def exchange(g, first, many):
        rows = rec.at[
            1, :, pl.ds(first, many), pl.ds(pl.multiple_of((g % 2) * part_rows, 8), part_rows), :
        ]
        return remote(rows, rows, h_send, h_recv, beside)

    pump(1)
    shared.arrive_all()
    eighth = n // 8
    trickle += [exchange(q, p * eighth, eighth).start for p in range(8)]
    for j in range(2, 5):
        pump(j)
    for k in (1, 2):
        u_rows.forward(k)
    pump(5)
    while trickle:
        trickle.pop(0)()
    trickle += [functools.partial(g_rows.start, p, 8) for p in range(8)]
    u_rows.forward(3)
    for a in gats + recs:
        a.arrive_all()
    for h in range(2):
        if rb % 16 == 0:
            o_gate[h] = gat[h].reshape(blk, 2 * blk)
        else:
            for s in range(n):
                gfull[s * rb : (s + 1) * rb, :] = gat[h, s].astype(F32)
            o_gate[h] = gfull[...].astype(BF)
    for k in range(4):
        u_rows.arrive(k)
    keep = [pltpu.make_async_copy(rec, o_rec, fin.at[1]), pltpu.make_async_copy(u_buf, o_u, fin.at[2])]
    keep[1].start()

    sums = Sums(part, sibb, got, s1, u_rows)

    def step(i, carry):
        h = i // 4
        k = ((i + 1) % 4) * ((7 - i) // 4)
        pq, _ = u_rows.at(k)
        at = pq + h * (4 - pq)

        @pl.when(i == 4)
        def _():
            exchange(q + 1, 0, n).wait_recv()
            keep[0].start()

        rows = u_buf[pq].reshape(2 * half, width)
        for j in range(2):
            w = rec[h, j].reshape(width, blk)
            pre[at, :, j * blk : (j + 1) * blk] = mm(rows, w)
        mx = rec_unit(
            taps, pre[at, :, :blk], pre[at, :, blk:], o_vec[h], o_gate[h], o_ends[pq][0:1, :], state.at[at], a_scr
        )
        mixed[at] = mx
        per = 512 // rr if rr <= 512 else 1

        def cols_out(t, carry):
            w = rec[h, 2, pl.ds(t * per, per)].reshape(per * rr, blk)
            tile = mm_t(mx, w)
            lanes = pl.ds(pl.multiple_of(t * (per * rr), 128), per * rr)
            tile = tile + jnp.where(i == 4, extra[:, lanes], 0.0)

            @pl.when(i == 3)
            def _():
                extra[:, lanes] = tile

            @pl.when(i != 3)
            def _():
                part[pq, 0, :, lanes] = tile[:half].astype(BF)
                part[pq, 1, :, lanes] = tile[half:].astype(BF)

            return carry

        lax.fori_loop(0, width // (per * rr), cols_out, 0)

        @pl.when(i != 3)
        def _():
            sums.push(k)

        @pl.when((i > 0) & (i < 4))
        def _():
            sums.pass_on(i)

        for j in range(4):

            @pl.when(i == j)
            def _():
                pump(6 + j)

        return carry

    extra[...] = jnp.zeros_like(extra)
    lax.fori_loop(0, 5, step, 0)
    pump(10)
    pump(11)
    for k in (1, 2):
        g_rows.forward(k)
    sums.ready()

    def finish(i, carry):
        at = pl.ds(pl.multiple_of(i * 32, 32), 32)
        total = tok[at, :].astype(F32) + sums.own(at)
        resid[at, :] = total
        unit = total * lax.rsqrt(jnp.mean(total * total, axis=-1, keepdims=True) + EPS)
        o_norm[at, :] = (unit * o_gain[1:2, :]).astype(BF)
        return carry

    lax.fori_loop(0, half // 32, finish, 0)
    pump(12)
    pump(13)
    g_rows.forward(3)
    for j in range(14, len(order)):
        pump(j)
    for a in mlps:
        a.arrive_all()
    for k in range(4):
        g_rows.arrive(k)
    exchange(q, 0, n).wait_send()
    for a in [smalls, shared] + mlps + gats + recs + [u_rows, g_rows, sums]:
        a.finish()
    for cp in keep:
        cp.wait()


def forward(tok, cot, wb, wi, wo, wg, wu, wd, wr, wig, small, n, taps, cid):
    half, width = tok.shape
    heads, rb, blk = wr.shape
    rr = wb.shape[0]
    length = 2 * half
    ff = wg.shape[1] // 4
    turn = rr % 128 == 0
    if not turn:
        wo, wd = wo.T, wd.T
    vm = pl.BlockSpec(memory_space=pltpu.VMEM)
    hb = pl.BlockSpec(memory_space=pl.ANY)

    def sds(*shape, t=F32):
        return jax.ShapeDtypeStruct(shape, t)

    unit = sds(5, length, blk)
    outs = (
        (sds(2, 3, n, rr, blk, t=BF), hb),
        (sds(3 * ff // blk, n, rr, blk, t=BF), hb),
        (sds(2, blk, 2 * blk, t=BF), vm),
        (sds(2, 16, blk), vm),
        (sds(8, width), vm),
        (sds(4, 8, 128), vm),
        (sds(4, 2, half, width, t=BF), hb),
        (sds(4, 2, half, width, t=BF), hb),
        (sds(5, length, 2 * blk), vm),
        (unit, vm),
        (sds(5, length, blk, t=BF), vm),
        (sds(half, width), vm),
        (sds(half, width, t=BF), vm),
    )
    count = n // 2
    return pl.pallas_call(
        functools.partial(forward_kernel, n, taps, heads, turn),
        out_shape=tuple(o for o, _ in outs),
        in_specs=[vm, vm, hb, hb, vm if turn else hb, hb, hb, vm if turn else hb, hb, hb, hb],
        out_specs=[s for _, s in outs],
        scratch_shapes=[
            pltpu.VMEM((2, 3, n, rr, blk), BF),
            pltpu.VMEM((2, n, rb, 2 * blk), BF),
            pltpu.VMEM((n, SMALL_ROWS, 128), BF),
            pltpu.VMEM((4, 2, half, width), BF),
            pltpu.VMEM((half, width), BF),
            pltpu.VMEM((4, 2, half, width), BF),
            pltpu.VMEM((4, half, width), BF),
            pltpu.VMEM((4, half, width), BF),
            pltpu.VMEM((length, width), F32),
            pltpu.VMEM((length, blk), F32),
            pltpu.VMEM((blk, 2 * blk), F32),
        ]
        + [
            pltpu.SemaphoreType.DMA((count,)),
            pltpu.SemaphoreType.DMA((n,)),
            pltpu.SemaphoreType.DMA((count,)),
        ]
        * 16
        + row_sems() * 3
        + [pltpu.SemaphoreType.DMA((3,)), pltpu.SemaphoreType.DMA, pltpu.SemaphoreType.DMA]
        + ([pltpu.VMEM((rr, heads * blk), BF), pltpu.VMEM((rr, 4 * ff), BF)] if turn else []),
        compiler_params=pltpu.CompilerParams(
            collective_id=cid, has_side_effects=True, vmem_limit_bytes=VMEM_LIMIT
        ),
        name="forward",
    )(tok, cot, wb, wi, wo, wg, wu, wd, wr, wig, small)


def mlp_kernel(norm, resid, gain, cot, ends, w_hbm, mg_hbm, g_hbm, o_rec, o_rgrad, o_hid, o_gain,
               w, nbuf, mg, hg, hu, gbuf, part, sibb, got, wsem, msem, gsem, *sems):
    zh, zl, y, x, c = place()
    here = (zh, zl, y, x)
    q, me = zl * 2 + x, dp_at(zh, zl, y, x)
    half, width = norm.shape
    nt, n, rr, blk = w.shape
    tiles, steps, per = nt // 3, width // blk, blk // rr
    rows = Rows(nbuf, sems[:4], here, c)
    sums = Sums(part, sibb, got, sems[4:8], rows)
    greet([dev(me, 1 - c)] + [rows.at(k)[1] for k in (1, 2, 3)])
    nbuf[q, c] = norm[...]
    rows.start()
    loads = []
    for t in range(tiles):
        for i in range(3):
            j = i * tiles + t
            loads.append((t, pltpu.make_async_copy(w_hbm.at[j], w.at[j], wsem.at[j])))
    loads.insert(2, (0, pltpu.make_async_copy(mg_hbm, mg, msem)))
    for _, cp in loads:
        cp.start()

    def row(k, carry):
        pq, _ = rows.at(k)
        rows.arrive(k)

        def first(t, carry):
            @pl.when(k == 0)
            def _():
                for j, cp in loads:

                    @pl.when(t == j)
                    def _():
                        cp.wait()

            a = nbuf[pq].reshape(2 * half, width)
            gate = mm(a, w[t].reshape(width, blk))
            up = mm(a, w[tiles + t].reshape(width, blk))
            grad = mm(mg[pq].reshape(2 * half, width), w[2 * tiles + t].reshape(width, blk))
            act, der = gelu_parts(gate)
            o_hid[t, pq] = (act * up).astype(BF)
            hg[t, pq] = (grad * up * der).astype(BF)
            hu[t, pq] = (grad * act).astype(BF)
            return carry

        lax.fori_loop(0, tiles, first, 0)

        @pl.when(k < 3)
        def _():
            rows.forward(k + 1)

        @pl.when(k > 1)
        def _():
            sums.pass_on(k - 1)

        def second(d, carry):
            left = jnp.concatenate([a[t, pq] for a in (hg, hu) for t in range(tiles)], axis=1)
            right = jnp.concatenate(
                [w[t, pl.ds(d * per, per)].reshape(blk, blk) for t in range(2 * tiles)], axis=1
            )
            total = mm_t(left, right)
            lanes = pl.ds(pl.multiple_of(d * blk, 128), blk)
            part[pq, 0, :, lanes] = total[:half].astype(BF)
            part[pq, 1, :, lanes] = total[half:].astype(BF)
            return carry

        lax.fori_loop(0, steps, second, 0)
        sums.push(k)
        return carry

    def rows_from(k, carry):
        return row(k, carry)

    lax.fori_loop(0, 4, rows_from, 0)
    sums.pass_on(3)

    def out_tile(d):
        at = pl.ds(d * per, per)
        return pltpu.make_async_copy(gbuf.at[:, at], g_hbm.at[:, at], gsem.at[d])

    def grads(d, carry):
        lanes = pl.ds(pl.multiple_of(d * blk, 128), blk)
        nt_ = nbuf[:, :, :, lanes].reshape(8 * half, blk).T
        mt_ = mg[:, :, :, lanes].reshape(8 * half, blk).T
        for i, (left, right) in enumerate(((nt_, hg), (nt_, hu), (mt_, o_hid))):
            for t in range(tiles):
                tile = mm(left, right[t].reshape(8 * half, blk))
                gbuf[i * tiles + t, pl.ds(d * per, per)] = tile.astype(BF).reshape(per, rr, blk)
        out_tile(d).start()
        return carry

    lax.fori_loop(0, steps, grads, 0)
    sums.ready()
    e3 = ends[q][0:1, 3:4]

    def finish(i, acc):
        at = pl.ds(pl.multiple_of(i * 32, 32), 32)
        total, r = sums.own(at), resid[at, :]
        scale = lax.rsqrt(jnp.mean(r * r, axis=-1, keepdims=True) + EPS)
        unit = r * scale
        g2 = total * gain[1:2, :]
        back = scale * (g2 - unit * jnp.mean(g2 * unit, axis=-1, keepdims=True))
        spot = lax.broadcasted_iota(jnp.int32, (32, 1), 0) + (c * half + i * 32)
        back = back + jnp.where(spot.astype(F32) < e3, cot[at, :], 0.0)
        o_rgrad[at, :] = back
        o_rec[at, :] = back.astype(BF)
        return acc + jnp.sum(total * unit, axis=0, keepdims=True)

    gsum = lax.fori_loop(0, half // 32, finish, jnp.zeros((1, width), F32))
    o_gain[...] = jnp.broadcast_to(gsum, o_gain.shape)
    for d in range(steps):
        out_tile(d).wait()
    rows.finish()
    sums.finish()


def mlp_block(norm, resid, gain, cot, ends, mlp_w, mlp_grad, cid):
    half, width = norm.shape
    nt, n, rr, blk = mlp_w.shape
    tiles = nt // 3
    vm = pl.BlockSpec(memory_space=pltpu.VMEM)
    hb = pl.BlockSpec(memory_space=pl.ANY)
    hid = (tiles, 4, 2 * half, blk)
    return pl.pallas_call(
        mlp_kernel,
        out_shape=(
            jax.ShapeDtypeStruct(mlp_w.shape, BF),
            jax.ShapeDtypeStruct((half, width), BF),
            jax.ShapeDtypeStruct((half, width), F32),
            jax.ShapeDtypeStruct(hid, BF),
            jax.ShapeDtypeStruct((8, width), F32),
        ),
        in_specs=[vm] * 5 + [hb] * 2,
        out_specs=[hb] + [vm] * 4,
        scratch_shapes=[
            pltpu.VMEM(mlp_w.shape, BF),
            pltpu.VMEM((4, 2, half, width), BF),
            pltpu.VMEM((4, 2, half, width), BF),
            pltpu.VMEM(hid, BF),
            pltpu.VMEM(hid, BF),
            pltpu.VMEM(mlp_w.shape, BF),
            pltpu.VMEM((4, 2, half, width), BF),
            pltpu.VMEM((4, half, width), BF),
            pltpu.VMEM((4, half, width), BF),
            pltpu.SemaphoreType.DMA((nt,)),
            pltpu.SemaphoreType.DMA,
            pltpu.SemaphoreType.DMA((width // blk,)),
        ]
        + row_sems() * 2,
        compiler_params=pltpu.CompilerParams(
            collective_id=cid, has_side_effects=True, vmem_limit_bytes=VMEM_LIMIT
        ),
        name="mlp_block",
    )(norm, resid, gain, cot, ends, mlp_w, mlp_grad)


class Scatter:
    def __init__(self, away, both, mine, pair, landed, sems, here, there, core):
        self.away, self.both, self.mine, self.pair, self.landed = away, both, mine, pair, landed
        self.ysend, self.yrecv, self.send, self.recv = sems
        zh, zl, y, x = here
        self.core = core
        self.own = zh * 4 + zl * 2 + x
        self.places = [(h * 4 + z * 2 + w, dp_at(h, z, y, w)) for h, z, w in (*there[4:], *there[1:4], there[0])]
        self.other = dev(dp_at(zh, zl, 1 - y, x), core)

    def start(self):
        remote(self.away, self.both, self.ysend, self.yrecv, self.other).start()

    def pass_on(self):
        last = len(self.places) - 1
        remote(self.away, self.both, self.ysend, self.yrecv, self.other).wait_recv()
        for i, (j, near) in enumerate(self.places):
            slot = self.pair(j)
            slot[...] = (self.mine(near).astype(F32) + slot[...].astype(F32)).astype(slot.dtype)
            if i == last:
                pltpu.make_async_copy(slot, self.landed(self.own), self.send.at[j]).start()
            else:
                remote(
                    slot, self.landed(self.own), self.send.at[j], self.recv.at[self.own], dev(near, self.core)
                ).start()

    def collect(self):
        last = len(self.places) - 1
        remote(self.away, self.both, self.ysend, self.yrecv, self.other).wait_send()
        for i, (j, _) in enumerate(self.places):
            slot, land = self.pair(j), self.landed(j)
            if i == last:
                pltpu.make_async_copy(land, land, self.send.at[j]).wait()
            else:
                remote(land, land, self.send.at[j], self.recv.at[j], self.other).wait_recv()
                remote(slot, slot, self.send.at[j], self.recv.at[j], self.other).wait_send()


def scatter_sems(high):
    return [pltpu.SemaphoreType.DMA, pltpu.SemaphoreType.DMA] + [pltpu.SemaphoreType.DMA((high * 4,))] * 2


def rec_gates(taps, conv_in, vec, gates, ends):
    length, blk = conv_in.shape
    same = segments(ends, length, blk, taps)
    conv = conv_in * vec[4:5] + vec[4 + taps : 5 + taps]
    for k in range(1, taps):
        conv = conv + pltpu.roll(conv_in, k, 0) * same[k - 1] * vec[4 + k : 5 + k]
    pre = jnp.dot(conv.astype(BF), gates, preferred_element_type=F32)
    r = jax.nn.sigmoid(pre[:, :blk] + vec[0:1])
    gate = jax.nn.sigmoid(pre[:, blk:] + vec[1:2])
    return same, conv, r, gate


def rec_unit_back(taps, branch, conv_in, vec, gates, ends, state, mg, carry_ref, a_ref):
    length, blk = branch.shape
    same, conv, r, gate = rec_gates(taps, conv_in, vec, gates, ends)
    start = same[0] == 0.0
    act, der = gelu_parts(branch)
    branch_low = (mg * state * der).astype(BF)
    log_a = (-DECAY * r) * vec[2:3]
    a = jnp.exp(log_a)
    a_eff = jnp.where(start, 0.0, a)
    row = lax.broadcasted_iota(jnp.int32, (length, blk), 0)
    a_next = jnp.where(row < length - 1, pltpu.roll(a_eff, length - 1, 0), 0.0)
    full_scan(a_next, mg * act, carry_ref, a_ref, True)
    carry = carry_ref[...]
    prev = jnp.where(row > 0, pltpu.roll(state, 1, 0), 0.0)
    raw = jnp.sqrt(-jnp.tanh(log_a) * (1.0 + a * a))
    mult = jnp.where(start, 1.0, raw)
    log_grad = jnp.where(start, 0.0, carry * prev * a - carry * gate * conv * (a * a) / raw)
    r_grad = log_grad * (-DECAY * vec[2:3]) * (r * (1.0 - r))
    i_grad = carry * mult * conv * (gate * (1.0 - gate))
    pre_low = jnp.concatenate([r_grad.astype(BF), i_grad.astype(BF)], axis=1)
    conv_grad = carry * mult * gate + mm_t(pre_low, gates)
    gate_grads = t_mm(conv.astype(BF), pre_low)

    def total(v):
        return jnp.sum(v, axis=0, keepdims=True)

    sums = [total(r_grad), total(i_grad), total(log_grad * (DECAY * r) * vec[3:4]), total(conv_grad)]
    inp = conv_grad * vec[4:5]
    sums.append(total(conv_grad * conv_in))
    for k in range(1, taps):
        masked = conv_grad * same[k - 1]
        sums.append(total(masked * pltpu.roll(conv_in, k, 0)))
        inp = inp + pltpu.roll(masked, length - k, 0) * vec[4 + k : 5 + k]
    return branch_low, inp.astype(BF), gate_grads, jnp.concatenate(sums, axis=0)


def backward_kernel(n, taps, *refs):
    (tok, rgrad, resid, gain, gsum2, ends, vec, gates, pre, state, mixed) = refs[:11]
    (rec_own, hid, g_hbm, rec_hbm, mlp_hbm, u_hbm) = refs[11:17]
    (o_res, o_tok, l_mlp, l_rec, l_sh, l_gate, l_small) = refs[17:24]
    (rec, ub, rg, part, sib1, got1, low, grec, gsh, gshin, g_own, y_mlp, y_rec, y_sh, a_scr, c_scr,
     gg, vg, ggl, y_gate, sml, sml_sib, y_sml) = refs[24:47]
    sems = refs[47:]
    zh, zl, y, x, c = place()
    here = (zh, zl, y, x)
    q, me = zl * 2 + x, dp_at(zh, zl, y, x)
    high = n // 8
    there = plane(zh, zl, y, x, high)
    half, width = tok.shape
    length = 2 * half
    blk = mixed.shape[2]
    rr = width // n
    rb = blk // n
    nt = g_own.shape[0]
    per, steps = blk // rr, width // blk
    taken = [0]

    def some(k):
        taken[0] += k
        return sems[taken[0] - k : taken[0]]

    rows = Rows(rg, some(4), here, c)
    sums1 = Sums(part, sib1, got1, some(4), rows)
    sums2 = Sums(part, sib1, got1, some(4), rows)
    (loads,) = some(1)
    greet(
        [dev(dp_at(h, z, y, w), c) for h, z, w in there[1:]]
        + [dev(dp_at(zh, zl, 1 - y, x), c), dev(me, 1 - c)]
    )
    first = pltpu.make_async_copy(rec_own, rg.at[q, c], loads.at[0])
    first.start()
    first.wait()
    rows.start()
    grab = [
        pltpu.make_async_copy(rec_hbm, rec, loads.at[0]),
        pltpu.make_async_copy(u_hbm, ub, loads.at[1]),
        pltpu.make_async_copy(g_hbm.at[:, :, y], g_own, loads.at[2]),
    ]
    for cp in grab:
        cp.start()

    tiles = nt // 3

    def cols_at(i):
        return pl.ds(pl.multiple_of(i * blk, 128), blk)

    def chunk(i, sem):
        return Scatter(
            g_hbm.at[i, :, 1 - y],
            y_mlp.at[i],
            lambda s: g_own[i, s // 4, s % 2],
            lambda j: y_mlp.at[i, j // 2, j % 2],
            lambda j: l_mlp.at[j // 4, i // tiles, :, cols_at((j % 4) * tiles + i % tiles)],
            sem, here, there, c,
        )

    mlps = [chunk(i, some(4)) for i in range(nt)]
    for a in mlps[:3]:
        a.start()
    recs = [
        Scatter(
            grec.at[i, :, 1 - y],
            y_rec.at[i],
            lambda s, i=i: grec[i, s // 4, (s // 2) % 2, s % 2],
            lambda j, i=i: y_rec.at[i, j // 2, j % 2],
            lambda j, i=i: l_rec.at[j // 4, i, :, cols_at(j % 4)],
            some(4), here, there, c,
        )
        for i in range(3)
    ]
    part_rows = rr // 2

    shared = Scatter(
        gshin.at[:, :, 1 - y],
        y_sh,
        lambda s: gshin[:, s // 4, (s // 2) % 2, s % 2],
        lambda j: y_sh.at[:, j // 2, j % 2],
        lambda j: l_sh.at[j // 2, :, pl.ds(pl.multiple_of((j % 2) * part_rows, 8), part_rows), :],
        some(4), here, there, c,
    )
    gate_sc = Scatter(
        ggl.at[:, :, 1 - y],
        y_gate,
        lambda s: ggl[:, s // 4, (s // 2) % 2, s % 2],
        lambda j: y_gate.at[:, j // 2, j % 2],
        lambda j: l_gate.at[j],
        some(4), here, there, c,
    )
    h_send, h_recv, s_send, s_recv, z_send, z_recv, m_send, m_recv, again = some(9)
    order = mlps + [shared] + recs + [gate_sc]
    trickle = []
    _, beside = rows.at(1)
    eighth = n // 16

    def pump(j):
        order[j].pass_on()
        for _ in range(2 if j else 0):
            if trickle:
                trickle.pop(0)()
        if j + 3 < len(order):
            order[j + 3].start()

    gg[...] = jnp.zeros_like(gg)
    vg[...] = jnp.zeros_like(vg)
    grab[0].wait()

    def exchange(first, many):
        there_rows = pl.ds(pl.multiple_of((1 - x) * part_rows, 8), part_rows)
        cut = pl.ds(first, many)
        return remote(gsh.at[:, cut, :, :, there_rows, :], gshin.at[:, cut], h_send, h_recv, beside)

    def store(ref, i, d, tile):
        tile = tile.astype(BF)
        if per == 2:
            ref[i, d // 2, d % 2] = tile.reshape(2, rr, blk)
        else:
            ref[i, pl.ds(d * (per // 4), per // 4)] = tile.reshape(per // 4, 2, 2, rr, blk)

    def shared_grads(d, carry):
        lanes = pl.ds(pl.multiple_of(d * blk, 128), blk)
        uo = ub[q, :, :, lanes].reshape(length, blk).T
        ro = rg[q, :, :, lanes].reshape(length, blk).T
        for i in range(3):
            own = low[4, :, i * blk : (i + 1) * blk] if i < 2 else mixed[4]
            store(gsh, i, d, mm(uo if i < 2 else ro, own))
        return carry

    trickle += [exchange(p * eighth, eighth).start for p in range(4)]

    def step(i, carry):
        h = jnp.where(i == 1, 1, 0)
        k = jnp.maximum(i - 1, 0)
        pq, _ = rows.at(k)
        at = pq + h * (4 - pq)

        @pl.when(i != 1)
        def _():
            rows.arrive(k)

        mg = mm(rg[pq].reshape(length, width), rec[h, 2].reshape(width, blk))

        @pl.when((i > 0) & (i < 4))
        def _():
            rows.forward(k + 1)

        b_low, i_low, g_add, v_add = rec_unit_back(
            taps, pre[at, :, :blk], pre[at, :, blk:], vec[h], gates[h], ends[pq][0:1, :], state[at], mg, c_scr, a_scr,
        )
        low[at, :, :blk], low[at, :, blk:] = b_low, i_low
        gg[h] += g_add
        vg[h] += v_add

        @pl.when(i > 2)
        def _():
            sums1.pass_on(k - 1)

        def cols_out(t, carry):
            cut = pl.ds(t * per, per)
            lanes = pl.ds(pl.multiple_of(t * blk, 128), blk)

            def tile_of(left, head):
                return mm_t(left, jnp.concatenate([rec[head, j, cut].reshape(blk, blk) for j in range(2)], axis=1))

            def emit(tile):
                part[pq, 0, :, lanes] = tile[:half].astype(BF)
                part[pq, 1, :, lanes] = tile[half:].astype(BF)

            @pl.when(i == 1)
            def _():
                emit(tile_of(low[4], 1) + tile_of(low[pq], 0))

            @pl.when(i > 1)
            def _():
                emit(tile_of(low[pq], 0))

            return carry

        @pl.when(i > 0)
        def _():
            lax.fori_loop(0, steps, cols_out, 0)

        @pl.when(i > 0)
        def _():
            sums1.push(k)

        for j in range(5):

            @pl.when(i == j)
            def _():
                if j == 0:
                    grab[2].wait()
                if j == 1:
                    grab[1].wait()
                    lax.fori_loop(0, steps, shared_grads, 0)
                pump(j)

        return carry

    lax.fori_loop(0, 5, step, 0)
    sums1.pass_on(3)
    for h in range(2):
        for s in range(n):
            ggl[h, s // 4, (s // 2) % 2, s % 2] = gg[h, s * rb : (s + 1) * rb, :].astype(BF)
    fetch = pltpu.make_async_copy(mlp_hbm.at[pl.ds(2 * (nt // 3), nt // 3)], rec.at[0], loads.at[0])
    fetch.start()
    pump(5)

    def grads(d, carry):
        lanes = pl.ds(pl.multiple_of(d * blk, 128), blk)
        ut = ub[:, :, :, lanes].reshape(4 * length, blk).T
        rt = rg[:, :, :, lanes].reshape(4 * length, blk).T
        for i in range(3):
            if i < 2:
                right = low[0:4, :, i * blk : (i + 1) * blk].reshape(4 * length, blk)
            else:
                right = mixed[0:4].reshape(4 * length, blk)
            store(grec, i, d, mm(ut if i < 2 else rt, right))
        return carry

    lax.fori_loop(0, steps, grads, 0)
    exchange(0, n // 4).wait()
    for s in range(n // 4):
        gshin[:, s] = (
            gshin[:, s].astype(F32)
            + gsh[:, s, :, :, pl.ds(pl.multiple_of(x * part_rows, 8), part_rows), :].astype(F32)
        ).astype(BF)
    per_row = length // rr
    fetch_hid = pltpu.make_async_copy(hid, gsh.at[:, pl.ds(0, per_row)], loads.at[1])
    fetch_hid.start()
    pump(6)

    sums1.ready()

    def finish(i, acc):
        at = pl.ds(pl.multiple_of(i * 32, 32), 32)
        total, xin = sums1.own(at), tok[at, :].astype(F32)
        scale = lax.rsqrt(jnp.mean(xin * xin, axis=-1, keepdims=True) + EPS)
        unit = xin * scale
        g1 = total * gain[0:1, :]
        o_tok[at, :] = rgrad[at, :] + scale * (g1 - unit * jnp.mean(g1 * unit, axis=-1, keepdims=True))
        return acc + jnp.sum(total * unit, axis=0, keepdims=True)

    gsum1 = lax.fori_loop(0, half // 32, finish, jnp.zeros((1, width), F32))
    sums1.finish()
    for d in [rows.sib] + [rows.at(k)[1] for k in (1, 2, 3)]:
        pl.semaphore_signal(again, inc=1, device_id=d, device_id_type=MESH)
    for h in range(2):
        sml[8 * h : 8 * h + 8, :] = vg[h]
    for i in range(steps):
        sml[16 + i : 17 + i, :] = gsum1[:, i * blk : (i + 1) * blk]
        sml[16 + steps + i : 17 + steps + i, :] = gsum2[0:1, i * blk : (i + 1) * blk]
    gain_rows = sml.at[pl.ds(16, 2 * steps)]
    with_sib = remote(gain_rows, sml_sib, s_send, s_recv, rows.sib)
    with_sib.start()
    pump(7)

    fetch.wait()
    fetch_hid.wait()

    pl.semaphore_wait(again, 4)

    def hid_rows(t, row):
        if per_row == 2:
            return gsh[t, row // 2, row % 2].reshape(length, blk)
        return gsh[t, pl.ds(row * (per_row // 4), per_row // 4)].reshape(length, blk)

    def out_rows(i, carry):
        k = (i + 1) % 4
        pq, _ = rows.at(k)

        def cols_out(d, carry):
            tile = jnp.zeros((length, blk), F32)
            for t in range(nt // 3):
                left = hid_rows(t, pq)
                tile = tile + mm_t(left, rec[0, t, pl.ds(d * per, per)].reshape(blk, blk))
            lanes = pl.ds(pl.multiple_of(d * blk, 128), blk)
            part[pq, 0, :, lanes] = tile[:half].astype(BF)
            part[pq, 1, :, lanes] = tile[half:].astype(BF)
            return carry

        lax.fori_loop(0, steps, cols_out, 0)
        sums2.push(k)

        @pl.when(i > 0)
        def _():
            sums2.pass_on(i)

        return carry

    lax.fori_loop(0, 4, out_rows, 0)
    pump(8)
    with_sib.wait()
    sml[16 : 16 + 2 * steps, :] += sml_sib[...]
    with_y = remote(sml, y_sml, z_send, z_recv, dev(dp_at(zh, zl, 1 - y, x), c))
    with_y.start()
    pump(9)
    pump(10)
    with_y.wait()
    sml[...] = sml[...] + y_sml[...]
    mine = zh * 4 + q
    small_out = []
    for i, (h, z, w) in enumerate(there):
        if i == 0:
            cp = pltpu.make_async_copy(sml, l_small.at[mine], m_send.at[i])
        else:
            cp = remote(sml, l_small.at[mine], m_send.at[i], m_recv.at[mine], dev(dp_at(h, z, y, w), c))
        cp.start()
        small_out.append(cp)
    pump(11)
    sums2.ready()
    e3 = ends[q][0:1, 3:4]

    def result(i, carry):
        at = pl.ds(pl.multiple_of(i * 32, 32), 32)
        spot = lax.broadcasted_iota(jnp.int32, (32, 1), 0) + (c * half + i * 32)
        o_res[at, :] = jnp.where(spot.astype(F32) < e3, resid[at, :] + sums2.own(at), 0.0).astype(BF)
        return carry

    lax.fori_loop(0, half // 32, result, 0)
    sums2.finish()
    pump(12)
    pump(13)
    rows.finish()
    for a in mlps + recs + [gate_sc, shared]:
        a.collect()
    for i, (h, z, w) in enumerate(there):
        if i == 0:
            small_out[i].wait()
        else:
            j = h * 4 + z * 2 + w
            land = l_small.at[j]
            remote(land, land, m_send.at[i], m_recv.at[j], rows.sib).wait_recv()
            small_out[i].wait_send()


def backward(tok, rec_own, rgrad, resid, gain, gsum2, ends, vec, gates, saved, hid, g_mlp, rec_w, mlp_w, u, n, taps, cid):
    half, width = tok.shape
    pre, state, mixed = saved
    blk = mixed.shape[2]
    length = 2 * half
    rr, rb, high = width // n, blk // n, n // 8
    nt = g_mlp.shape[0]
    slots = high * 4
    vm = pl.BlockSpec(memory_space=pltpu.VMEM)
    hb = pl.BlockSpec(memory_space=pl.ANY)
    g_view = g_mlp.reshape(nt, n // 4, 2, 2, rr, blk)
    hid = hid.reshape(nt // 3, length // rr, 2, 2, rr, blk)
    small_rows = 16 + 2 * (width // blk)

    def sds(*shape, t=BF):
        return jax.ShapeDtypeStruct(shape, t)

    def v(*shape, t=BF):
        return pltpu.VMEM(shape, t)

    dma = pltpu.SemaphoreType.DMA
    return pl.pallas_call(
        functools.partial(backward_kernel, n, taps),
        out_shape=(
            sds(half, width),
            sds(half, width, t=F32),
            sds(high, 3, rr, 4 * (nt // 3) * blk),
            sds(high, 3, rr, 4 * blk),
            sds(slots // 2, 3, rr, blk),
            sds(slots, 2, rb, 2 * blk),
            sds(slots, small_rows, blk, t=F32),
        ),
        in_specs=[vm] * 11 + [hb] * 6,
        out_specs=[vm, vm] + [hb] * 5,
        scratch_shapes=[
            v(2, 3, n, rr, blk),
            v(4, 2, half, width),
            v(4, 2, half, width),
            v(4, 2, half, width),
            v(4, half, width),
            v(4, half, width),
            v(5, length, 2 * blk),
            v(3, n // 4, 2, 2, rr, blk),
            v(3, n // 4, 2, 2, rr, blk),
            v(3, n // 4, 2, 2, rr // 2, blk),
            v(nt, n // 4, 2, rr, blk),
            v(nt, n // 4, 2, rr, blk),
            v(3, n // 4, 2, rr, blk),
            v(3, n // 4, 2, rr // 2, blk),
            v(length, blk, t=F32),
            v(length, blk, t=F32),
            v(2, blk, 2 * blk, t=F32),
            v(2, 4 + taps, blk, t=F32),
            v(2, n // 4, 2, 2, rb, 2 * blk),
            v(2, n // 4, 2, rb, 2 * blk),
            v(small_rows, blk, t=F32),
            v(small_rows - 16, blk, t=F32),
            v(small_rows, blk, t=F32),
        ]
        + row_sems() * 3
        + [dma((4,))]
        + scatter_sems(high) * (nt + 5)
        + [dma, dma, dma, dma, dma, dma, dma((slots,)), dma((slots,)), pltpu.SemaphoreType.REGULAR],
        compiler_params=pltpu.CompilerParams(
            collective_id=cid, has_side_effects=True, vmem_limit_bytes=VMEM_LIMIT
        ),
        name="backward",
    )(tok, rgrad, resid, gain, gsum2, ends, vec, gates, *saved, rec_own, hid, g_view, rec_w, mlp_w, u)


def mm(a, b):
    return jnp.dot(a, b, preferred_element_type=F32)


def mm_t(a, b):
    return lax.dot_general(a, b, (((1,), (1,)), ((), ())), preferred_element_type=F32)


def t_mm(a, b):
    return lax.dot_general(a, b, (((0,), (0,)), ((), ())), preferred_element_type=F32)


def local(
    tokens, doc_lengths, rec_gain, w_branch, w_input, w_rgate, w_igate, rgate_bias, igate_bias,
    decay_param, conv_weight, conv_bias, w_output, mlp_gain, w_gate, w_up, w_down, cotangent,
):
    n = lax.axis_size("dp")
    zh, zl, y, x, c = place()
    q = zl * 2 + x
    _, half, width = tokens.shape
    length = half * 2
    heads, rb, blk = w_rgate.shape
    taps = conv_weight.shape[0]
    rows = w_branch.shape[0]
    ff = w_gate.shape[1] // 4

    dp = lax.axis_index("dp")

    def lanes(v, per):
        v = v.astype(BF).reshape(-1, per)
        at = (dp * per) % 128
        return lax.dynamic_update_slice(jnp.zeros((v.shape[0], 128), BF), v, (0, at))

    params = jnp.concatenate(
        [rgate_bias[None], igate_bias[None], decay_param[None], conv_weight, conv_bias[None]], axis=0
    ).transpose(1, 0, 2)
    params = jnp.pad(params, ((0, 0), (0, 16 - params.shape[1]), (0, 0))).reshape(heads * 16, rb)
    lens_own = jnp.pad(doc_lengths.astype(BF), ((0, 13), (0, 124)))
    small = jnp.concatenate([lanes(params, rb), lanes(jnp.stack([rec_gain, mlp_gain]), rows), lens_own], axis=0)
    (
        rec_w, mlp_w, gates, vec, gains_all, group_ends, u, mlp_grad, pre, state, mixed, resid, norm_own,
    ) = forward(
        tokens[0], cotangent[0], w_branch, w_input, w_output, w_gate, w_up, w_down, w_rgate, w_igate, small, n, taps, 1,
    )
    g_mlp, rec_own, resid_grad, hid, gain2_sum = mlp_block(
        norm_own, resid, gains_all, cotangent[0], group_ends, mlp_w, mlp_grad, 4
    )
    result, token_grad, l_mlp, l_rec, l_sh, l_gate, l_small = backward(
        tokens[0], rec_own, resid_grad, resid, gains_all, gain2_sum, group_ends, vec, gates,
        (pre, state, mixed), hid, g_mlp, rec_w, mlp_w, u, n, taps, 5,
    )
    high = n // 8

    def owned(a):
        return jnp.sum(a.reshape((high, 4) + a.shape[1:]).astype(F32), axis=0)

    def add(a):
        return jnp.sum(a.astype(F32), axis=0)

    o_mlp = [add(l_mlp[:, i]) for i in range(3)]
    o_rec = [jnp.concatenate([add(l_rec[:, i]), add(l_sh[:, i])], axis=1) for i in range(3)]
    o_gate = owned(l_gate)
    o_gate = jnp.concatenate([o_gate[:, 0], jnp.sum(o_gate[:, 1], axis=0, keepdims=True)], axis=0)
    o_small = owned(l_small)
    at = dp * rb
    o_vec = jnp.concatenate([o_small[:, :8], jnp.sum(o_small[:, 8:16], axis=0, keepdims=True)], axis=0)
    o_vec = lax.dynamic_slice_in_dim(o_vec, at, rb, 2)
    o_gain = jnp.sum(o_small[:, 16:], axis=0).reshape(2, width)
    o_gain = lax.dynamic_slice_in_dim(o_gain, dp * rows, rows, 1)
    return (
        result[None],
        token_grad[None],
        o_gain[0],
        o_rec[0],
        o_rec[1],
        o_gate[:, :, :blk],
        o_gate[:, :, blk:],
        o_vec[:, 0],
        o_vec[:, 1],
        o_vec[:, 2],
        o_vec[:, 4 : 4 + taps].transpose(1, 0, 2),
        o_vec[:, 3],
        o_rec[2].T,
        o_gain[1],
        o_mlp[0],
        o_mlp[1],
        o_mlp[2].T,
    )


def solution(mesh):
    return jax.shard_map(
        local,
        mesh=mesh,
        in_specs=(
            P("dp", "tensor", None),
            P("dp", None),
            P("dp"),
            P("dp", "tensor"),
            P("dp", "tensor"),
            P("tensor", "dp", None),
            P("tensor", "dp", None),
            P("tensor", "dp"),
            P("tensor", "dp"),
            P("tensor", "dp"),
            P(None, "tensor", "dp"),
            P("tensor", "dp"),
            P("tensor", "dp"),
            P("dp"),
            P("dp", "tensor"),
            P("dp", "tensor"),
            P("tensor", "dp"),
            P("dp", "tensor", None),
        ),
        out_specs=(
            P("dp", "tensor", None),
            P("dp", "tensor", None),
            P("dp"),
            P("dp", "tensor"),
            P("dp", "tensor"),
            P("tensor", "dp", None),
            P("tensor", "dp", None),
            P("tensor", "dp"),
            P("tensor", "dp"),
            P("tensor", "dp"),
            P(None, "tensor", "dp"),
            P("tensor", "dp"),
            P("tensor", "dp"),
            P("dp"),
            P("dp", "tensor"),
            P("dp", "tensor"),
            P("tensor", "dp"),
        ),
        check_vma=False,
    )
```
